32 devices in a mesh: seq: 4 (over x, core), head: 8 (over z, y).
Axes of the slice: x: 2, y: 2, z: 4, core: 2. Of those that a mesh axis runs over, the one named last changes fastest.
Arguments:
- tokens: bfloat16 [1024, 4096], P('seq', 'head'), may hold values from -6 to 6
- w_query: bfloat16 [4096, 2048], P(None, 'head'), may hold values from -0.09375 to 0.09375
- w_key: bfloat16 [4096, 2048], P(None, 'head'), may hold values from -0.09375 to 0.09375
- w_value: bfloat16 [4096, 2048], P(None, 'head'), may hold values from -0.09375 to 0.09375
- w_out: bfloat16 [2048, 4096], P('head'), may hold values from -0.125 to 0.125
- grad_out: bfloat16 [1024, 4096], P('seq', 'head'), may hold values from -6 to 6
- state_in: float32 [16, 128, 128], P('head'), may hold values from -384 to 384
Outputs:
- result: bfloat16 [1024, 4096], P('seq', 'head')
- grad_tokens: float32 [1024, 4096], P('seq', 'head')
- grad_wq: float32 [4096, 2048], P('seq', 'head')
- grad_wk: float32 [4096, 2048], P('seq', 'head')
- grad_wv: float32 [4096, 2048], P('seq', 'head')
- grad_wo: float32 [2048, 4096], P('head', 'seq')
- grad_state_in: float32 [16, 128, 128], P('head')
The draws below stay inside these ranges and needn't reach their ends.
All inputs are finite; a program needn't handle non-finite values.
Results may differ from the reference program's by a relative error of at most 0.018.
Values may be sent and summed in bfloat16 or wider, within the bound.
A program may use at most 64 MiB of HBM per device.

```python
import jax
import jax.numpy as jnp
from jax import lax

D = 4096
HEADS = 16
DH = 128
BLOCK = 256
TOKENS = 1024
N_HEAD = 8


def block_levels(stream_key, extent, shards, smallest, largest):
    gain, own = 1.0, jax.random.fold_in(stream_key, 6)
    for dim, parts in shards:
        steps = jnp.exp(jax.random.uniform(jax.random.fold_in(own, dim), (parts,), jnp.float32, smallest / len(shards), largest / len(shards)))
        gain = gain * jnp.repeat(steps, extent[dim] // parts).reshape([-1 if axis == dim else 1 for axis in range(len(extent))])
    return gain


def centred(rng, shape, scale, most, cuts=(), kind=jnp.bfloat16):
    drawn = scale * jax.random.normal(rng, shape, jnp.float32)
    if cuts:
        drawn = drawn * block_levels(rng, shape, cuts, -0.22, 0.18)
    return jnp.clip(drawn, -most, most).astype(kind)


def setup_inputs(seed: int = 0) -> dict:
    arg_keys = jax.random.split(jax.random.key(seed), 8)
    return {
        "tokens": centred(arg_keys[0], (TOKENS, D), 1.0, 6.0, ((0, 4), (1, 8))),
        "w_query": centred(arg_keys[1], (D, HEADS * DH), D ** -0.5, 0.09375, ((1, 8),)),
        "w_key": centred(arg_keys[2], (D, HEADS * DH), D ** -0.5, 0.09375, ((1, 8),)),
        "w_value": centred(arg_keys[3], (D, HEADS * DH), D ** -0.5, 0.09375, ((1, 8),)),
        "w_out": centred(arg_keys[4], (HEADS * DH, D), (HEADS * DH) ** -0.5, 0.125, ((0, 8),)),
        "grad_out": centred(arg_keys[5], (TOKENS, D), 1.0, 6.0, ((0, 4), (1, 8))),
        "state_in": centred(arg_keys[6], (HEADS, DH, DH), (DH // 2), 384.0, ((0, 8),), jnp.float32),
    }


EPSILON = 1e-06
WIDE_TYPE = jnp.float32
HALF_TYPE = jnp.bfloat16

def causal_mask(width):
    return jnp.tril(jnp.ones((width, width), WIDE_TYPE)) > 0.5

def excl_prefix(states):
    running = jnp.cumsum(states, axis=0)
    return jnp.concatenate([jnp.zeros_like(states[:1]), running[:-1]], axis=0)

def excl_suffix(states):
    return jnp.flip(excl_prefix(jnp.flip(states, 0)), 0)

def block_scores(query_blk, keys_blk):
    allowed = causal_mask(query_blk.shape[0])
    scores = jnp.einsum('thd,shd->hts', query_blk.astype(WIDE_TYPE), keys_blk.astype(WIDE_TYPE))
    return jnp.where(allowed[None], scores, 0.0).astype(HALF_TYPE)

def forward_block(pieces):
    query_blk, keys_blk, value_blk, prior_bf = pieces
    scores_bf = block_scores(query_blk, keys_blk)
    local_part = jnp.einsum('hts,shd->thd', scores_bf.astype(WIDE_TYPE), value_blk.astype(WIDE_TYPE))
    carried = jnp.einsum('thd,hde->the', query_blk.astype(WIDE_TYPE), prior_bf.astype(WIDE_TYPE))
    return local_part + carried

def backward_block(pieces):
    query_blk, keys_blk, value_blk, grad_mixed, prior_bf, later_bf = pieces
    allowed = causal_mask(query_blk.shape[0])
    scores_bf = block_scores(query_blk, keys_blk).astype(WIDE_TYPE)
    query_w = query_blk.astype(WIDE_TYPE)
    keys_w = keys_blk.astype(WIDE_TYPE)
    value_w = value_blk.astype(WIDE_TYPE)
    grad_w = grad_mixed.astype(WIDE_TYPE)
    prior_w = prior_bf.astype(WIDE_TYPE)
    later_w = later_bf.astype(WIDE_TYPE)
    grad_scores = jnp.einsum('thd,shd->hts', grad_w, value_w)
    grad_scores = jnp.where(allowed[None], grad_scores, 0.0).astype(HALF_TYPE).astype(WIDE_TYPE)
    grad_query = jnp.einsum('hts,shd->thd', grad_scores, keys_w) + jnp.einsum('the,hde->thd', grad_w, prior_w)
    grad_keys = jnp.einsum('hts,thd->shd', grad_scores, query_w) + jnp.einsum('she,hde->shd', value_w, later_w)
    grad_value = jnp.einsum('hts,the->she', scores_bf, grad_w) + jnp.einsum('shd,hde->she', keys_w, later_w)
    return (grad_query.astype(HALF_TYPE), grad_keys.astype(HALF_TYPE), grad_value.astype(HALF_TYPE))

def reference(tokens, w_query, w_key, w_value, w_out, grad_out, state_in):
    group_cols = HEADS * DH // N_HEAD
    blocks = TOKENS // BLOCK
    block_shape = (blocks, BLOCK, HEADS, DH)
    query = jnp.dot(tokens, w_query, preferred_element_type=WIDE_TYPE).astype(HALF_TYPE).reshape(block_shape)
    keys = jnp.dot(tokens, w_key, preferred_element_type=WIDE_TYPE).astype(HALF_TYPE).reshape(block_shape)
    values = jnp.dot(tokens, w_value, preferred_element_type=WIDE_TYPE).astype(HALF_TYPE).reshape(block_shape)
    states = jnp.einsum('cshd,cshe->chde', keys.astype(WIDE_TYPE), values.astype(WIDE_TYPE))
    prior_bf = (state_in[None] + excl_prefix(states)).astype(HALF_TYPE)
    mixed = lax.map(forward_block, (query, keys, values, prior_bf))
    inv_norm = lax.rsqrt(lax.optimization_barrier(jnp.mean(mixed * mixed, axis=-1, keepdims=True)) + EPSILON)
    normed = (mixed * inv_norm).astype(HALF_TYPE).reshape(TOKENS, HEADS * DH)
    out_groups = normed.reshape(TOKENS, N_HEAD, group_cols).transpose(1, 0, 2)
    out_weights = w_out.reshape(N_HEAD, group_cols, D)

    def add_out(running, group_pair):
        piece_out = jnp.dot(group_pair[0], group_pair[1], preferred_element_type=WIDE_TYPE).astype(HALF_TYPE)
        piece_out = lax.optimization_barrier(piece_out)
        return (running + piece_out.astype(WIDE_TYPE), None)
    out_sum, _ = lax.scan(add_out, jnp.zeros((TOKENS, D), WIDE_TYPE), (out_groups, out_weights))
    result = out_sum.astype(HALF_TYPE)
    contract_last = (((1,), (1,)), ((), ()))
    grad_normed = lax.dot_general(grad_out, w_out, contract_last, preferred_element_type=WIDE_TYPE).reshape(block_shape)
    grad_mixed = inv_norm * (grad_normed - mixed * inv_norm * inv_norm * lax.optimization_barrier(jnp.mean(grad_normed * mixed, axis=-1, keepdims=True)))
    grad_mixed = grad_mixed.astype(HALF_TYPE)
    back_states = jnp.einsum('cthd,cthe->chde', query.astype(WIDE_TYPE), grad_mixed.astype(WIDE_TYPE))
    later_bf = excl_suffix(back_states).astype(HALF_TYPE)
    grad_state_in = lax.optimization_barrier(jnp.sum(back_states, axis=0))
    grad_query, grad_keys, grad_value = lax.map(backward_block, (query, keys, values, grad_mixed, prior_bf, later_bf))
    grad_query = grad_query.reshape(TOKENS, HEADS * DH)
    grad_keys = grad_keys.reshape(TOKENS, HEADS * DH)
    grad_value = grad_value.reshape(TOKENS, HEADS * DH)

    def split_cols(matrix):
        return matrix.reshape(matrix.shape[0], N_HEAD, group_cols).transpose(1, 0, 2)

    def add_input(running, group_set):
        piece_in = lax.dot_general(group_set[0], group_set[3], contract_last, preferred_element_type=WIDE_TYPE)
        piece_in = piece_in + lax.dot_general(group_set[1], group_set[4], contract_last, preferred_element_type=WIDE_TYPE)
        piece_in = piece_in + lax.dot_general(group_set[2], group_set[5], contract_last, preferred_element_type=WIDE_TYPE)
        piece_in = lax.optimization_barrier(piece_in.astype(HALF_TYPE))
        return (running + piece_in.astype(WIDE_TYPE), None)
    grad_tokens, _ = lax.scan(add_input, jnp.zeros((TOKENS, D), WIDE_TYPE), (split_cols(grad_query), split_cols(grad_keys), split_cols(grad_value), split_cols(w_query), split_cols(w_key), split_cols(w_value)))
    grad_wq = jnp.dot(tokens.T, grad_query, preferred_element_type=WIDE_TYPE)
    grad_wk = jnp.dot(tokens.T, grad_keys, preferred_element_type=WIDE_TYPE)
    grad_wv = jnp.dot(tokens.T, grad_value, preferred_element_type=WIDE_TYPE)
    grad_wo = jnp.dot(normed.T, grad_out, preferred_element_type=WIDE_TYPE)
    return (result, grad_tokens, grad_wq, grad_wk, grad_wv, grad_wo, grad_state_in)
```

```python
import jax
import jax.numpy as jnp
from jax import lax
from jax.experimental import pallas as pl
from jax.experimental.pallas import tpu as pltpu
from jax.sharding import PartitionSpec as P

DH = 128
BLOCK = 256
EPSILON = 1e-06
WIDE = jnp.float32
HALF = jnp.bfloat16
MESH = pl.DeviceIdType.MESH
NN = (((1,), (0,)), ((), ()))
NT = (((1,), (1,)), ((), ()))
TN = (((0,), (0,)), ((), ()))


def mul(left, right, dims=NN):
    return lax.dot_general(left, right, dims, preferred_element_type=WIDE)


def inner_size(count):
    inner = 1
    while 4 * inner * inner <= count:
        inner *= 2
    return inner


class Line:
    def __init__(self, place, size, device):
        self.place, self.size, self.device = place, size, device

    def has(self, way):
        return self.place < self.size - 1 if way == 0 else self.place > 0

    def next(self, way):
        return self.device(self.place + (1 if way == 0 else -1))


class Gather:
    def __init__(self, source, slots, recv, sent_outer, sent_inner, outer, inner, cut, seen):
        self.source, self.slots, self.recv = source, slots, recv
        self.sent_outer, self.sent_inner = sent_outer, sent_inner
        self.outer, self.inner, self.seen = outer, inner, seen
        rows = slots.shape[1]
        self.parts = [part for part in ((0, 0, cut), (1, cut, rows - cut)) if part[2]]

    def slot(self, place_outer, place_inner):
        return place_outer * self.inner.size + place_inner

    def copy(self, part, slot, line, way, source=None):
        number, start, rows = part
        sent = self.sent_outer if line is self.outer else self.sent_inner
        piece = self.slots.at[slot, pl.ds(start, rows)]
        return pltpu.make_async_remote_copy(
            src_ref=piece if source is None else source.at[pl.ds(start, rows)],
            dst_ref=piece,
            send_sem=sent.at[number, slot, way],
            recv_sem=self.recv.at[number, slot],
            device_id=line.next(way),
            device_id_type=MESH,
        )

    def send(self, part, slot, line, way, also=True, source=None):
        @pl.when(line.has(way) & also)
        def _():
            self.copy(part, slot, line, way, source).start()

    def arrive(self, part, slot):
        number, start, rows = part
        piece = self.slots.at[slot, pl.ds(start, rows)]
        pltpu.make_async_copy(piece, piece, self.recv.at[number, slot]).wait()

    def own(self, line):
        slot = self.slot(self.outer.place, self.inner.place)
        for part in self.parts:
            for way in (0, 1):
                self.send(part, slot, line, way, source=self.source)

    def cross_row(self):
        for part in self.parts[1:]:
            for way in (0, 1):
                for step in range(1, self.inner.size):
                    place = self.inner.place + (-step if way == 0 else step)

                    @pl.when((place >= 0) & (place < self.inner.size))
                    def _():
                        slot = self.slot(self.outer.place, place)
                        self.arrive(part, slot)
                        self.send(part, slot, self.inner, way)
                        self.send(part, slot, self.outer, 0)
                        self.send(part, slot, self.outer, 1)

    def from_outer(self, distance):
        @pl.loop(0, 2)
        def _(side):
            place = self.outer.place + (2 * side - 1) * distance

            @pl.when((place >= 0) & (place < self.outer.size))
            def _():
                mine = self.slot(place, self.inner.place)
                for part in self.parts:
                    owners = [self.inner.place] if part[0] == 0 else range(self.inner.size)
                    for owner in owners:
                        slot = self.slot(place, owner)
                        self.arrive(part, slot)
                        self.send(part, slot, self.outer, 0, side == 0)
                        self.send(part, slot, self.outer, 1, side == 1)
                    if part[0] == 0:
                        self.send(part, mine, self.inner, 0)
                        self.send(part, mine, self.inner, 1)
                self.seen(mine)

    def from_inner(self, distance):
        @pl.loop(0, 2)
        def _(side):
            row = self.outer.place + (2 * side - 1) * distance

            @pl.when((row >= 0) & (row < self.outer.size) & ((distance > 0) | (side == 0)))
            def _():
                @pl.loop(0, 2)
                def _(way):
                    @pl.loop(1, self.inner.size)
                    def _(step):
                        place = self.inner.place + (2 * way - 1) * step

                        @pl.when((place >= 0) & (place < self.inner.size))
                        def _():
                            slot = self.slot(row, place)
                            self.arrive(self.parts[0], slot)
                            self.send(self.parts[0], slot, self.inner, 0, way == 0)
                            self.send(self.parts[0], slot, self.inner, 1, way == 1)
                            self.seen(slot)

    def finish(self):
        @pl.loop(0, self.outer.size)
        def _(row):
            @pl.loop(0, self.inner.size)
            def _(place):
                slot = self.slot(row, place)
                for part in self.parts:
                    for way in (0, 1):
                        passed = (row <= self.outer.place) if way == 0 else (row >= self.outer.place)
                        if part[0] == 0:
                            passed &= place == self.inner.place

                        @pl.when(self.outer.has(way) & passed)
                        def _():
                            self.copy(part, slot, self.outer, way).wait_send()

                        passed = (place <= self.inner.place) if way == 0 else (place >= self.inner.place)
                        if part[0] == 1:
                            passed &= row == self.outer.place

                        @pl.when(self.inner.has(way) & passed)
                        def _():
                            self.copy(part, slot, self.inner, way).wait_send()


class Reduce:
    def __init__(self, line, term, landed, sent, recv):
        self.line, self.term, self.landed, self.sent, self.recv = line, term, landed, sent, recv

    def copy(self, way, owner):
        return pltpu.make_async_remote_copy(
            src_ref=self.term(owner),
            dst_ref=self.landed(way, owner),
            send_sem=self.sent(way, owner),
            recv_sem=self.recv(way, owner),
            device_id=self.line.next(way),
            device_id_type=MESH,
        )

    def arrive(self, way, owner):
        piece = self.landed(way, owner)
        pltpu.make_async_copy(piece, piece, self.recv(way, owner)).wait()

    def add(self, way, owner):
        @pl.when(self.line.has(1 - way))
        def _():
            self.arrive(way, owner)
            total = self.term(owner)[...].astype(WIDE) + self.landed(way, owner)[...].astype(WIDE)
            self.term(owner)[...] = total.astype(HALF)

    def step(self, distance):
        for way in (0, 1):
            owner = self.line.place + (distance if way == 0 else -distance)

            @pl.when((owner >= 0) & (owner < self.line.size))
            def _():
                self.add(way, owner)
                self.copy(way, owner).start()

    def total(self, out):
        place = self.line.place
        out[...] = self.term(place)[...].astype(out.dtype)
        for way in (0, 1):

            @pl.when(self.line.has(1 - way))
            def _():
                self.arrive(way, place)
                out[...] = (out[...].astype(WIDE) + self.landed(way, place)[...].astype(WIDE)).astype(out.dtype)

    def finish(self):
        for distance in range(1, self.line.size):
            for way in (0, 1):
                owner = self.line.place + (distance if way == 0 else -distance)

                @pl.when((owner >= 0) & (owner < self.line.size))
                def _():
                    self.copy(way, owner).wait_send()


def layer(
    sizes,
    tokens_in, wq_in, wk_in, wv_in, wo_in, cot_in, state_in,
    result, grad_tokens, grad_wq, grad_wk, grad_wv, grad_wo, grad_state,
    tok, cot, moved_tok, moved_cot, wq, wk, wv, wo, state,
    acc, grad_normed, mixed, query, keys, values, scores_t, prior,
    fore, rear, grads, normed,
    terms, terms_outer, terms_inner, summed,
    inputs, inputs_inner, inputs_outer,
    load_sem, fore_sem, rear_sem,
    tok_recv, tok_outer, tok_inner, tok_moved, tok_landed,
    cot_recv, cot_outer, cot_inner, cot_moved, cot_landed,
    grads_recv, grads_outer, grads_inner, normed_recv, normed_outer, normed_inner,
    terms_outer_sem, terms_inner_sem, inputs_inner_sem, inputs_outer_sem,
):
    seq, head, cut = sizes
    head_inner, seq_inner = inner_size(head), inner_size(seq)
    head_outer, seq_outer = head // head_inner, seq // seq_inner
    shared = head // seq
    rows, wide = tok.shape[1:]
    columns = wq.shape[1]
    heads_here = columns // DH
    s, h = lax.axis_index("seq"), lax.axis_index("head")
    z, y = h // head_inner, h % head_inner
    outer = Line(z, head_outer, lambda place: (s, place * head_inner + y))
    inner = Line(y, head_inner, lambda place: (s, z * head_inner + place))
    chip = Line(s // seq_inner, seq_outer, lambda place: (place * seq_inner + s % seq_inner, h))
    core = Line(s % seq_inner, seq_inner, lambda place: (s // seq_inner * seq_inner + place, h))

    loads = [
        pltpu.make_async_copy(source, target, load_sem.at[number])
        for number, (source, target) in enumerate(
            [
                (tokens_in, tok.at[h]),
                (wq_in, wq), (wk_in, wk), (wv_in, wv),
                (cot_in, cot.at[h]), (wo_in, wo), (state_in, state),
            ]
        )
    ]
    for load in loads:
        load.start()

    barrier = pltpu.get_barrier_semaphore()
    expected = seq - 1
    for line in (outer, inner):
        for way in (0, 1):
            expected = expected + line.has(way).astype(jnp.int32)

            @pl.when(line.has(way))
            def _():
                pl.semaphore_signal(barrier, inc=1, device_id=line.next(way), device_id_type=MESH)
    for other in range(1, seq):
        pl.semaphore_signal(barrier, inc=1, device_id=((s + other) % seq, h), device_id_type=MESH)
    pl.semaphore_wait(barrier, expected)

    def moves(slots, moved, sent, landed):
        def copy(slot):
            return pltpu.make_async_remote_copy(
                src_ref=slots.at[slot],
                dst_ref=moved.at[s, slot % shared],
                send_sem=sent.at[slot],
                recv_sem=landed.at[s, slot % shared],
                device_id=(slot // shared, h),
                device_id_type=MESH,
            )

        def start(slot):
            @pl.when(slot // shared != s)
            def _():
                copy(slot).start()

            @pl.when(slot // shared == s)
            def _():
                own = moved.at[s, slot % shared]
                pltpu.make_async_copy(slots.at[slot], own, landed.at[s, slot % shared]).start()

        def row(distance):
            @pl.loop(0, 2)
            def _(side):
                place = z + (2 * side - 1) * distance

                @pl.when((place >= 0) & (place < head_outer))
                def _():
                    for owner in range(head_inner):
                        start(place * head_inner + owner)

        def finish():
            @pl.loop(0, head)
            def _(slot):
                @pl.when(slot // shared != s)
                def _():
                    copy(slot).wait_send()

        return start, row, finish

    move_tok, move_tok_row, finish_tok = moves(tok, moved_tok, tok_moved, tok_landed)
    move_cot, move_cot_row, finish_cot = moves(cot, moved_cot, cot_moved, cot_landed)

    def project(slot):
        block = tok[slot]
        span = pl.ds(pl.multiple_of(slot * wide, wide), wide)
        for number, weight in enumerate((wq, wk, wv)):
            acc[number] += mul(block, weight[span, :])

        @pl.when((abs(slot // head_inner - z) < head_outer - 1))
        def _():
            move_tok(slot)

    def pull(slot):
        span = pl.ds(pl.multiple_of(slot * wide, wide), wide)
        grad_normed[...] += mul(cot[slot], wo[:, span], NT)
        move_cot(slot)

    tok_gather = Gather(tokens_in, tok, tok_recv, tok_outer, tok_inner, outer, inner, cut, project)
    cot_gather = Gather(cot_in, cot, cot_recv, cot_outer, cot_inner, outer, inner, cut, pull)
    nothing = lambda slot: None
    grads_gather = Gather(
        grads.at[s], grads, grads_recv, grads_outer, grads_inner, chip, core, rows, nothing
    )
    normed_gather = Gather(
        normed.at[s], normed, normed_recv, normed_outer, normed_inner, chip, core, rows, nothing
    )

    tok_gather.own(outer)
    tok_gather.own(inner)
    acc[...] = jnp.zeros_like(acc)
    grad_normed[...] = jnp.zeros_like(grad_normed)
    for load in loads[:4]:
        load.wait()
    project(h)
    tok_gather.cross_row()

    @pl.loop(1, head_outer + 1)
    def _(distance):
        pl.when(distance == head_outer - 1)(lambda: cot_gather.own(outer))
        pl.when(distance < head_outer)(lambda: tok_gather.from_outer(distance))
        pl.when(distance == head_outer - 1)(lambda: cot_gather.own(inner))
        tok_gather.from_inner(distance - 1)


    for number, target in enumerate((query, keys, values)):
        target[...] = acc[number].astype(HALF)

    def part(ref, number):
        return ref[:, number * DH : (number + 1) * DH]

    for number in range(heads_here):
        fore[s, number] = mul(part(keys, number), part(values, number), TN).astype(HALF)

    def share(states, sems, wanted):
        def copy(other):
            return pltpu.make_async_remote_copy(
                src_ref=states.at[s],
                dst_ref=states.at[s],
                send_sem=sems.at[0, other],
                recv_sem=sems.at[1, s],
                device_id=(other, h),
                device_id_type=MESH,
            )

        def start():
            for other in range(seq):
                pl.when((other != s) & wanted(s, other))(lambda: copy(other).start())

        def arrive():
            for other in range(seq):

                @pl.when((other != s) & wanted(other, s))
                def _():
                    pltpu.make_async_copy(states.at[other], states.at[other], sems.at[1, other]).wait()

        def finish():
            for other in range(seq):
                pl.when((other != s) & wanted(s, other))(lambda: copy(other).wait_send())

        return start, arrive, finish

    start_fore, arrive_fore, finish_fore = share(fore, fore_sem, lambda source, target: source < target)
    start_rear, arrive_rear, finish_rear = share(rear, rear_sem, lambda source, target: target >= 0)
    start_fore()
    for load in loads[4:]:
        load.wait()
    pull(h)
    cot_gather.cross_row()
    cot_gather.from_outer(1)
    move_tok_row(head_outer - 1)

    below = lax.broadcasted_iota(jnp.int32, (rows, rows), 1) <= lax.broadcasted_iota(jnp.int32, (rows, rows), 0)
    above = lax.broadcasted_iota(jnp.int32, (rows, rows), 1) >= lax.broadcasted_iota(jnp.int32, (rows, rows), 0)
    for number in range(heads_here):
        query_h, keys_h = part(query, number), part(keys, number)
        scores = jnp.where(below, mul(query_h, keys_h, NT), 0.0).astype(HALF)
        scores_t[number] = jnp.where(above, mul(keys_h, query_h, NT), 0.0).astype(HALF)
        mixed[:, number * DH : (number + 1) * DH] = mul(scores, part(values, number))
    arrive_fore()
    for number in range(heads_here):
        before = state[number]
        for other in range(seq):
            before = before + jnp.where(other < s, fore[other, number].astype(WIDE), 0.0)
        prior[number] = before.astype(HALF)
        whole = part(mixed, number) + mul(part(query, number), prior[number])
        mixed[:, number * DH : (number + 1) * DH] = whole
        inv_norm = lax.rsqrt(jnp.mean(whole * whole, axis=-1, keepdims=True) + EPSILON)
        normed[s, :, number * DH : (number + 1) * DH] = (whole * inv_norm).astype(HALF)
    normed_gather.own(chip)
    normed_gather.own(core)

    @pl.loop(0, head)
    def _(slot):
        span = pl.ds(pl.multiple_of(slot * wide, wide), wide)
        terms[slot // head_inner, slot % head_inner] = mul(normed[s], wo[:, span]).astype(HALF)

    outer_sums = [
        Reduce(
            outer,
            lambda owner, place=place: terms.at[owner, place],
            lambda way, owner, place=place: terms_outer.at[way, owner, place],
            lambda way, owner, place=place: terms_outer_sem.at[0, way, owner, place],
            lambda way, owner, place=place: terms_outer_sem.at[1, way, owner, place],
        )
        for place in range(head_inner)
    ]
    inner_sum = Reduce(
        inner,
        lambda owner: summed.at[owner],
        lambda way, owner: terms_inner.at[way, owner],
        lambda way, owner: terms_inner_sem.at[0, way, owner],
        lambda way, owner: terms_inner_sem.at[1, way, owner],
    )

    def result_step(distance):
        for one in outer_sums:
            one.step(distance)

    result_step(head_outer - 1)
    cot_gather.from_inner(0)
    for distance in range(2, head_outer):
        cot_gather.from_outer(distance)
        cot_gather.from_inner(distance - 1)
    for distance in range(head_outer - 2, 1, -1):
        result_step(distance)
    cot_gather.from_inner(head_outer - 1)

    for number in range(heads_here):
        whole, pulled = part(mixed, number), part(grad_normed, number)
        inv_norm = lax.rsqrt(jnp.mean(whole * whole, axis=-1, keepdims=True) + EPSILON)
        slope = jnp.mean(pulled * whole, axis=-1, keepdims=True)
        grad_mixed = (inv_norm * (pulled - whole * inv_norm * inv_norm * slope)).astype(HALF)
        grads[s, :, number * DH : (number + 1) * DH] = grad_mixed
        rear[s, number] = mul(part(query, number), grad_mixed, TN).astype(HALF)
    start_rear()
    for number in range(heads_here):
        span = slice(number * DH, (number + 1) * DH)
        grad_mixed = grads[s, :, span]
        query_h, keys_h, values_h = part(query, number), part(keys, number), part(values, number)
        grad_scores = jnp.where(below, mul(grad_mixed, values_h, NT), 0.0).astype(HALF)
        grad_scores_t = jnp.where(above, mul(values_h, grad_mixed, NT), 0.0).astype(HALF)
        acc[0, :, span] = mul(grad_scores, keys_h) + mul(grad_mixed, prior[number], NT)
        acc[1, :, span] = mul(grad_scores_t, query_h)
        acc[2, :, span] = mul(scores_t[number], grad_mixed)
    arrive_rear()
    for number in range(heads_here):
        later = jnp.zeros((DH, DH), WIDE)
        every = jnp.zeros((DH, DH), WIDE)
        for other in range(seq):
            one = rear[other, number].astype(WIDE)
            later = later + jnp.where(other > s, one, 0.0)
            every = every + one
        grad_state[number] = every
        later = later.astype(HALF)
        span = slice(number * DH, (number + 1) * DH)
        acc[1, :, span] += mul(part(values, number), later, NT)
        acc[2, :, span] += mul(part(keys, number), later)
    for number in range(3):
        grads[s, :, number * columns : (number + 1) * columns] = acc[number].astype(HALF)

    input_sums = lambda place: Reduce(
        inner,
        lambda owner: inputs.at[place, owner],
        lambda way, owner: inputs_inner.at[way, place, owner],
        lambda way, owner: inputs_inner_sem.at[0, way, place, owner],
        lambda way, owner: inputs_inner_sem.at[1, way, place, owner],
    )
    input_sum = Reduce(
        outer,
        lambda owner: inputs.at[owner, y],
        lambda way, owner: inputs_outer.at[way, owner],
        lambda way, owner: inputs_outer_sem.at[0, way, owner],
        lambda way, owner: inputs_outer_sem.at[1, way, owner],
    )

    def each_row(distance, act):
        @pl.loop(0, 2)
        def _(side):
            place = z + (2 * side - 1) * distance
            pl.when((place >= 0) & (place < head_outer) & ((distance > 0) | (side == 0)))(lambda: act(place))

    def input_terms(place):
        @pl.loop(0, head_inner)
        def _(turn):
            owner = (y + 1 + turn) % head_inner
            span = pl.ds(pl.multiple_of((place * head_inner + owner) * wide, wide), wide)
            term = mul(grads[s, :, :columns], wq[span, :], NT)
            term += mul(grads[s, :, columns : 2 * columns], wk[span, :], NT)
            term += mul(grads[s, :, 2 * columns :], wv[span, :], NT)
            inputs[place, owner] = term.astype(HALF)

        sums = input_sums(place)
        for distance in range(head_inner - 1, 0, -1):
            sums.step(distance)

    def input_inner_total(place):
        sums = input_sums(place)
        for way in (0, 1):
            sums.add(way, y)

    def input_step(distance):
        each_row(distance, input_inner_total)
        if distance:
            input_sum.step(distance)

    @pl.loop(0, head_outer)
    def _(turn):
        each_row(head_outer - 1 - turn, input_terms)
    grads_gather.own(chip)
    grads_gather.own(core)

    def weight_grads(place):
        for number in range(shared):
            piece, block = moved_tok.at[place, number], moved_cot.at[place, number]
            span = slice(number * wide, (number + 1) * wide)
            pltpu.make_async_copy(piece, piece, tok_landed.at[place, number]).wait()
            pltpu.make_async_copy(block, block, cot_landed.at[place, number]).wait()
            for target, start in ((grad_wq, 0), (grad_wk, columns), (grad_wv, 2 * columns)):
                target[span, :] += mul(piece[...], grads[place, :, start : start + columns], TN)
            grad_wo[:, span] += mul(normed[place], block[...], TN)

    for target in (grad_wq, grad_wk, grad_wv, grad_wo):
        target[...] = jnp.zeros_like(target)
    if head_outer > 2:
        result_step(1)
    normed_gather.from_outer(1)
    normed_gather.from_inner(0)
    for distance in range(2, seq_outer):
        normed_gather.from_outer(distance)
        normed_gather.from_inner(distance - 1)
    normed_gather.from_inner(seq_outer - 1)
    weight_grads(s)
    input_step(head_outer - 1)
    for place, one in enumerate(outer_sums):
        one.total(summed.at[place])
    for distance in range(head_inner - 1, 0, -1):
        inner_sum.step(distance)
    grads_gather.from_outer(1)
    grads_gather.from_inner(0)
    for distance in range(2, seq_outer):
        grads_gather.from_outer(distance)
        grads_gather.from_inner(distance - 1)
    for distance in range(head_outer - 2, 0, -1):
        input_step(distance)
    grads_gather.from_inner(seq_outer - 1)

    @pl.loop(1, seq)
    def _(other):
        weight_grads((s + other) % seq)

    inner_sum.total(result)
    input_step(0)
    input_sum.total(grad_tokens)

    for one in (tok_gather, cot_gather, grads_gather, normed_gather, *outer_sums, inner_sum, input_sum):
        one.finish()
    pl.loop(0, head_outer)(lambda place: input_sums(place).finish())
    for finish in (finish_tok, finish_cot, finish_fore, finish_rear):
        finish()


def solution(mesh):
    seq, head = mesh.shape["seq"], mesh.shape["head"]

    def on_device(tokens, w_query, w_key, w_value, w_out, grad_out, state_in):
        rows, wide = tokens.shape
        depth, columns = w_query.shape
        heads_here = columns // DH
        shared = head // seq
        assert rows == BLOCK and head % seq == 0
        head_inner, seq_inner = inner_size(head), inner_size(seq)
        head_outer, seq_outer = head // head_inner, seq // seq_inner
        cut = rows
        vmem = lambda *shape: pltpu.VMEM(shape, HALF)
        full = lambda *shape: pltpu.VMEM(shape, WIDE)
        dma = lambda *shape: pltpu.SemaphoreType.DMA(shape)
        gathers = lambda: [dma(2, head), dma(2, head, 2), dma(2, head, 2), dma(head), dma(seq, shared)]
        spans = lambda: [dma(1, seq), dma(1, seq, 2), dma(1, seq, 2)]
        outs = [
            ((rows, wide), HALF), ((rows, wide), WIDE),
            ((shared * wide, columns), WIDE), ((shared * wide, columns), WIDE), ((shared * wide, columns), WIDE),
            ((columns, shared * wide), WIDE), ((heads_here, DH, DH), WIDE),
        ]
        return pl.pallas_call(
            lambda *refs: layer((seq, head, cut), *refs),
            out_shape=[jax.ShapeDtypeStruct(shape, kind) for shape, kind in outs],
            in_specs=[pl.BlockSpec(memory_space=pl.ANY)] * 7,
            out_specs=[pl.BlockSpec(memory_space=pltpu.VMEM)] * 7,
            scratch_shapes=[
                vmem(head, rows, wide), vmem(head, rows, wide),
                vmem(seq, shared, rows, wide), vmem(seq, shared, rows, wide),
                vmem(depth, columns), vmem(depth, columns), vmem(depth, columns), vmem(columns, depth),
                full(heads_here, DH, DH),
                full(3, rows, columns), full(rows, columns), full(rows, columns),
                vmem(rows, columns), vmem(rows, columns), vmem(rows, columns),
                vmem(heads_here, rows, rows), vmem(heads_here, DH, DH),
                vmem(seq, heads_here, DH, DH), vmem(seq, heads_here, DH, DH),
                vmem(seq, rows, 3 * columns), vmem(seq, rows, columns),
                vmem(head_outer, head_inner, rows, wide), vmem(2, head_outer, head_inner, rows, wide),
                vmem(2, head_inner, rows, wide), vmem(head_inner, rows, wide),
                vmem(head_outer, head_inner, rows, wide), vmem(2, head_outer, head_inner, rows, wide),
                vmem(2, head_outer, rows, wide),
                dma(7), dma(2, seq), dma(2, seq),
                *gathers(), *gathers(), *spans(), *spans(),
                dma(2, 2, head_outer, head_inner), dma(2, 2, head_inner),
                dma(2, 2, head_outer, head_inner), dma(2, 2, head_outer),
            ],
            compiler_params=pltpu.CompilerParams(
                collective_id=0, has_side_effects=True, vmem_limit_bytes=52 * 1024 * 1024
            ),
        )(tokens, w_query, w_key, w_value, w_out, grad_out, state_in)

    by_head = P(None, "head")
    tiled = P("seq", "head")
    return jax.shard_map(
        on_device,
        mesh=mesh,
        in_specs=(tiled, by_head, by_head, by_head, P("head", None), tiled, P("head", None, None)),
        out_specs=(tiled, tiled, tiled, tiled, tiled, P("head", "seq"), P("head", None, None)),
        check_vma=False,
    )
```

```python
import jax
import jax.numpy as jnp
from jax import lax
from jax.experimental import pallas as pl
from jax.experimental.pallas import tpu as pltpu
from jax.sharding import PartitionSpec as P

DH = 128
BLOCK = 256
EPSILON = 1e-06
WIDE = jnp.float32
HALF = jnp.bfloat16
MESH = pl.DeviceIdType.MESH
NN = (((1,), (0,)), ((), ()))
NT = (((1,), (1,)), ((), ()))
TN = (((0,), (0,)), ((), ()))


def mul(left, right, dims=NN):
    return lax.dot_general(left, right, dims, preferred_element_type=WIDE)


def parts(rows, shares):
    unit, start, cut = rows // 16, 0, []
    for order, share in shares:
        cut.append((order, start, share * unit))
        start += share * unit
    return cut


def gather_parts(rows):
    return parts(rows, ((0, 7), (0, 6), (1, 3)))


def result_parts(rows):
    return parts(rows, ((1, 10), (0, 6)))


def input_parts(rows):
    return parts(rows, ((0, 8), (0, 8)))


def inner_size(count):
    inner = 1
    while 4 * inner * inner <= count:
        inner *= 2
    return inner


class Line:
    def __init__(self, place, size, device):
        self.place, self.size, self.device = place, size, device

    def has(self, way):
        return self.place < self.size - 1 if way == 0 else self.place > 0

    def next(self, way):
        return self.device(self.place + (1 if way == 0 else -1))


class Gather:
    def __init__(self, source, slots, recv, sent_outer, sent_inner, outer, inner, parts, seen):
        self.source, self.slots, self.recv = source, slots, recv
        self.sent_outer, self.sent_inner = sent_outer, sent_inner
        self.outer, self.inner, self.seen = outer, inner, seen
        self.parts = [(number, *part) for number, part in enumerate(parts)]

    def slot(self, place_outer, place_inner):
        return place_outer * self.inner.size + place_inner

    def copy(self, part, slot, line, way, source=None):
        number, _, start, rows = part
        sent = self.sent_outer if line is self.outer else self.sent_inner
        piece = self.slots.at[slot, pl.ds(start, rows)]
        return pltpu.make_async_remote_copy(
            src_ref=piece if source is None else source.at[pl.ds(start, rows)],
            dst_ref=piece,
            send_sem=sent.at[number, slot, way],
            recv_sem=self.recv.at[number, slot],
            device_id=line.next(way),
            device_id_type=MESH,
        )

    def send(self, part, slot, line, way, also=True, source=None):
        @pl.when(line.has(way) & also)
        def _():
            self.copy(part, slot, line, way, source).start()

    def arrive(self, part, slot):
        number, _, start, rows = part
        piece = self.slots.at[slot, pl.ds(start, rows)]
        pltpu.make_async_copy(piece, piece, self.recv.at[number, slot]).wait()

    def own(self, line, orders=(0, 1)):
        slot = self.slot(self.outer.place, self.inner.place)
        for part in self.parts:
            if part[1] in orders:
                for way in (0, 1):
                    self.send(part, slot, line, way, source=self.source)

    def cross_row(self):
        for part in self.parts:
            if part[1] == 1:
                for way in (0, 1):
                    for step in range(1, self.inner.size):
                        place = self.inner.place + (-step if way == 0 else step)

                        @pl.when((place >= 0) & (place < self.inner.size))
                        def _():
                            slot = self.slot(self.outer.place, place)
                            self.arrive(part, slot)
                            self.send(part, slot, self.inner, way)
                            self.send(part, slot, self.outer, 0)
                            self.send(part, slot, self.outer, 1)

    def each_side(self, distance, act):
        @pl.loop(0, 2)
        def _(side):
            row = self.outer.place + (2 * side - 1) * distance

            @pl.when((row >= 0) & (row < self.outer.size) & ((distance > 0) | (side == 0)))
            def _():
                act(side, row)

    def from_outer(self, distance):
        steps = [(part, 0) for part in self.parts]
        steps += [(part, turn) for turn in range(1, self.inner.size) for part in self.parts if part[1] == 1]
        for part, turn in steps:

            def pass_on(side, row):
                slot = self.slot(row, (self.inner.place + turn) % self.inner.size)
                self.arrive(part, slot)
                self.send(part, slot, self.outer, 0, side == 0)
                self.send(part, slot, self.outer, 1, side == 1)
                if part[1] == 0:
                    self.send(part, slot, self.inner, 0)
                    self.send(part, slot, self.inner, 1)

            self.each_side(distance, pass_on)
        self.each_side(distance, lambda side, row: self.seen(self.slot(row, self.inner.place)))

    def from_inner(self, distance):
        def each_place(side, row):
            @pl.loop(0, 2)
            def _(way):
                @pl.loop(1, self.inner.size)
                def _(step):
                    place = self.inner.place + (2 * way - 1) * step

                    @pl.when((place >= 0) & (place < self.inner.size))
                    def _():
                        slot = self.slot(row, place)
                        for part in self.parts:
                            if part[1] == 0:
                                self.arrive(part, slot)
                                self.send(part, slot, self.inner, 0, way == 0)
                                self.send(part, slot, self.inner, 1, way == 1)
                        self.seen(slot)

        self.each_side(distance, each_place)

    def finish(self):
        @pl.loop(0, self.outer.size)
        def _(row):
            @pl.loop(0, self.inner.size)
            def _(place):
                slot = self.slot(row, place)
                for part in self.parts:
                    for way in (0, 1):
                        passed = (row <= self.outer.place) if way == 0 else (row >= self.outer.place)
                        if part[1] == 0:
                            passed &= place == self.inner.place

                        @pl.when(self.outer.has(way) & passed)
                        def _():
                            self.copy(part, slot, self.outer, way).wait_send()

                        passed = (place <= self.inner.place) if way == 0 else (place >= self.inner.place)
                        if part[1] == 1:
                            passed &= row == self.outer.place

                        @pl.when(self.inner.has(way) & passed)
                        def _():
                            self.copy(part, slot, self.inner, way).wait_send()


class Reduce:
    def __init__(self, line, term, landed, sems):
        self.line, self.term, self.landed, self.sems = line, term, landed, sems

    def copy(self, way, owner):
        return pltpu.make_async_remote_copy(
            src_ref=self.term(owner),
            dst_ref=self.landed(way, owner),
            send_sem=self.sems(0, way, owner),
            recv_sem=self.sems(1, way, owner),
            device_id=self.line.next(way),
            device_id_type=MESH,
        )

    def arrive(self, way, owner, act):
        @pl.when(self.line.has(1 - way))
        def _():
            piece = self.landed(way, owner)
            pltpu.make_async_copy(piece, piece, self.sems(1, way, owner)).wait()
            act(piece[...].astype(WIDE))

    def add(self, way, owner):
        term = self.term(owner)

        def act(value):
            term[...] = (term[...].astype(WIDE) + value).astype(HALF)

        self.arrive(way, owner, act)

    def each(self, distance, act):
        for way in (0, 1):
            owner = self.line.place + (distance if way == 0 else -distance)
            pl.when((owner >= 0) & (owner < self.line.size))(lambda: act(way, owner))

    def step(self, distance):
        def act(way, owner):
            self.add(way, owner)
            self.copy(way, owner).start()

        self.each(distance, act)

    def finish(self):
        for distance in range(1, self.line.size):
            self.each(distance, lambda way, owner: self.copy(way, owner).wait_send())


class Scatter:
    def __init__(self, terms, landed, sems, outer, inner, parts):
        self.terms, self.landed, self.sems = terms, landed, sems
        self.outer, self.inner = outer, inner
        self.parts = [(number, *part) for number, part in enumerate(parts)]

    def along_outer(self, part, place):
        number, _, start, rows = part
        span = pl.ds(start, rows)
        return Reduce(
            self.outer,
            lambda owner: self.terms.at[owner, place, span],
            lambda way, owner: self.landed.at[0, way, owner, place, span],
            lambda end, way, owner: self.sems.at[number, 0, end, way, owner, place],
        )

    def along_inner(self, part, row):
        number, _, start, rows = part
        span = pl.ds(start, rows)
        return Reduce(
            self.inner,
            lambda owner: self.terms.at[row, owner, span],
            lambda way, owner: self.landed.at[1, way, row, owner, span],
            lambda end, way, owner: self.sems.at[number, 1, end, way, row, owner],
        )

    def steps_inner(self, part, row):
        line = self.along_inner(part, row)
        for distance in range(self.inner.size - 1, 0, -1):
            line.step(distance)

    def start_row(self, row):
        for part in self.parts:
            if part[1] == 0:
                self.steps_inner(part, row)

    def outer_first(self, distance):
        for part in self.parts:
            if part[1] == 1:
                for place in range(self.inner.size):
                    self.along_outer(part, place).step(distance)

    def outer_second(self, distance):
        for part in self.parts:
            if part[1] == 0:

                def act(way, row):
                    for side in (0, 1):
                        self.along_inner(part, row).add(side, self.inner.place)

                self.along_outer(part, self.inner.place).each(distance, act)
                self.along_outer(part, self.inner.place).step(distance)

    def turn(self):
        for part in self.parts:
            if part[1] == 1:
                for place in range(self.inner.size):

                    @pl.when(place != self.inner.place)
                    def _():
                        for way in (0, 1):
                            self.along_outer(part, place).add(way, self.outer.place)

                self.steps_inner(part, self.outer.place)

    def total(self, out):
        row, place = self.outer.place, self.inner.place
        for part in self.parts:
            span = pl.ds(part[2], part[3])
            held = [self.terms[row, place, span].astype(WIDE)]
            out[span, :] = held[0].astype(out.dtype)

            def act(value):
                out[span, :] = (out[span, :].astype(WIDE) + value).astype(out.dtype)

            for way in (0, 1):
                self.along_outer(part, place).arrive(way, row, act)
                self.along_inner(part, row).arrive(way, place, act)

    def finish(self):
        for part in self.parts:
            if part[1] == 0:
                pl.loop(0, self.outer.size)(lambda row: self.along_inner(part, row).finish())
                self.along_outer(part, self.inner.place).finish()
            else:
                pl.loop(0, self.inner.size)(lambda place: self.along_outer(part, place).finish())
                self.along_inner(part, self.outer.place).finish()


def layer(
    sizes,
    tokens_in, wq_in, wk_in, wv_in, wo_in, cot_in, state_in,
    result, grad_tokens, grad_wq, grad_wk, grad_wv, grad_wo, grad_state,
    tok, cot, moved_tok, moved_cot, wq, wk, wv, wo, state,
    acc, grad_normed, mixed, query, keys, values, scores_t, prior,
    fore, rear, grads, normed,
    terms, terms_landed, inputs, inputs_landed, total,
    load_sem, fore_sem, rear_sem,
    tok_recv, tok_outer, tok_inner, tok_moved, tok_landed,
    cot_recv, cot_outer, cot_inner, cot_moved, cot_landed,
    grads_recv, grads_outer, grads_inner, normed_recv, normed_outer, normed_inner,
    terms_sem, inputs_sem,
):
    seq, head = sizes
    head_inner, seq_inner = inner_size(head), inner_size(seq)
    head_outer, seq_outer = head // head_inner, seq // seq_inner
    shared = head // seq
    rows, wide = tok.shape[1:]
    columns = wq.shape[1]
    heads_here = columns // DH
    s, h = lax.axis_index("seq"), lax.axis_index("head")
    z, y = h // head_inner, h % head_inner
    outer = Line(z, head_outer, lambda place: (s, place * head_inner + y))
    inner = Line(y, head_inner, lambda place: (s, z * head_inner + place))
    chip = Line(s // seq_inner, seq_outer, lambda place: (place * seq_inner + s % seq_inner, h))
    core = Line(s % seq_inner, seq_inner, lambda place: (s // seq_inner * seq_inner + place, h))

    loads = [
        pltpu.make_async_copy(source, target, load_sem.at[number])
        for number, (source, target) in enumerate(
            [
                (tokens_in, tok.at[h]),
                (wq_in, wq), (wk_in, wk), (wv_in, wv),
                (cot_in, cot.at[h]), (wo_in, wo), (state_in, state),
            ]
        )
    ]
    for load in loads:
        load.start()

    barrier = pltpu.get_barrier_semaphore()
    expected = seq - 1
    for line in (outer, inner):
        for way in (0, 1):
            expected = expected + line.has(way).astype(jnp.int32)

            @pl.when(line.has(way))
            def _():
                pl.semaphore_signal(barrier, inc=1, device_id=line.next(way), device_id_type=MESH)
    for other in range(1, seq):
        pl.semaphore_signal(barrier, inc=1, device_id=((s + other) % seq, h), device_id_type=MESH)
    pl.semaphore_wait(barrier, expected)

    def moves(slots, moved, sent, landed):
        def copy(slot):
            return pltpu.make_async_remote_copy(
                src_ref=slots.at[slot],
                dst_ref=moved.at[s, slot % shared],
                send_sem=sent.at[slot],
                recv_sem=landed.at[s, slot % shared],
                device_id=(slot // shared, h),
                device_id_type=MESH,
            )

        def start(slot):
            @pl.when(slot // shared != s)
            def _():
                copy(slot).start()

            @pl.when(slot // shared == s)
            def _():
                own = moved.at[s, slot % shared]
                pltpu.make_async_copy(slots.at[slot], own, landed.at[s, slot % shared]).start()

        def row(distance):
            @pl.loop(0, 2)
            def _(side):
                place = z + (2 * side - 1) * distance

                @pl.when((place >= 0) & (place < head_outer))
                def _():
                    for owner in range(head_inner):
                        start(place * head_inner + owner)

        def finish():
            @pl.loop(0, head)
            def _(slot):
                @pl.when(slot // shared != s)
                def _():
                    copy(slot).wait_send()

        return start, row, finish

    move_tok, move_tok_row, finish_tok = moves(tok, moved_tok, tok_moved, tok_landed)
    move_cot, move_cot_row, finish_cot = moves(cot, moved_cot, cot_moved, cot_landed)

    def project(slot):
        block = tok[slot]
        span = pl.ds(pl.multiple_of(slot * wide, wide), wide)
        for number, weight in enumerate((wq, wk, wv)):
            acc[number] += mul(block, weight[span, :])

        @pl.when((abs(slot // head_inner - z) < head_outer - 1))
        def _():
            move_tok(slot)

    def pull(slot):
        span = pl.ds(pl.multiple_of(slot * wide, wide), wide)
        grad_normed[...] += mul(cot[slot], wo[:, span], NT)

        @pl.when((abs(slot // head_inner - z) < head_outer - 1))
        def _():
            move_cot(slot)

    def each_row(distance, act):
        @pl.loop(0, 2)
        def _(side):
            place = z + (2 * side - 1) * distance
            pl.when((place >= 0) & (place < head_outer) & ((distance > 0) | (side == 0)))(lambda: act(place))

    tok_gather = Gather(tokens_in, tok, tok_recv, tok_outer, tok_inner, outer, inner, gather_parts(rows), project)
    cot_gather = Gather(cot_in, cot, cot_recv, cot_outer, cot_inner, outer, inner, gather_parts(rows), pull)
    nothing = lambda slot: None
    grads_gather = Gather(
        grads.at[s], grads, grads_recv, grads_outer, grads_inner, chip, core, ((0, 0, rows),), nothing
    )
    normed_gather = Gather(
        normed.at[s], normed, normed_recv, normed_outer, normed_inner, chip, core, ((0, 0, rows),), nothing
    )

    tok_gather.own(inner, (1,))
    tok_gather.own(outer)
    tok_gather.own(inner, (0,))
    acc[...] = jnp.zeros_like(acc)
    grad_normed[...] = jnp.zeros_like(grad_normed)
    for load in loads[:4]:
        load.wait()
    project(h)
    tok_gather.cross_row()

    @pl.loop(1, head_outer)
    def _(distance):
        tok_gather.from_outer(distance)

        @pl.when(distance == head_outer - 2)
        def _():
            cot_gather.own(outer)
            cot_gather.own(inner, (1,))

        tok_gather.from_inner(distance - 1)

    cot_gather.own(inner, (0,))
    cot_gather.cross_row()
    tok_gather.from_inner(head_outer - 1)

    for number, target in enumerate((query, keys, values)):
        target[...] = acc[number].astype(HALF)

    def part(ref, number):
        return ref[:, number * DH : (number + 1) * DH]

    for number in range(heads_here):
        fore[s, number] = mul(part(keys, number), part(values, number), TN).astype(HALF)

    def share(states, sems, wanted):
        def copy(other):
            return pltpu.make_async_remote_copy(
                src_ref=states.at[s],
                dst_ref=states.at[s],
                send_sem=sems.at[0, other],
                recv_sem=sems.at[1, s],
                device_id=(other, h),
                device_id_type=MESH,
            )

        def start():
            for other in range(seq):
                pl.when((other != s) & wanted(s, other))(lambda: copy(other).start())

        def arrive():
            for other in range(seq):

                @pl.when((other != s) & wanted(other, s))
                def _():
                    pltpu.make_async_copy(states.at[other], states.at[other], sems.at[1, other]).wait()

        def finish():
            for other in range(seq):
                pl.when((other != s) & wanted(s, other))(lambda: copy(other).wait_send())

        return start, arrive, finish

    start_fore, arrive_fore, finish_fore = share(fore, fore_sem, lambda source, target: source < target)
    start_rear, arrive_rear, finish_rear = share(rear, rear_sem, lambda source, target: target >= 0)
    start_fore()
    for load in loads[4:]:
        load.wait()
    move_tok_row(head_outer - 1)
    pull(h)
    cot_gather.from_outer(1)

    below = lax.broadcasted_iota(jnp.int32, (rows, rows), 1) <= lax.broadcasted_iota(jnp.int32, (rows, rows), 0)
    above = lax.broadcasted_iota(jnp.int32, (rows, rows), 1) >= lax.broadcasted_iota(jnp.int32, (rows, rows), 0)
    for number in range(heads_here):
        query_h, keys_h = part(query, number), part(keys, number)
        scores = jnp.where(below, mul(query_h, keys_h, NT), 0.0).astype(HALF)
        scores_t[number] = jnp.where(above, mul(keys_h, query_h, NT), 0.0).astype(HALF)
        mixed[:, number * DH : (number + 1) * DH] = mul(scores, part(values, number))
    arrive_fore()
    for number in range(heads_here):
        before = state[number]
        for other in range(seq):
            before = before + jnp.where(other < s, fore[other, number].astype(WIDE), 0.0)
        prior[number] = before.astype(HALF)
        whole = part(mixed, number) + mul(part(query, number), prior[number])
        mixed[:, number * DH : (number + 1) * DH] = whole
        inv_norm = lax.rsqrt(jnp.mean(whole * whole, axis=-1, keepdims=True) + EPSILON)
        normed[s, :, number * DH : (number + 1) * DH] = (whole * inv_norm).astype(HALF)
    normed_gather.own(chip)
    normed_gather.own(core)

    @pl.loop(0, head)
    def _(slot):
        span = pl.ds(pl.multiple_of(slot * wide, wide), wide)
        terms[slot // head_inner, slot % head_inner] = mul(normed[s], wo[:, span]).astype(HALF)

    result_sums = Scatter(terms, terms_landed, terms_sem, outer, inner, result_parts(rows))
    result_sums.outer_first(head_outer - 1)
    cot_gather.from_inner(0)
    for distance in range(2, head_outer):
        cot_gather.from_outer(distance)
        if distance < head_outer - 1:
            cot_gather.from_inner(distance - 1)
            result_sums.outer_first(head_outer - distance)

    @pl.loop(0, head_outer)
    def _(turn):
        each_row(head_outer - 1 - turn, result_sums.start_row)

    cot_gather.from_inner(head_outer - 2)
    cot_gather.from_inner(head_outer - 1)

    for number in range(heads_here):
        whole, pulled = part(mixed, number), part(grad_normed, number)
        inv_norm = lax.rsqrt(jnp.mean(whole * whole, axis=-1, keepdims=True) + EPSILON)
        slope = jnp.mean(pulled * whole, axis=-1, keepdims=True)
        grad_mixed = (inv_norm * (pulled - whole * inv_norm * inv_norm * slope)).astype(HALF)
        grads[s, :, number * DH : (number + 1) * DH] = grad_mixed
        rear[s, number] = mul(part(query, number), grad_mixed, TN).astype(HALF)
    start_rear()
    move_cot_row(head_outer - 1)
    result_sums.outer_second(head_outer - 1)
    tok_gather.finish()
    finish_tok()
    finish_fore()
    for number in range(heads_here):
        span = slice(number * DH, (number + 1) * DH)
        grad_mixed = grads[s, :, span]
        query_h, keys_h, values_h = part(query, number), part(keys, number), part(values, number)
        grad_scores = jnp.where(below, mul(grad_mixed, values_h, NT), 0.0).astype(HALF)
        grad_scores_t = jnp.where(above, mul(values_h, grad_mixed, NT), 0.0).astype(HALF)
        acc[0, :, span] = mul(grad_scores, keys_h) + mul(grad_mixed, prior[number], NT)
        acc[1, :, span] = mul(grad_scores_t, query_h)
        acc[2, :, span] = mul(scores_t[number], grad_mixed)
    arrive_rear()
    for number in range(heads_here):
        later = jnp.zeros((DH, DH), WIDE)
        every = jnp.zeros((DH, DH), WIDE)
        for other in range(seq):
            one = rear[other, number].astype(WIDE)
            later = later + jnp.where(other > s, one, 0.0)
            every = every + one
        grad_state[number] = every
        later = later.astype(HALF)
        span = slice(number * DH, (number + 1) * DH)
        acc[1, :, span] += mul(part(values, number), later, NT)
        acc[2, :, span] += mul(part(keys, number), later)
    for number in range(3):
        grads[s, :, number * columns : (number + 1) * columns] = acc[number].astype(HALF)

    input_sums = Scatter(inputs, inputs_landed, inputs_sem, outer, inner, input_parts(rows))

    def input_terms(place):
        @pl.loop(0, head_inner)
        def _(turn):
            owner = (y + 1 + turn) % head_inner
            span = pl.ds(pl.multiple_of((place * head_inner + owner) * wide, wide), wide)
            term = mul(grads[s, :, :columns], wq[span, :], NT)
            term += mul(grads[s, :, columns : 2 * columns], wk[span, :], NT)
            term += mul(grads[s, :, 2 * columns :], wv[span, :], NT)
            inputs[place, owner] = term.astype(HALF)

            @pl.when(turn == head_inner - 2)
            def _():
                input_sums.start_row(place)

    each_row(head_outer - 1, input_terms)
    input_sums.outer_first(head_outer - 1)
    grads_gather.own(chip)
    grads_gather.own(core)

    @pl.loop(1, head_outer)
    def _(turn):
        each_row(head_outer - 1 - turn, input_terms)

    def weight_grads(place):
        for number in range(shared):
            piece, block = moved_tok.at[place, number], moved_cot.at[place, number]
            span = slice(number * wide, (number + 1) * wide)
            pltpu.make_async_copy(piece, piece, tok_landed.at[place, number]).wait()
            pltpu.make_async_copy(block, block, cot_landed.at[place, number]).wait()
            for target, start in ((grad_wq, 0), (grad_wk, columns), (grad_wv, 2 * columns)):
                target[span, :] += mul(piece[...], grads[place, :, start : start + columns], TN)
            grad_wo[:, span] += mul(normed[place], block[...], TN)

    for target in (grad_wq, grad_wk, grad_wv, grad_wo):
        target[...] = jnp.zeros_like(target)
    result_sums.outer_first(1)
    input_sums.outer_second(head_outer - 1)
    normed_gather.from_outer(1)
    normed_gather.from_inner(0)
    for distance in range(2, seq_outer):
        normed_gather.from_outer(distance)
        normed_gather.from_inner(distance - 1)
    normed_gather.from_inner(seq_outer - 1)
    for distance in range(head_outer - 2, 0, -1):
        result_sums.outer_second(distance)
        input_sums.outer_first(distance)
        input_sums.outer_second(distance)
        if distance == head_outer - 2:
            grads_gather.from_outer(1)
            grads_gather.from_inner(0)
    for distance in range(2, seq_outer):
        grads_gather.from_outer(distance)
        grads_gather.from_inner(distance - 1)
    result_sums.turn()
    input_sums.turn()
    weight_grads(s)
    grads_gather.from_inner(seq_outer - 1)

    @pl.loop(1, seq)
    def _(other):
        weight_grads((s + other) % seq)

    cot_gather.finish()
    finish_cot()
    finish_rear()
    normed_gather.finish()
    result_sums.total(total)
    result[...] = total[...].astype(HALF)
    input_sums.total(grad_tokens)
    for one in (grads_gather, result_sums, input_sums):
        one.finish()


def write_out(*refs):
    count = (len(refs) - 1) // 2
    copies = [pltpu.make_async_copy(refs[k], refs[count + k], refs[-1].at[k]) for k in range(count)]
    for copy in copies:
        copy.start()
    for copy in copies:
        copy.wait()


def solution(mesh):
    seq, head = mesh.shape["seq"], mesh.shape["head"]

    def on_device(tokens, w_query, w_key, w_value, w_out, grad_out, state_in):
        rows, wide = tokens.shape
        depth, columns = w_query.shape
        heads_here = columns // DH
        shared = head // seq
        assert rows == BLOCK and head % seq == 0
        head_inner, seq_inner = inner_size(head), inner_size(seq)
        head_outer, seq_outer = head // head_inner, seq // seq_inner
        vmem = lambda *shape: pltpu.VMEM(shape, HALF)
        full = lambda *shape: pltpu.VMEM(shape, WIDE)
        dma = lambda *shape: pltpu.SemaphoreType.DMA(shape)
        pieces = len(gather_parts(rows))
        gathers = lambda: [
            dma(pieces, head), dma(pieces, head, 2), dma(pieces, head, 2), dma(head), dma(seq, shared)
        ]
        spans = lambda: [dma(1, seq), dma(1, seq, 2), dma(1, seq, 2)]
        outs = [
            ((rows, wide), HALF), ((rows, wide), WIDE),
            ((shared * wide, columns), WIDE), ((shared * wide, columns), WIDE), ((shared * wide, columns), WIDE),
            ((columns, shared * wide), WIDE), ((heads_here, DH, DH), WIDE),
        ]
        done = pl.pallas_call(
            lambda *refs: layer((seq, head), *refs),
            out_shape=[pltpu.VMEM(shape, kind) for shape, kind in outs],
            in_specs=[pl.BlockSpec(memory_space=pltpu.HBM)] * 7,
            out_specs=[pl.BlockSpec(memory_space=pltpu.VMEM)] * 7,
            scratch_shapes=[
                vmem(head, rows, wide), vmem(head, rows, wide),
                vmem(seq, shared, rows, wide), vmem(seq, shared, rows, wide),
                vmem(depth, columns), vmem(depth, columns), vmem(depth, columns), vmem(columns, depth),
                full(heads_here, DH, DH),
                full(3, rows, columns), full(rows, columns), full(rows, columns),
                vmem(rows, columns), vmem(rows, columns), vmem(rows, columns),
                vmem(heads_here, rows, rows), vmem(heads_here, DH, DH),
                vmem(seq, heads_here, DH, DH), vmem(seq, heads_here, DH, DH),
                vmem(seq, rows, 3 * columns), vmem(seq, rows, columns),
                vmem(head_outer, head_inner, rows, wide), vmem(2, 2, head_outer, head_inner, rows, wide),
                vmem(head_outer, head_inner, rows, wide), vmem(2, 2, head_outer, head_inner, rows, wide),
                full(rows, wide),
                dma(7), dma(2, seq), dma(2, seq),
                *gathers(), *gathers(), *spans(), *spans(),
                dma(len(result_parts(rows)), 2, 2, 2, head_outer, head_inner),
                dma(len(input_parts(rows)), 2, 2, 2, head_outer, head_inner),
            ],
            compiler_params=pltpu.CompilerParams(
                collective_id=0, has_side_effects=True, vmem_limit_bytes=54 * 1024 * 1024
            ),
        )(tokens, w_query, w_key, w_value, w_out, grad_out, state_in)
        return pl.pallas_call(
            write_out,
            out_shape=[jax.ShapeDtypeStruct(shape, kind) for shape, kind in outs],
            in_specs=[pl.BlockSpec(memory_space=pl.ANY)] * 7,
            out_specs=[pl.BlockSpec(memory_space=pltpu.HBM)] * 7,
            scratch_shapes=[dma(7)],
            compiler_params=pltpu.CompilerParams(vmem_limit_bytes=1024 * 1024),
        )(*done)

    by_head = P(None, "head")
    tiled = P("seq", "head")
    return jax.shard_map(
        on_device,
        mesh=mesh,
        in_specs=(tiled, by_head, by_head, by_head, P("head", None), tiled, P("head", None, None)),
        out_specs=(tiled, tiled, tiled, tiled, tiled, P("head", "seq"), P("head", None, None)),
        check_vma=False,
    )
```

```python
import jax
import jax.numpy as jnp
from jax import lax
from jax.experimental import pallas as pl
from jax.experimental.pallas import tpu as pltpu
from jax.sharding import PartitionSpec as P

DH = 128
BLOCK = 256
EPSILON = 1e-06
WIDE = jnp.float32
HALF = jnp.bfloat16
MESH = pl.DeviceIdType.MESH
NN = (((1,), (0,)), ((), ()))
NT = (((1,), (1,)), ((), ()))
TN = (((0,), (0,)), ((), ()))


def mul(left, right, dims=NN):
    return lax.dot_general(left, right, dims, preferred_element_type=WIDE)


def parts(rows, shares):
    unit, start, cut = rows // 16, 0, []
    for order, share in shares:
        cut.append((order, start, share * unit))
        start += share * unit
    return cut


def gather_parts(rows):
    return parts(rows, ((0, 7), (0, 6), (1, 3)))


def result_parts(rows):
    return parts(rows, ((1, 10), (0, 6)))


def input_parts(rows):
    return parts(rows, ((0, 7), (0, 7), (1, 2)))


def inner_size(count):
    inner = 1
    while 4 * inner * inner <= count:
        inner *= 2
    return inner


class Line:
    def __init__(self, place, size, device):
        self.place, self.size, self.device = place, size, device

    def has(self, way):
        return self.place < self.size - 1 if way == 0 else self.place > 0

    def next(self, way):
        return self.device(self.place + (1 if way == 0 else -1))


class Gather:
    def __init__(self, source, slots, recv, sent_outer, sent_inner, outer, inner, parts, seen):
        self.source, self.slots, self.recv = source, slots, recv
        self.sent_outer, self.sent_inner = sent_outer, sent_inner
        self.outer, self.inner, self.seen = outer, inner, seen
        self.parts = [(number, *part) for number, part in enumerate(parts)]

    def slot(self, place_outer, place_inner):
        return place_outer * self.inner.size + place_inner

    def copy(self, part, slot, line, way, source=None):
        number, _, start, rows = part
        sent = self.sent_outer if line is self.outer else self.sent_inner
        piece = self.slots.at[slot, pl.ds(start, rows)]
        return pltpu.make_async_remote_copy(
            src_ref=piece if source is None else source.at[pl.ds(start, rows)],
            dst_ref=piece,
            send_sem=sent.at[number, slot, way],
            recv_sem=self.recv.at[number, slot],
            device_id=line.next(way),
            device_id_type=MESH,
        )

    def send(self, part, slot, line, way, also=True, source=None):
        @pl.when(line.has(way) & also)
        def _():
            self.copy(part, slot, line, way, source).start()

    def arrive(self, part, slot):
        number, _, start, rows = part
        piece = self.slots.at[slot, pl.ds(start, rows)]
        pltpu.make_async_copy(piece, piece, self.recv.at[number, slot]).wait()

    def own(self, line, orders=(0, 1)):
        slot = self.slot(self.outer.place, self.inner.place)
        for part in self.parts:
            if part[1] in orders:
                for way in (0, 1):
                    self.send(part, slot, line, way, source=self.source)

    def cross_row(self):
        for part in self.parts:
            if part[1] == 1:
                for way in (0, 1):
                    for step in range(1, self.inner.size):
                        place = self.inner.place + (-step if way == 0 else step)

                        @pl.when((place >= 0) & (place < self.inner.size))
                        def _():
                            slot = self.slot(self.outer.place, place)
                            self.arrive(part, slot)
                            self.send(part, slot, self.inner, way)
                            self.send(part, slot, self.outer, 0)
                            self.send(part, slot, self.outer, 1)

    def each_side(self, distance, act):
        @pl.loop(0, 2)
        def _(side):
            row = self.outer.place + (2 * side - 1) * distance

            @pl.when((row >= 0) & (row < self.outer.size) & ((distance > 0) | (side == 0)))
            def _():
                act(side, row)

    def from_outer(self, distance):
        steps = [(part, 0) for part in self.parts]
        steps += [(part, turn) for turn in range(1, self.inner.size) for part in self.parts if part[1] == 1]
        for part, turn in steps:

            def pass_on(side, row):
                slot = self.slot(row, (self.inner.place + turn) % self.inner.size)
                self.arrive(part, slot)
                self.send(part, slot, self.outer, 0, side == 0)
                self.send(part, slot, self.outer, 1, side == 1)
                if part[1] == 0:
                    self.send(part, slot, self.inner, 0)
                    self.send(part, slot, self.inner, 1)

            self.each_side(distance, pass_on)
        self.each_side(distance, lambda side, row: self.seen(self.slot(row, self.inner.place)))

    def from_inner(self, distance):
        def each_place(side, row):
            @pl.loop(0, 2)
            def _(way):
                @pl.loop(1, self.inner.size)
                def _(step):
                    place = self.inner.place + (2 * way - 1) * step

                    @pl.when((place >= 0) & (place < self.inner.size))
                    def _():
                        slot = self.slot(row, place)
                        for part in self.parts:
                            if part[1] == 0:
                                self.arrive(part, slot)
                                self.send(part, slot, self.inner, 0, way == 0)
                                self.send(part, slot, self.inner, 1, way == 1)
                        self.seen(slot)

        self.each_side(distance, each_place)

    def finish(self):
        @pl.loop(0, self.outer.size)
        def _(row):
            @pl.loop(0, self.inner.size)
            def _(place):
                slot = self.slot(row, place)
                for part in self.parts:
                    for way in (0, 1):
                        passed = (row <= self.outer.place) if way == 0 else (row >= self.outer.place)
                        if part[1] == 0:
                            passed &= place == self.inner.place

                        @pl.when(self.outer.has(way) & passed)
                        def _():
                            self.copy(part, slot, self.outer, way).wait_send()

                        passed = (place <= self.inner.place) if way == 0 else (place >= self.inner.place)
                        if part[1] == 1:
                            passed &= row == self.outer.place

                        @pl.when(self.inner.has(way) & passed)
                        def _():
                            self.copy(part, slot, self.inner, way).wait_send()


class Reduce:
    def __init__(self, line, term, landed, sems):
        self.line, self.term, self.landed, self.sems = line, term, landed, sems

    def copy(self, way, owner):
        return pltpu.make_async_remote_copy(
            src_ref=self.term(owner),
            dst_ref=self.landed(way, owner),
            send_sem=self.sems(0, way, owner),
            recv_sem=self.sems(1, way, owner),
            device_id=self.line.next(way),
            device_id_type=MESH,
        )

    def arrive(self, way, owner, act):
        @pl.when(self.line.has(1 - way))
        def _():
            piece = self.landed(way, owner)
            pltpu.make_async_copy(piece, piece, self.sems(1, way, owner)).wait()
            act(piece[...].astype(WIDE))

    def add(self, way, owner):
        term = self.term(owner)

        def act(value):
            term[...] = (term[...].astype(WIDE) + value).astype(HALF)

        self.arrive(way, owner, act)

    def each(self, distance, act):
        for way in (0, 1):
            owner = self.line.place + (distance if way == 0 else -distance)
            pl.when((owner >= 0) & (owner < self.line.size))(lambda: act(way, owner))

    def step(self, distance):
        def act(way, owner):
            self.add(way, owner)
            self.copy(way, owner).start()

        self.each(distance, act)

    def finish(self):
        for distance in range(1, self.line.size):
            self.each(distance, lambda way, owner: self.copy(way, owner).wait_send())


class Scatter:
    def __init__(self, terms, landed, sems, outer, inner, parts):
        self.terms, self.landed, self.sems = terms, landed, sems
        self.outer, self.inner = outer, inner
        self.parts = [(number, *part) for number, part in enumerate(parts)]

    def along_outer(self, part, place):
        number, _, start, rows = part
        span = pl.ds(start, rows)
        return Reduce(
            self.outer,
            lambda owner: self.terms.at[owner, place, span],
            lambda way, owner: self.landed.at[0, way, owner, place, span],
            lambda end, way, owner: self.sems.at[number, 0, end, way, owner, place],
        )

    def along_inner(self, part, row):
        number, _, start, rows = part
        span = pl.ds(start, rows)
        return Reduce(
            self.inner,
            lambda owner: self.terms.at[row, owner, span],
            lambda way, owner: self.landed.at[1, way, row, owner, span],
            lambda end, way, owner: self.sems.at[number, 1, end, way, row, owner],
        )

    def steps_inner(self, part, row):
        line = self.along_inner(part, row)
        for distance in range(self.inner.size - 1, 0, -1):
            line.step(distance)

    def start_row(self, row):
        for part in self.parts:
            if part[1] == 0:
                self.steps_inner(part, row)

    def outer_first(self, distance):
        for part in self.parts:
            if part[1] == 1:
                for place in range(self.inner.size):
                    self.along_outer(part, place).step(distance)

    def outer_second(self, distance):
        for part in self.parts:
            if part[1] == 0:

                def act(way, row):
                    for side in (0, 1):
                        self.along_inner(part, row).add(side, self.inner.place)

                self.along_outer(part, self.inner.place).each(distance, act)
                self.along_outer(part, self.inner.place).step(distance)

    def turn(self):
        for part in self.parts:
            if part[1] == 1:
                for place in range(self.inner.size):

                    @pl.when(place != self.inner.place)
                    def _():
                        for way in (0, 1):
                            self.along_outer(part, place).add(way, self.outer.place)

                self.steps_inner(part, self.outer.place)

    def total(self, out):
        row, place = self.outer.place, self.inner.place
        for part in self.parts:
            span = pl.ds(part[2], part[3])
            held = [self.terms[row, place, span].astype(WIDE)]
            out[span, :] = held[0].astype(out.dtype)

            def act(value):
                out[span, :] = (out[span, :].astype(WIDE) + value).astype(out.dtype)

            for way in (0, 1):
                self.along_outer(part, place).arrive(way, row, act)
                self.along_inner(part, row).arrive(way, place, act)

    def finish(self):
        for part in self.parts:
            if part[1] == 0:
                pl.loop(0, self.outer.size)(lambda row: self.along_inner(part, row).finish())
                self.along_outer(part, self.inner.place).finish()
            else:
                pl.loop(0, self.inner.size)(lambda place: self.along_outer(part, place).finish())
                self.along_inner(part, self.outer.place).finish()


def layer(
    sizes,
    tokens_in, wq_in, wk_in, wv_in, wo_in, cot_in, state_in,
    result, grad_tokens, grad_wq, grad_wk, grad_wv, grad_wo, grad_state,
    tok, cot, moved_tok, wq, wk, wv, wo, state,
    acc, grad_normed, mixed, query, keys, values, scores_t, prior,
    fore, rear, grads, normed,
    terms, terms_landed, inputs, inputs_landed, outers, outers_landed, total, total_wo,
    load_sem, fore_sem, rear_sem,
    tok_recv, tok_outer, tok_inner, tok_moved, tok_landed,
    cot_recv, cot_outer, cot_inner,
    grads_recv, grads_outer, grads_inner,
    terms_sem, inputs_sem, outers_sem,
):
    seq, head = sizes
    head_inner, seq_inner = inner_size(head), inner_size(seq)
    head_outer, seq_outer = head // head_inner, seq // seq_inner
    shared = head // seq
    rows, wide = tok.shape[1:]
    columns = wq.shape[1]
    heads_here = columns // DH
    s, h = lax.axis_index("seq"), lax.axis_index("head")
    z, y = h // head_inner, h % head_inner
    outer = Line(z, head_outer, lambda place: (s, place * head_inner + y))
    inner = Line(y, head_inner, lambda place: (s, z * head_inner + place))
    chip = Line(s // seq_inner, seq_outer, lambda place: (place * seq_inner + s % seq_inner, h))
    core = Line(s % seq_inner, seq_inner, lambda place: (s // seq_inner * seq_inner + place, h))

    loads = [
        pltpu.make_async_copy(source, target, load_sem.at[number])
        for number, (source, target) in enumerate(
            [
                (tokens_in, tok.at[h]),
                (wq_in, wq), (wk_in, wk), (wv_in, wv),
                (cot_in, cot.at[h]), (wo_in, wo), (state_in, state),
            ]
        )
    ]
    for load in loads:
        load.start()

    barrier = pltpu.get_barrier_semaphore()
    expected = seq - 1
    for line in (outer, inner):
        for way in (0, 1):
            expected = expected + line.has(way).astype(jnp.int32)

            @pl.when(line.has(way))
            def _():
                pl.semaphore_signal(barrier, inc=1, device_id=line.next(way), device_id_type=MESH)
    for other in range(1, seq):
        pl.semaphore_signal(barrier, inc=1, device_id=((s + other) % seq, h), device_id_type=MESH)
    pl.semaphore_wait(barrier, expected)

    def early(slot):
        distance = abs(slot // head_inner - z)
        at_end = (z == 0) | (z == head_outer - 1)
        direct = (slot % head_inner == y) & at_end
        return (distance < head_outer - 2) | ((distance == head_outer - 2) & direct)

    def moves(slots, moved, sent, landed):
        def copy(slot):
            return pltpu.make_async_remote_copy(
                src_ref=slots.at[slot],
                dst_ref=moved.at[s, slot % shared],
                send_sem=sent.at[slot],
                recv_sem=landed.at[s, slot % shared],
                device_id=(slot // shared, h),
                device_id_type=MESH,
            )

        def start(slot):
            @pl.when(slot // shared != s)
            def _():
                copy(slot).start()

            @pl.when(slot // shared == s)
            def _():
                own = moved.at[s, slot % shared]
                pltpu.make_async_copy(slots.at[slot], own, landed.at[s, slot % shared]).start()

        def soon(slot):
            pl.when(early(slot))(lambda: start(slot))

        def late():
            @pl.loop(0, head)
            def _(slot):
                pl.when(jnp.logical_not(early(slot)))(lambda: start(slot))

        def finish():
            @pl.loop(0, head)
            def _(slot):
                @pl.when(slot // shared != s)
                def _():
                    copy(slot).wait_send()

        return soon, late, finish

    move_tok, move_tok_late, finish_tok = moves(tok, moved_tok, tok_moved, tok_landed)

    def project(slot):
        block = tok[slot]
        span = pl.ds(pl.multiple_of(slot * wide, wide), wide)
        for number, weight in enumerate((wq, wk, wv)):
            acc[number] += mul(block, weight[span, :])
        move_tok(slot)

    def pull(slot):
        span = pl.ds(pl.multiple_of(slot * wide, wide), wide)
        grad_normed[...] += mul(cot[slot], wo[:, span], NT)

    def each_row(distance, act):
        @pl.loop(0, 2)
        def _(side):
            place = z + (2 * side - 1) * distance
            pl.when((place >= 0) & (place < head_outer) & ((distance > 0) | (side == 0)))(lambda: act(place))

    tok_gather = Gather(tokens_in, tok, tok_recv, tok_outer, tok_inner, outer, inner, gather_parts(rows), project)
    cot_gather = Gather(cot_in, cot, cot_recv, cot_outer, cot_inner, outer, inner, gather_parts(rows), pull)
    nothing = lambda slot: None
    grads_gather = Gather(
        grads.at[s], grads, grads_recv, grads_outer, grads_inner, chip, core, ((0, 0, rows),), nothing
    )

    tok_gather.own(inner, (1,))
    tok_gather.own(outer)
    tok_gather.own(inner, (0,))
    acc[...] = jnp.zeros_like(acc)
    grad_normed[...] = jnp.zeros_like(grad_normed)
    for load in loads[:4]:
        load.wait()
    project(h)
    tok_gather.cross_row()

    @pl.loop(1, head_outer)
    def _(distance):
        tok_gather.from_outer(distance)

        @pl.when(distance == head_outer - 2)
        def _():
            cot_gather.own(outer)
            cot_gather.own(inner, (1,))

        tok_gather.from_inner(distance - 1)

    cot_gather.own(inner, (0,))
    cot_gather.cross_row()
    tok_gather.from_inner(head_outer - 1)

    for number, target in enumerate((query, keys, values)):
        target[...] = acc[number].astype(HALF)

    def part(ref, number):
        return ref[:, number * DH : (number + 1) * DH]

    for number in range(heads_here):
        fore[s, number] = mul(part(keys, number), part(values, number), TN).astype(HALF)

    def share(states, sems, wanted):
        def copy(other):
            return pltpu.make_async_remote_copy(
                src_ref=states.at[s],
                dst_ref=states.at[s],
                send_sem=sems.at[0, other],
                recv_sem=sems.at[1, s],
                device_id=(other, h),
                device_id_type=MESH,
            )

        def start():
            for other in range(seq):
                pl.when((other != s) & wanted(s, other))(lambda: copy(other).start())

        def arrive():
            for other in range(seq):

                @pl.when((other != s) & wanted(other, s))
                def _():
                    pltpu.make_async_copy(states.at[other], states.at[other], sems.at[1, other]).wait()

        def finish():
            for other in range(seq):
                pl.when((other != s) & wanted(s, other))(lambda: copy(other).wait_send())

        return start, arrive, finish

    start_fore, arrive_fore, finish_fore = share(fore, fore_sem, lambda source, target: source < target)
    start_rear, arrive_rear, finish_rear = share(rear, rear_sem, lambda source, target: target >= 0)
    start_fore()
    for load in loads[4:]:
        load.wait()
    move_tok_late()
    pull(h)
    cot_gather.from_outer(1)

    below = lax.broadcasted_iota(jnp.int32, (rows, rows), 1) <= lax.broadcasted_iota(jnp.int32, (rows, rows), 0)
    above = lax.broadcasted_iota(jnp.int32, (rows, rows), 1) >= lax.broadcasted_iota(jnp.int32, (rows, rows), 0)
    for number in range(heads_here):
        query_h, keys_h = part(query, number), part(keys, number)
        scores = jnp.where(below, mul(query_h, keys_h, NT), 0.0).astype(HALF)
        scores_t[number] = jnp.where(above, mul(keys_h, query_h, NT), 0.0).astype(HALF)
        mixed[:, number * DH : (number + 1) * DH] = mul(scores, part(values, number))
    arrive_fore()
    for number in range(heads_here):
        before = state[number]
        for other in range(seq):
            before = before + jnp.where(other < s, fore[other, number].astype(WIDE), 0.0)
        prior[number] = before.astype(HALF)
        whole = part(mixed, number) + mul(part(query, number), prior[number])
        mixed[:, number * DH : (number + 1) * DH] = whole
        inv_norm = lax.rsqrt(jnp.mean(whole * whole, axis=-1, keepdims=True) + EPSILON)
        normed[:, number * DH : (number + 1) * DH] = (whole * inv_norm).astype(HALF)

    @pl.loop(0, head)
    def _(slot):
        span = pl.ds(pl.multiple_of(slot * wide, wide), wide)
        terms[slot // head_inner, slot % head_inner] = mul(normed[...], wo[:, span]).astype(HALF)

    result_sums = Scatter(terms, terms_landed, terms_sem, outer, inner, result_parts(rows))
    result_sums.outer_first(head_outer - 1)
    cot_gather.from_inner(0)
    for distance in range(2, head_outer):
        cot_gather.from_outer(distance)
        if distance < head_outer - 1:
            cot_gather.from_inner(distance - 1)
            result_sums.outer_first(head_outer - distance)

    @pl.loop(0, head_outer)
    def _(turn):
        each_row(head_outer - 1 - turn, result_sums.start_row)

    cot_gather.from_inner(head_outer - 2)
    cot_gather.from_inner(head_outer - 1)

    for number in range(heads_here):
        whole, pulled = part(mixed, number), part(grad_normed, number)
        inv_norm = lax.rsqrt(jnp.mean(whole * whole, axis=-1, keepdims=True) + EPSILON)
        slope = jnp.mean(pulled * whole, axis=-1, keepdims=True)
        grad_mixed = (inv_norm * (pulled - whole * inv_norm * inv_norm * slope)).astype(HALF)
        grads[s, :, number * DH : (number + 1) * DH] = grad_mixed
        rear[s, number] = mul(part(query, number), grad_mixed, TN).astype(HALF)
    start_rear()

    outer_grads = Scatter(outers, outers_landed, outers_sem, chip, core, ((0, 0, shared * columns),))

    @pl.loop(0, head)
    def _(slot):
        owner = slot // shared
        span = pl.ds(pl.multiple_of(slot % shared * columns, columns), columns)
        share_wo = mul(normed[...], cot[slot], TN).astype(HALF)
        outers[owner // seq_inner, owner % seq_inner, span] = share_wo

    pl.loop(0, seq_outer)(outer_grads.start_row)
    for number in range(heads_here):
        span = slice(number * DH, (number + 1) * DH)
        grad_mixed = grads[s, :, span]
        query_h, keys_h, values_h = part(query, number), part(keys, number), part(values, number)
        grad_scores = jnp.where(below, mul(grad_mixed, values_h, NT), 0.0).astype(HALF)
        grad_scores_t = jnp.where(above, mul(values_h, grad_mixed, NT), 0.0).astype(HALF)
        acc[0, :, span] = mul(grad_scores, keys_h) + mul(grad_mixed, prior[number], NT)
        acc[1, :, span] = mul(grad_scores_t, query_h)
        acc[2, :, span] = mul(scores_t[number], grad_mixed)
    result_sums.outer_second(head_outer - 1)
    tok_gather.finish()
    finish_tok()
    finish_fore()
    result_sums.outer_first(1)
    arrive_rear()
    for number in range(heads_here):
        later = jnp.zeros((DH, DH), WIDE)
        every = jnp.zeros((DH, DH), WIDE)
        for other in range(seq):
            one = rear[other, number].astype(WIDE)
            later = later + jnp.where(other > s, one, 0.0)
            every = every + one
        grad_state[number] = every
        later = later.astype(HALF)
        span = slice(number * DH, (number + 1) * DH)
        acc[1, :, span] += mul(part(values, number), later, NT)
        acc[2, :, span] += mul(part(keys, number), later)
    for number in range(3):
        grads[s, :, number * columns : (number + 1) * columns] = acc[number].astype(HALF)

    input_sums = Scatter(inputs, inputs_landed, inputs_sem, outer, inner, input_parts(rows))

    def input_terms(place):
        @pl.loop(0, head_inner)
        def _(turn):
            owner = (y + 1 + turn) % head_inner
            span = pl.ds(pl.multiple_of((place * head_inner + owner) * wide, wide), wide)
            term = mul(grads[s, :, :columns], wq[span, :], NT)
            term += mul(grads[s, :, columns : 2 * columns], wk[span, :], NT)
            term += mul(grads[s, :, 2 * columns :], wv[span, :], NT)
            inputs[place, owner] = term.astype(HALF)

            @pl.when(turn == head_inner - 2)
            def _():
                input_sums.start_row(place)

    each_row(head_outer - 1, input_terms)
    input_sums.outer_first(head_outer - 1)
    grads_gather.own(chip)
    grads_gather.own(core)

    @pl.loop(1, head_outer)
    def _(turn):
        each_row(head_outer - 1 - turn, input_terms)

    def weight_grads(place):
        for number in range(shared):
            piece = moved_tok.at[place, number]
            span = slice(number * wide, (number + 1) * wide)
            pltpu.make_async_copy(piece, piece, tok_landed.at[place, number]).wait()
            for target, start in ((grad_wq, 0), (grad_wk, columns), (grad_wv, 2 * columns)):
                target[span, :] += mul(piece[...], grads[place, :, start : start + columns], TN)

    for target in (grad_wq, grad_wk, grad_wv):
        target[...] = jnp.zeros_like(target)
    for distance in range(seq_outer - 1, 0, -1):
        outer_grads.outer_second(distance)
    input_sums.outer_second(head_outer - 1)
    for distance in range(head_outer - 2, 0, -1):
        result_sums.outer_second(distance)
        input_sums.outer_first(distance)
        input_sums.outer_second(distance)
        if distance == head_outer - 2:
            grads_gather.from_outer(1)
            grads_gather.from_inner(0)
    for distance in range(2, seq_outer):
        grads_gather.from_outer(distance)
        grads_gather.from_inner(distance - 1)
    result_sums.turn()
    input_sums.turn()
    weight_grads(s)
    grads_gather.from_inner(seq_outer - 1)

    @pl.loop(1, seq)
    def _(other):
        weight_grads((s + other) % seq)

    outer_grads.total(total_wo)
    for number in range(shared):
        grad_wo[:, number * wide : (number + 1) * wide] = total_wo[number * columns : (number + 1) * columns, :]
    cot_gather.finish()
    finish_rear()
    outer_grads.finish()
    result_sums.total(total)
    result[...] = total[...].astype(HALF)
    input_sums.total(grad_tokens)
    for one in (grads_gather, result_sums, input_sums):
        one.finish()


def write_out(*refs):
    count = (len(refs) - 1) // 2
    copies = [pltpu.make_async_copy(refs[k], refs[count + k], refs[-1].at[k]) for k in range(count)]
    for copy in copies:
        copy.start()
    for copy in copies:
        copy.wait()


def solution(mesh):
    seq, head = mesh.shape["seq"], mesh.shape["head"]

    def on_device(tokens, w_query, w_key, w_value, w_out, grad_out, state_in):
        rows, wide = tokens.shape
        depth, columns = w_query.shape
        heads_here = columns // DH
        shared = head // seq
        assert rows == BLOCK and head % seq == 0
        head_inner, seq_inner = inner_size(head), inner_size(seq)
        head_outer, seq_outer = head // head_inner, seq // seq_inner
        vmem = lambda *shape: pltpu.VMEM(shape, HALF)
        full = lambda *shape: pltpu.VMEM(shape, WIDE)
        dma = lambda *shape: pltpu.SemaphoreType.DMA(shape)
        pieces = len(gather_parts(rows))
        gathers = lambda: [
            dma(pieces, head), dma(pieces, head, 2), dma(pieces, head, 2)
        ]
        spans = lambda: [dma(1, seq), dma(1, seq, 2), dma(1, seq, 2)]
        outs = [
            ((rows, wide), HALF), ((rows, wide), WIDE),
            ((shared * wide, columns), WIDE), ((shared * wide, columns), WIDE), ((shared * wide, columns), WIDE),
            ((columns, shared * wide), WIDE), ((heads_here, DH, DH), WIDE),
        ]
        done = pl.pallas_call(
            lambda *refs: layer((seq, head), *refs),
            out_shape=[pltpu.VMEM(shape, kind) for shape, kind in outs],
            in_specs=[pl.BlockSpec(memory_space=pltpu.HBM)] * 7,
            out_specs=[pl.BlockSpec(memory_space=pltpu.VMEM)] * 7,
            scratch_shapes=[
                vmem(head, rows, wide), vmem(head, rows, wide),
                vmem(seq, shared, rows, wide),
                vmem(depth, columns), vmem(depth, columns), vmem(depth, columns), vmem(columns, depth),
                full(heads_here, DH, DH),
                full(3, rows, columns), full(rows, columns), full(rows, columns),
                vmem(rows, columns), vmem(rows, columns), vmem(rows, columns),
                vmem(heads_here, rows, rows), vmem(heads_here, DH, DH),
                vmem(seq, heads_here, DH, DH), vmem(seq, heads_here, DH, DH),
                vmem(seq, rows, 3 * columns), vmem(rows, columns),
                vmem(head_outer, head_inner, rows, wide), vmem(2, 2, head_outer, head_inner, rows, wide),
                vmem(head_outer, head_inner, rows, wide), vmem(2, 2, head_outer, head_inner, rows, wide),
                vmem(seq_outer, seq_inner, shared * columns, wide),
                vmem(2, 2, seq_outer, seq_inner, shared * columns, wide),
                full(rows, wide), full(shared * columns, wide),
                dma(7), dma(2, seq), dma(2, seq),
                *gathers(), dma(head), dma(seq, shared), *gathers(), *spans(),
                dma(len(result_parts(rows)), 2, 2, 2, head_outer, head_inner),
                dma(len(input_parts(rows)), 2, 2, 2, head_outer, head_inner),
                dma(1, 2, 2, 2, seq_outer, seq_inner),
            ],
            compiler_params=pltpu.CompilerParams(
                collective_id=0, has_side_effects=True, vmem_limit_bytes=54 * 1024 * 1024
            ),
        )(tokens, w_query, w_key, w_value, w_out, grad_out, state_in)
        return pl.pallas_call(
            write_out,
            out_shape=[jax.ShapeDtypeStruct(shape, kind) for shape, kind in outs],
            in_specs=[pl.BlockSpec(memory_space=pl.ANY)] * 7,
            out_specs=[pl.BlockSpec(memory_space=pltpu.HBM)] * 7,
            scratch_shapes=[dma(7)],
            compiler_params=pltpu.CompilerParams(vmem_limit_bytes=1024 * 1024),
        )(*done)

    by_head = P(None, "head")
    tiled = P("seq", "head")
    return jax.shard_map(
        on_device,
        mesh=mesh,
        in_specs=(tiled, by_head, by_head, by_head, P("head", None), tiled, P("head", None, None)),
        out_specs=(tiled, tiled, tiled, tiled, tiled, P("head", "seq"), P("head", None, None)),
        check_vma=False,
    )
```

```python
import jax
import jax.numpy as jnp
from jax import lax
from jax.experimental import pallas as pl
from jax.experimental.pallas import tpu as pltpu
from jax.sharding import PartitionSpec as P

DH = 128
BLOCK = 256
EPSILON = 1e-06
WIDE = jnp.float32
HALF = jnp.bfloat16
MESH = pl.DeviceIdType.MESH
NN = (((1,), (0,)), ((), ()))
NT = (((1,), (1,)), ((), ()))
TN = (((0,), (0,)), ((), ()))


def mul(left, right, dims=NN):
    return lax.dot_general(left, right, dims, preferred_element_type=WIDE)


def parts(rows, shares):
    unit, start, cut = rows // 16, 0, []
    for order, share in shares:
        cut.append((order, start, share * unit))
        start += share * unit
    return cut


def gather_parts(rows):
    return parts(rows, ((0, 7), (0, 6), (1, 3)))


def result_parts(rows):
    return parts(rows, ((1, 9), (0, 7)))


def input_parts(rows):
    return parts(rows, ((0, 8), (0, 8)))


def inner_size(count):
    inner = 1
    while 4 * inner * inner <= count:
        inner *= 2
    return inner


class Line:
    def __init__(self, place, size, device):
        self.place, self.size, self.device = place, size, device

    def has(self, way):
        return self.place < self.size - 1 if way == 0 else self.place > 0

    def next(self, way):
        return self.device(self.place + (1 if way == 0 else -1))


def outer_sems(order, outer, inner):
    return outer + 1 if order == 0 else outer * inner + inner


def inner_sems(order, outer, inner):
    if inner == 2:
        return outer if order == 0 else 1
    return outer * inner + outer if order == 0 else inner + 1


def gather_sems(order, outer, inner):
    return outer * inner + outer_sems(order, outer, inner) + inner_sems(order, outer, inner)


def scatter_sems(order, outer, inner):
    first, second = (inner, outer) if order == 0 else (outer, inner)
    return second * (2 * first + 1) + 2 * second + 1


class Gather:
    def __init__(self, source, slots, sems, outer, inner, parts, seen):
        self.source, self.slots, self.sems = source, slots, sems
        self.outer, self.inner, self.seen = outer, inner, seen
        self.parts, base = [], 0
        for order, start, rows in parts:
            self.parts.append((base, order, start, rows))
            base += gather_sems(order, outer.size, inner.size)

    def slot(self, place_outer, place_inner):
        return place_outer * self.inner.size + place_inner

    def copy(self, part, slot, line, way, source=None):
        base, order, start, rows = part
        row, place = slot // self.inner.size, slot % self.inner.size
        sent = base + self.outer.size * self.inner.size
        if line is self.outer:
            if order == 0:
                twice, once, more = row == line.place, row, line.size
            else:
                twice, once, more = row == line.place, slot, line.size * self.inner.size + place
        else:
            sent += outer_sems(order, self.outer.size, self.inner.size)
            index = row if order == 0 else 0
            if line.size > 2:
                index = slot if order == 0 else place
            more = index if line.size == 2 else (line.size * self.outer.size + row if order == 0 else line.size)
            twice, once = place == line.place, index
        sent += jnp.where(twice, more, once) if way == 1 else once
        piece = self.slots.at[slot, pl.ds(start, rows)]
        return pltpu.make_async_remote_copy(
            src_ref=piece if source is None else source.at[pl.ds(start, rows)],
            dst_ref=piece,
            send_sem=self.sems.at[sent],
            recv_sem=self.sems.at[base + slot],
            device_id=line.next(way),
            device_id_type=MESH,
        )

    def send(self, part, slot, line, way, also=True, source=None):
        @pl.when(line.has(way) & also)
        def _():
            self.copy(part, slot, line, way, source).start()

    def arrive(self, part, slot):
        base, _, start, rows = part
        piece = self.slots.at[slot, pl.ds(start, rows)]
        pltpu.make_async_copy(piece, piece, self.sems.at[base + slot]).wait()

    def own(self, line, orders=(0, 1)):
        slot = self.slot(self.outer.place, self.inner.place)
        for part in self.parts:
            if part[1] in orders:
                for way in (0, 1):
                    self.send(part, slot, line, way, source=self.source)

    def cross_row(self):
        for part in self.parts:
            if part[1] == 1:
                for way in (0, 1):
                    for step in range(1, self.inner.size):
                        place = self.inner.place + (-step if way == 0 else step)

                        @pl.when((place >= 0) & (place < self.inner.size))
                        def _():
                            slot = self.slot(self.outer.place, place)
                            self.arrive(part, slot)
                            self.send(part, slot, self.inner, way)
                            self.send(part, slot, self.outer, 0)
                            self.send(part, slot, self.outer, 1)

    def each_side(self, distance, act):
        @pl.loop(0, 2)
        def _(side):
            row = self.outer.place + (2 * side - 1) * distance

            @pl.when((row >= 0) & (row < self.outer.size) & ((distance > 0) | (side == 0)))
            def _():
                act(side, row)

    def from_outer(self, distance):
        steps = [(part, 0) for part in self.parts]
        steps += [(part, turn) for turn in range(1, self.inner.size) for part in self.parts if part[1] == 1]
        for part, turn in steps:

            def pass_on(side, row):
                slot = self.slot(row, (self.inner.place + turn) % self.inner.size)
                self.arrive(part, slot)
                self.send(part, slot, self.outer, 0, side == 0)
                self.send(part, slot, self.outer, 1, side == 1)
                if part[1] == 0:
                    self.send(part, slot, self.inner, 0)
                    self.send(part, slot, self.inner, 1)

            self.each_side(distance, pass_on)
        self.each_side(distance, lambda side, row: self.seen(self.slot(row, self.inner.place)))

    def from_inner(self, distance):
        def each_place(side, row):
            @pl.loop(0, 2)
            def _(way):
                @pl.loop(1, self.inner.size)
                def _(step):
                    place = self.inner.place + (2 * way - 1) * step

                    @pl.when((place >= 0) & (place < self.inner.size))
                    def _():
                        slot = self.slot(row, place)
                        for part in self.parts:
                            if part[1] == 0:
                                self.arrive(part, slot)
                                self.send(part, slot, self.inner, 0, way == 0)
                                self.send(part, slot, self.inner, 1, way == 1)
                        self.seen(slot)

        self.each_side(distance, each_place)

    def finish(self):
        @pl.loop(0, self.outer.size)
        def _(row):
            @pl.loop(0, self.inner.size)
            def _(place):
                slot = self.slot(row, place)
                for part in self.parts:
                    for way in (0, 1):
                        passed = (row <= self.outer.place) if way == 0 else (row >= self.outer.place)
                        if part[1] == 0:
                            passed &= place == self.inner.place

                        @pl.when(self.outer.has(way) & passed)
                        def _():
                            self.copy(part, slot, self.outer, way).wait_send()

                        passed = (place <= self.inner.place) if way == 0 else (place >= self.inner.place)
                        if part[1] == 1:
                            passed &= row == self.outer.place

                        @pl.when(self.inner.has(way) & passed)
                        def _():
                            self.copy(part, slot, self.inner, way).wait_send()


class Reduce:
    def __init__(self, line, term, landed, sems, base):
        self.line, self.term, self.landed, self.sems, self.base = line, term, landed, sems, base

    def landing(self, way, owner, place):
        index = self.base + self.line.size + owner
        return self.sems.at[index if way == 0 else jnp.where(owner == place, self.base + 2 * self.line.size, index)]

    def copy(self, way, owner):
        return pltpu.make_async_remote_copy(
            src_ref=self.term(owner),
            dst_ref=self.landed(way, owner),
            send_sem=self.sems.at[self.base + owner],
            recv_sem=self.landing(way, owner, self.line.place + (1 if way == 0 else -1)),
            device_id=self.line.next(way),
            device_id_type=MESH,
        )

    def arrive(self, way, owner, act):
        @pl.when(self.line.has(1 - way))
        def _():
            piece = self.landed(way, owner)
            pltpu.make_async_copy(piece, piece, self.landing(way, owner, self.line.place)).wait()
            act(piece[...].astype(WIDE))

    def add(self, way, owner):
        term = self.term(owner)

        def act(value):
            term[...] = (term[...].astype(WIDE) + value).astype(HALF)

        self.arrive(way, owner, act)

    def each(self, distance, act):
        for way in (0, 1):
            owner = self.line.place + (distance if way == 0 else -distance)
            pl.when((owner >= 0) & (owner < self.line.size))(lambda: act(way, owner))

    def step(self, distance):
        def act(way, owner):
            self.add(way, owner)
            self.copy(way, owner).start()

        self.each(distance, act)

    def finish(self):
        for distance in range(1, self.line.size):
            self.each(distance, lambda way, owner: self.copy(way, owner).wait_send())


class Scatter:
    def __init__(self, terms, landed, sems, outer, inner, parts):
        self.terms, self.landed, self.sems = terms, landed, sems
        self.outer, self.inner = outer, inner
        self.parts, base = [], 0
        for order, start, rows in parts:
            self.parts.append((base, order, start, rows))
            base += scatter_sems(order, outer.size, inner.size)

    def along_outer(self, part, place):
        base, order, start, rows = part
        span = pl.ds(start, rows)
        base += self.outer.size * (2 * self.inner.size + 1) if order == 0 else place * (2 * self.outer.size + 1)
        return Reduce(
            self.outer,
            lambda owner: self.terms.at[owner, place, span],
            lambda way, owner: self.landed.at[0, way, owner, place, span],
            self.sems,
            base,
        )

    def along_inner(self, part, row):
        base, order, start, rows = part
        span = pl.ds(start, rows)
        base += self.inner.size * (2 * self.outer.size + 1) if order == 1 else row * (2 * self.inner.size + 1)
        return Reduce(
            self.inner,
            lambda owner: self.terms.at[row, owner, span],
            lambda way, owner: self.landed.at[1, way, row, owner, span],
            self.sems,
            base,
        )

    def steps_inner(self, part, row):
        line = self.along_inner(part, row)
        for distance in range(self.inner.size - 1, 0, -1):
            line.step(distance)

    def start_row(self, row):
        for part in self.parts:
            if part[1] == 0:
                self.steps_inner(part, row)

    def outer_first(self, distance):
        for part in self.parts:
            if part[1] == 1:
                for place in range(self.inner.size):
                    self.along_outer(part, place).step(distance)

    def outer_second(self, distance):
        for part in self.parts:
            if part[1] == 0:

                def act(way, row):
                    for side in (0, 1):
                        self.along_inner(part, row).add(side, self.inner.place)

                self.along_outer(part, self.inner.place).each(distance, act)
                self.along_outer(part, self.inner.place).step(distance)

    def turn(self):
        for part in self.parts:
            if part[1] == 1:
                for place in range(self.inner.size):

                    @pl.when(place != self.inner.place)
                    def _():
                        for way in (0, 1):
                            self.along_outer(part, place).add(way, self.outer.place)

                self.steps_inner(part, self.outer.place)

    def total(self, out):
        row, place = self.outer.place, self.inner.place
        for part in self.parts:
            span = pl.ds(part[2], part[3])
            held = [self.terms[row, place, span].astype(WIDE)]
            out[span, :] = held[0].astype(out.dtype)

            def act(value):
                out[span, :] = (out[span, :].astype(WIDE) + value).astype(out.dtype)

            for way in (0, 1):
                self.along_outer(part, place).arrive(way, row, act)
                self.along_inner(part, row).arrive(way, place, act)

    def finish(self):
        for part in self.parts:
            if part[1] == 0:
                pl.loop(0, self.outer.size)(lambda row: self.along_inner(part, row).finish())
                self.along_outer(part, self.inner.place).finish()
            else:
                pl.loop(0, self.inner.size)(lambda place: self.along_outer(part, place).finish())
                self.along_inner(part, self.outer.place).finish()


def layer(
    sizes,
    tokens_in, wq_in, wk_in, wv_in, wo_in, cot_in, state_in,
    result, grad_tokens, grad_wq, grad_wk, grad_wv, grad_wo, grad_state,
    tok, cot, moved_tok, wq, wk, wv, wo, state,
    acc, grad_normed, mixed, query, keys, values, scores_t, prior,
    fore, rear, grads, normed,
    terms, terms_landed, inputs, inputs_landed, outers, outers_landed, total, total_wo,
    load_sem, fore_sem, rear_sem,
    tok_sem, tok_moved, tok_landed, cot_sem, grads_sem, terms_sem, inputs_sem, outers_sem,
):
    seq, head = sizes
    head_inner, seq_inner = inner_size(head), inner_size(seq)
    head_outer, seq_outer = head // head_inner, seq // seq_inner
    shared = head // seq
    rows, wide = tok.shape[1:]
    columns = wq.shape[1]
    heads_here = columns // DH
    s, h = lax.axis_index("seq"), lax.axis_index("head")
    z, y = h // head_inner, h % head_inner
    outer = Line(z, head_outer, lambda place: (s, place * head_inner + y))
    inner = Line(y, head_inner, lambda place: (s, z * head_inner + place))
    chip = Line(s // seq_inner, seq_outer, lambda place: (place * seq_inner + s % seq_inner, h))
    core = Line(s % seq_inner, seq_inner, lambda place: (s // seq_inner * seq_inner + place, h))

    loads = [
        pltpu.make_async_copy(source, target, load_sem.at[number])
        for number, (source, target) in enumerate(
            [
                (tokens_in, tok.at[h]),
                (wq_in, wq), (wk_in, wk), (wv_in, wv),
                (cot_in, cot.at[h]), (wo_in, wo), (state_in, state),
            ]
        )
    ]
    for load in loads:
        load.start()

    barrier = pltpu.get_barrier_semaphore()
    expected = seq - 1
    for line in (outer, inner):
        for way in (0, 1):
            expected = expected + line.has(way).astype(jnp.int32)

            @pl.when(line.has(way))
            def _():
                pl.semaphore_signal(barrier, inc=1, device_id=line.next(way), device_id_type=MESH)
    for other in range(1, seq):
        pl.semaphore_signal(barrier, inc=1, device_id=((s + other) % seq, h), device_id_type=MESH)
    pl.semaphore_wait(barrier, expected)

    def early(slot):
        distance = abs(slot // head_inner - z)
        at_end = (z == 0) | (z == head_outer - 1)
        direct = (slot % head_inner == y) & at_end
        return (distance < head_outer - 2) | ((distance == head_outer - 2) & direct)

    def moves(slots, moved, sent, landed):
        def copy(slot):
            return pltpu.make_async_remote_copy(
                src_ref=slots.at[slot],
                dst_ref=moved.at[s, slot % shared],
                send_sem=sent.at[slot],
                recv_sem=landed.at[s, slot % shared],
                device_id=(slot // shared, h),
                device_id_type=MESH,
            )

        def start(slot):
            @pl.when(slot // shared != s)
            def _():
                copy(slot).start()

            @pl.when(slot // shared == s)
            def _():
                own = moved.at[s, slot % shared]
                pltpu.make_async_copy(slots.at[slot], own, landed.at[s, slot % shared]).start()

        def soon(slot):
            pl.when(early(slot))(lambda: start(slot))

        def late():
            @pl.loop(0, head)
            def _(slot):
                pl.when(jnp.logical_not(early(slot)))(lambda: start(slot))

        def finish():
            @pl.loop(0, head)
            def _(slot):
                @pl.when(slot // shared != s)
                def _():
                    copy(slot).wait_send()

        return soon, late, finish

    move_tok, move_tok_late, finish_tok = moves(tok, moved_tok, tok_moved, tok_landed)

    def project(slot):
        block = tok[slot]
        span = pl.ds(pl.multiple_of(slot * wide, wide), wide)
        for number, weight in enumerate((wq, wk, wv)):
            acc[number] += mul(block, weight[span, :])
        move_tok(slot)

    def pull(slot):
        span = pl.ds(pl.multiple_of(slot * wide, wide), wide)
        grad_normed[...] += mul(cot[slot], wo[:, span], NT)

    def each_row(distance, act):
        @pl.loop(0, 2)
        def _(side):
            place = z + (2 * side - 1) * distance
            pl.when((place >= 0) & (place < head_outer) & ((distance > 0) | (side == 0)))(lambda: act(place))

    tok_gather = Gather(tokens_in, tok, tok_sem, outer, inner, gather_parts(rows), project)
    cot_gather = Gather(cot_in, cot, cot_sem, outer, inner, gather_parts(rows), pull)
    nothing = lambda slot: None
    grads_gather = Gather(grads.at[s], grads, grads_sem, chip, core, ((0, 0, rows),), nothing)

    tok_gather.own(inner, (1,))
    tok_gather.own(outer)
    tok_gather.own(inner, (0,))
    acc[...] = jnp.zeros_like(acc)
    grad_normed[...] = jnp.zeros_like(grad_normed)
    for load in loads[:4]:
        load.wait()
    project(h)
    tok_gather.cross_row()

    @pl.loop(1, head_outer)
    def _(distance):
        tok_gather.from_outer(distance)

        @pl.when(distance == head_outer - 2)
        def _():
            cot_gather.own(outer)
            cot_gather.own(inner, (1,))

        tok_gather.from_inner(distance - 1)

    cot_gather.own(inner, (0,))
    cot_gather.cross_row()
    tok_gather.from_inner(head_outer - 1)

    for number, target in enumerate((query, keys, values)):
        target[...] = acc[number].astype(HALF)

    def part(ref, number):
        return ref[:, number * DH : (number + 1) * DH]

    for number in range(heads_here):
        fore[s, number] = mul(part(keys, number), part(values, number), TN).astype(HALF)

    def share(states, sems, wanted):
        def copy(other):
            return pltpu.make_async_remote_copy(
                src_ref=states.at[s],
                dst_ref=states.at[s],
                send_sem=sems.at[0, other],
                recv_sem=sems.at[1, s],
                device_id=(other, h),
                device_id_type=MESH,
            )

        def start():
            for other in range(seq):
                pl.when((other != s) & wanted(s, other))(lambda: copy(other).start())

        def arrive():
            for other in range(seq):

                @pl.when((other != s) & wanted(other, s))
                def _():
                    pltpu.make_async_copy(states.at[other], states.at[other], sems.at[1, other]).wait()

        def finish():
            for other in range(seq):
                pl.when((other != s) & wanted(s, other))(lambda: copy(other).wait_send())

        return start, arrive, finish

    start_fore, arrive_fore, finish_fore = share(fore, fore_sem, lambda source, target: source < target)
    start_rear, arrive_rear, finish_rear = share(rear, rear_sem, lambda source, target: target >= 0)
    start_fore()
    for load in loads[4:]:
        load.wait()
    move_tok_late()
    pull(h)
    at_end = (z == 0) | (z == head_outer - 1)
    pl.when(jnp.logical_not(at_end))(lambda: cot_gather.from_outer(1))

    below = lax.broadcasted_iota(jnp.int32, (rows, rows), 1) <= lax.broadcasted_iota(jnp.int32, (rows, rows), 0)
    above = lax.broadcasted_iota(jnp.int32, (rows, rows), 1) >= lax.broadcasted_iota(jnp.int32, (rows, rows), 0)
    for number in range(heads_here):
        query_h, keys_h = part(query, number), part(keys, number)
        scores = jnp.where(below, mul(query_h, keys_h, NT), 0.0).astype(HALF)
        scores_t[number] = jnp.where(above, mul(keys_h, query_h, NT), 0.0).astype(HALF)
        mixed[:, number * DH : (number + 1) * DH] = mul(scores, part(values, number))
    arrive_fore()
    for number in range(heads_here):
        before = state[number]
        for other in range(seq):
            before = before + jnp.where(other < s, fore[other, number].astype(WIDE), 0.0)
        prior[number] = before.astype(HALF)
        whole = part(mixed, number) + mul(part(query, number), prior[number])
        mixed[:, number * DH : (number + 1) * DH] = whole
        inv_norm = lax.rsqrt(jnp.mean(whole * whole, axis=-1, keepdims=True) + EPSILON)
        normed[:, number * DH : (number + 1) * DH] = (whole * inv_norm).astype(HALF)

    result_sums = Scatter(terms, terms_landed, terms_sem, outer, inner, result_parts(rows))

    def result_terms(row):
        @pl.loop(0, head_inner)
        def _(place):
            span = pl.ds(pl.multiple_of((row * head_inner + place) * wide, wide), wide)
            terms[row, place] = mul(normed[...], wo[:, span]).astype(HALF)

    each_row(head_outer - 1, result_terms)
    result_sums.outer_first(head_outer - 1)

    @pl.loop(1, head_outer)
    def _(turn):
        each_row(head_outer - 1 - turn, result_terms)

    pl.when(at_end)(lambda: cot_gather.from_outer(1))
    cot_gather.from_inner(0)
    for distance in range(2, head_outer):
        cot_gather.from_outer(distance)
        if distance < head_outer - 1:
            cot_gather.from_inner(distance - 1)
            result_sums.outer_first(head_outer - distance)

    @pl.loop(0, head_outer)
    def _(turn):
        each_row(head_outer - 1 - turn, result_sums.start_row)

    cot_gather.from_inner(head_outer - 2)
    if head_outer > 2:
        result_sums.outer_first(1)
    cot_gather.from_inner(head_outer - 1)

    for number in range(heads_here):
        whole, pulled = part(mixed, number), part(grad_normed, number)
        inv_norm = lax.rsqrt(jnp.mean(whole * whole, axis=-1, keepdims=True) + EPSILON)
        slope = jnp.mean(pulled * whole, axis=-1, keepdims=True)
        grad_mixed = (inv_norm * (pulled - whole * inv_norm * inv_norm * slope)).astype(HALF)
        grads[s, :, number * DH : (number + 1) * DH] = grad_mixed
        rear[s, number] = mul(part(query, number), grad_mixed, TN).astype(HALF)
    start_rear()

    outer_grads = Scatter(outers, outers_landed, outers_sem, chip, core, ((0, 0, shared * columns),))

    @pl.loop(0, head)
    def _(slot):
        owner = slot // shared
        span = pl.ds(pl.multiple_of(slot % shared * columns, columns), columns)
        share_wo = mul(normed[...], cot[slot], TN).astype(HALF)
        outers[owner // seq_inner, owner % seq_inner, span] = share_wo

    pl.loop(0, seq_outer)(outer_grads.start_row)
    for number in range(heads_here):
        span = slice(number * DH, (number + 1) * DH)
        grad_mixed = grads[s, :, span]
        query_h, keys_h, values_h = part(query, number), part(keys, number), part(values, number)
        grad_scores = jnp.where(below, mul(grad_mixed, values_h, NT), 0.0).astype(HALF)
        grad_scores_t = jnp.where(above, mul(values_h, grad_mixed, NT), 0.0).astype(HALF)
        acc[0, :, span] = mul(grad_scores, keys_h) + mul(grad_mixed, prior[number], NT)
        acc[1, :, span] = mul(grad_scores_t, query_h)
        acc[2, :, span] = mul(scores_t[number], grad_mixed)
    result_sums.outer_second(head_outer - 1)
    tok_gather.finish()
    finish_tok()
    finish_fore()
    arrive_rear()
    for number in range(heads_here):
        later = jnp.zeros((DH, DH), WIDE)
        every = jnp.zeros((DH, DH), WIDE)
        for other in range(seq):
            one = rear[other, number].astype(WIDE)
            later = later + jnp.where(other > s, one, 0.0)
            every = every + one
        grad_state[number] = every
        later = later.astype(HALF)
        span = slice(number * DH, (number + 1) * DH)
        acc[1, :, span] += mul(part(values, number), later, NT)
        acc[2, :, span] += mul(part(keys, number), later)
    for number in range(3):
        grads[s, :, number * columns : (number + 1) * columns] = acc[number].astype(HALF)

    input_sums = Scatter(inputs, inputs_landed, inputs_sem, outer, inner, input_parts(rows))

    def input_terms(place):
        @pl.loop(0, head_inner)
        def _(turn):
            owner = (y + 1 + turn) % head_inner
            span = pl.ds(pl.multiple_of((place * head_inner + owner) * wide, wide), wide)
            term = mul(grads[s, :, :columns], wq[span, :], NT)
            term += mul(grads[s, :, columns : 2 * columns], wk[span, :], NT)
            term += mul(grads[s, :, 2 * columns :], wv[span, :], NT)
            inputs[place, owner] = term.astype(HALF)

            @pl.when(turn == head_inner - 2)
            def _():
                input_sums.start_row(place)

    each_row(head_outer - 1, input_terms)
    input_sums.outer_first(head_outer - 1)
    grads_gather.own(chip)
    grads_gather.own(core)

    @pl.loop(1, head_outer)
    def _(turn):
        each_row(head_outer - 1 - turn, input_terms)

    def weight_grads(place):
        for number in range(shared):
            piece = moved_tok.at[place, number]
            span = slice(number * wide, (number + 1) * wide)
            pltpu.make_async_copy(piece, piece, tok_landed.at[place, number]).wait()
            for target, start in ((grad_wq, 0), (grad_wk, columns), (grad_wv, 2 * columns)):
                target[span, :] += mul(piece[...], grads[place, :, start : start + columns], TN)

    for target in (grad_wq, grad_wk, grad_wv):
        target[...] = jnp.zeros_like(target)
    for distance in range(seq_outer - 1, 0, -1):
        outer_grads.outer_second(distance)
    for distance in range(head_outer - 2, 1, -1):
        result_sums.outer_second(distance)
    for distance in range(head_outer - 2, 0, -1):
        input_sums.outer_first(distance)
    weight_grads(s)
    grads_gather.from_inner(0)

    @pl.loop(1, seq_inner)
    def _(step):
        weight_grads(chip.place * seq_inner + (core.place + step) % seq_inner)

    input_sums.outer_second(head_outer - 1)
    if head_outer > 2:
        result_sums.outer_second(1)
    for distance in range(head_outer - 2, 0, -1):
        input_sums.outer_second(distance)
        if distance == head_outer - 2:
            grads_gather.from_outer(1)
    for distance in range(2, seq_outer):
        grads_gather.from_outer(distance)
        grads_gather.from_inner(distance - 1)
    result_sums.turn()
    input_sums.turn()
    grads_gather.from_inner(seq_outer - 1)

    @pl.loop(seq_inner, seq)
    def _(step):
        place = (chip.place + step // seq_inner) % seq_outer
        weight_grads(place * seq_inner + step % seq_inner)

    outer_grads.total(total_wo)
    for number in range(shared):
        grad_wo[:, number * wide : (number + 1) * wide] = total_wo[number * columns : (number + 1) * columns, :]
    result_sums.total(total)
    result[...] = total[...].astype(HALF)
    cot_gather.finish()
    finish_rear()
    outer_grads.finish()
    input_sums.total(grad_tokens)
    for one in (grads_gather, result_sums, input_sums):
        one.finish()


def write_out(*refs):
    count = (len(refs) - 1) // 2
    copies = [pltpu.make_async_copy(refs[k], refs[count + k], refs[-1].at[k]) for k in range(count)]
    for copy in copies:
        copy.start()
    for copy in copies:
        copy.wait()


def solution(mesh):
    seq, head = mesh.shape["seq"], mesh.shape["head"]

    def on_device(tokens, w_query, w_key, w_value, w_out, grad_out, state_in):
        rows, wide = tokens.shape
        depth, columns = w_query.shape
        heads_here = columns // DH
        shared = head // seq
        assert rows == BLOCK and head % seq == 0
        head_inner, seq_inner = inner_size(head), inner_size(seq)
        head_outer, seq_outer = head // head_inner, seq // seq_inner
        vmem = lambda *shape: pltpu.VMEM(shape, HALF)
        full = lambda *shape: pltpu.VMEM(shape, WIDE)
        dma = lambda *shape: pltpu.SemaphoreType.DMA(shape)
        gathers = dma(sum(gather_sems(order, head_outer, head_inner) for order, *_ in gather_parts(rows)))
        sums = lambda parts: dma(sum(scatter_sems(order, head_outer, head_inner) for order, *_ in parts))
        outs = [
            ((rows, wide), HALF), ((rows, wide), WIDE),
            ((shared * wide, columns), WIDE), ((shared * wide, columns), WIDE), ((shared * wide, columns), WIDE),
            ((columns, shared * wide), WIDE), ((heads_here, DH, DH), WIDE),
        ]
        done = pl.pallas_call(
            lambda *refs: layer((seq, head), *refs),
            out_shape=[pltpu.VMEM(shape, kind) for shape, kind in outs],
            in_specs=[pl.BlockSpec(memory_space=pltpu.HBM)] * 7,
            out_specs=[pl.BlockSpec(memory_space=pltpu.VMEM)] * 7,
            scratch_shapes=[
                vmem(head, rows, wide), vmem(head, rows, wide),
                vmem(seq, shared, rows, wide),
                vmem(depth, columns), vmem(depth, columns), vmem(depth, columns), vmem(columns, depth),
                full(heads_here, DH, DH),
                full(3, rows, columns), full(rows, columns), full(rows, columns),
                vmem(rows, columns), vmem(rows, columns), vmem(rows, columns),
                vmem(heads_here, rows, rows), vmem(heads_here, DH, DH),
                vmem(seq, heads_here, DH, DH), vmem(seq, heads_here, DH, DH),
                vmem(seq, rows, 3 * columns), vmem(rows, columns),
                vmem(head_outer, head_inner, rows, wide), vmem(2, 2, head_outer, head_inner, rows, wide),
                vmem(head_outer, head_inner, rows, wide), vmem(2, 2, head_outer, head_inner, rows, wide),
                vmem(seq_outer, seq_inner, shared * columns, wide),
                vmem(2, 2, seq_outer, seq_inner, shared * columns, wide),
                full(rows, wide), full(shared * columns, wide),
                dma(7), dma(2, seq), dma(2, seq),
                gathers, dma(head), dma(seq, shared), gathers, dma(gather_sems(0, seq_outer, seq_inner)),
                sums(result_parts(rows)), sums(input_parts(rows)), dma(scatter_sems(0, seq_outer, seq_inner)),
            ],
            compiler_params=pltpu.CompilerParams(
                collective_id=0, has_side_effects=True, vmem_limit_bytes=54 * 1024 * 1024
            ),
        )(tokens, w_query, w_key, w_value, w_out, grad_out, state_in)
        return pl.pallas_call(
            write_out,
            out_shape=[jax.ShapeDtypeStruct(shape, kind) for shape, kind in outs],
            in_specs=[pl.BlockSpec(memory_space=pl.ANY)] * 7,
            out_specs=[pl.BlockSpec(memory_space=pltpu.HBM)] * 7,
            scratch_shapes=[dma(7)],
            compiler_params=pltpu.CompilerParams(vmem_limit_bytes=1024 * 1024),
        )(*done)

    by_head = P(None, "head")
    tiled = P("seq", "head")
    return jax.shard_map(
        on_device,
        mesh=mesh,
        in_specs=(tiled, by_head, by_head, by_head, P("head", None), tiled, P("head", None, None)),
        out_specs=(tiled, tiled, tiled, tiled, tiled, P("head", "seq"), P("head", None, None)),
        check_vma=False,
    )
```

```python
import jax
import jax.numpy as jnp
from jax import lax
from jax.experimental import pallas as pl
from jax.experimental.pallas import tpu as pltpu
from jax.sharding import PartitionSpec as P

DH = 128
BLOCK = 256
EPSILON = 1e-06
WIDE = jnp.float32
HALF = jnp.bfloat16
MESH = pl.DeviceIdType.MESH
NN = (((1,), (0,)), ((), ()))
NT = (((1,), (1,)), ((), ()))
TN = (((0,), (0,)), ((), ()))


def mul(left, right, dims=NN):
    return lax.dot_general(left, right, dims, preferred_element_type=WIDE)


def parts(rows, shares):
    unit, start, cut = rows // 16, 0, []
    for order, share in shares:
        cut.append((order, start, share * unit))
        start += share * unit
    return cut


def gather_parts(rows):
    return parts(rows, ((0, 7), (0, 6), (1, 3)))


def result_parts(rows):
    return parts(rows, ((1, 10), (0, 6)))


def input_parts(rows):
    return parts(rows, ((0, 7), (0, 7), (1, 2)))


def inner_size(count):
    inner = 1
    while 4 * inner * inner <= count:
        inner *= 2
    return inner


class Line:
    def __init__(self, place, size, device):
        self.place, self.size, self.device = place, size, device

    def has(self, way):
        return self.place < self.size - 1 if way == 0 else self.place > 0

    def next(self, way):
        return self.device(self.place + (1 if way == 0 else -1))


def outer_sems(order, outer, inner):
    return outer + 1 if order == 0 else outer * inner + inner


def inner_sems(order, outer, inner):
    if inner == 2:
        return outer if order == 0 else 1
    return outer * inner + outer if order == 0 else inner + 1


def gather_sems(order, outer, inner):
    return outer * inner + outer_sems(order, outer, inner) + inner_sems(order, outer, inner)


def scatter_sems(order, outer, inner):
    first, second = (inner, outer) if order == 0 else (outer, inner)
    return second * (2 * first + 1) + 2 * second + 1


class Gather:
    def __init__(self, source, slots, sems, outer, inner, parts, seen):
        self.source, self.slots, self.sems = source, slots, sems
        self.outer, self.inner, self.seen = outer, inner, seen
        self.parts, base = [], 0
        for order, start, rows in parts:
            self.parts.append((base, order, start, rows))
            base += gather_sems(order, outer.size, inner.size)

    def slot(self, place_outer, place_inner):
        return place_outer * self.inner.size + place_inner

    def copy(self, part, slot, line, way, source=None):
        base, order, start, rows = part
        row, place = slot // self.inner.size, slot % self.inner.size
        sent = base + self.outer.size * self.inner.size
        if line is self.outer:
            if order == 0:
                twice, once, more = row == line.place, row, line.size
            else:
                twice, once, more = row == line.place, slot, line.size * self.inner.size + place
        else:
            sent += outer_sems(order, self.outer.size, self.inner.size)
            index = row if order == 0 else 0
            if line.size > 2:
                index = slot if order == 0 else place
            more = index if line.size == 2 else (line.size * self.outer.size + row if order == 0 else line.size)
            twice, once = place == line.place, index
        sent += jnp.where(twice, more, once) if way == 1 else once
        piece = self.slots.at[slot, pl.ds(start, rows)]
        return pltpu.make_async_remote_copy(
            src_ref=piece if source is None else source.at[pl.ds(start, rows)],
            dst_ref=piece,
            send_sem=self.sems.at[sent],
            recv_sem=self.sems.at[base + slot],
            device_id=line.next(way),
            device_id_type=MESH,
        )

    def send(self, part, slot, line, way, also=True, source=None):
        @pl.when(line.has(way) & also)
        def _():
            self.copy(part, slot, line, way, source).start()

    def arrive(self, part, slot):
        base, _, start, rows = part
        piece = self.slots.at[slot, pl.ds(start, rows)]
        pltpu.make_async_copy(piece, piece, self.sems.at[base + slot]).wait()

    def own(self, line, orders=(0, 1)):
        slot = self.slot(self.outer.place, self.inner.place)
        for part in self.parts:
            if part[1] in orders:
                for way in (0, 1):
                    self.send(part, slot, line, way, source=self.source)

    def cross_row(self):
        for part in self.parts:
            if part[1] == 1:
                for way in (0, 1):
                    for step in range(1, self.inner.size):
                        place = self.inner.place + (-step if way == 0 else step)

                        @pl.when((place >= 0) & (place < self.inner.size))
                        def _():
                            slot = self.slot(self.outer.place, place)
                            self.arrive(part, slot)
                            self.send(part, slot, self.inner, way)
                            self.send(part, slot, self.outer, 0)
                            self.send(part, slot, self.outer, 1)

    def each_side(self, distance, act):
        @pl.loop(0, 2)
        def _(side):
            row = self.outer.place + (2 * side - 1) * distance

            @pl.when((row >= 0) & (row < self.outer.size) & ((distance > 0) | (side == 0)))
            def _():
                act(side, row)

    def from_outer(self, distance):
        steps = [(part, 0) for part in self.parts]
        steps += [(part, turn) for turn in range(1, self.inner.size) for part in self.parts if part[1] == 1]
        for part, turn in steps:

            def pass_on(side, row):
                slot = self.slot(row, (self.inner.place + turn) % self.inner.size)
                self.arrive(part, slot)
                self.send(part, slot, self.outer, 0, side == 0)
                self.send(part, slot, self.outer, 1, side == 1)
                if part[1] == 0:
                    self.send(part, slot, self.inner, 0)
                    self.send(part, slot, self.inner, 1)

            self.each_side(distance, pass_on)
        self.each_side(distance, lambda side, row: self.seen(self.slot(row, self.inner.place)))

    def from_inner(self, distance):
        def each_place(side, row):
            @pl.loop(0, 2)
            def _(way):
                @pl.loop(1, self.inner.size)
                def _(step):
                    place = self.inner.place + (2 * way - 1) * step

                    @pl.when((place >= 0) & (place < self.inner.size))
                    def _():
                        slot = self.slot(row, place)
                        for part in self.parts:
                            if part[1] == 0:
                                self.arrive(part, slot)
                                self.send(part, slot, self.inner, 0, way == 0)
                                self.send(part, slot, self.inner, 1, way == 1)
                        self.seen(slot)

        self.each_side(distance, each_place)

    def finish(self):
        @pl.loop(0, self.outer.size)
        def _(row):
            @pl.loop(0, self.inner.size)
            def _(place):
                slot = self.slot(row, place)
                for part in self.parts:
                    for way in (0, 1):
                        passed = (row <= self.outer.place) if way == 0 else (row >= self.outer.place)
                        if part[1] == 0:
                            passed &= place == self.inner.place

                        @pl.when(self.outer.has(way) & passed)
                        def _():
                            self.copy(part, slot, self.outer, way).wait_send()

                        passed = (place <= self.inner.place) if way == 0 else (place >= self.inner.place)
                        if part[1] == 1:
                            passed &= row == self.outer.place

                        @pl.when(self.inner.has(way) & passed)
                        def _():
                            self.copy(part, slot, self.inner, way).wait_send()


class Reduce:
    def __init__(self, line, term, landed, sems, base):
        self.line, self.term, self.landed, self.sems, self.base = line, term, landed, sems, base

    def landing(self, way, owner, place):
        index = self.base + self.line.size + owner
        return self.sems.at[index if way == 0 else jnp.where(owner == place, self.base + 2 * self.line.size, index)]

    def copy(self, way, owner):
        return pltpu.make_async_remote_copy(
            src_ref=self.term(owner),
            dst_ref=self.landed(way, owner),
            send_sem=self.sems.at[self.base + owner],
            recv_sem=self.landing(way, owner, self.line.place + (1 if way == 0 else -1)),
            device_id=self.line.next(way),
            device_id_type=MESH,
        )

    def arrive(self, way, owner, act):
        @pl.when(self.line.has(1 - way))
        def _():
            piece = self.landed(way, owner)
            pltpu.make_async_copy(piece, piece, self.landing(way, owner, self.line.place)).wait()
            act(piece[...].astype(WIDE))

    def add(self, way, owner):
        term = self.term(owner)

        def act(value):
            term[...] = (term[...].astype(WIDE) + value).astype(HALF)

        self.arrive(way, owner, act)

    def each(self, distance, act):
        for way in (0, 1):
            owner = self.line.place + (distance if way == 0 else -distance)
            pl.when((owner >= 0) & (owner < self.line.size))(lambda: act(way, owner))

    def step(self, distance):
        def act(way, owner):
            self.add(way, owner)
            self.copy(way, owner).start()

        self.each(distance, act)

    def finish(self):
        for distance in range(1, self.line.size):
            self.each(distance, lambda way, owner: self.copy(way, owner).wait_send())


class Scatter:
    def __init__(self, terms, landed, sems, outer, inner, parts):
        self.terms, self.landed, self.sems = terms, landed, sems
        self.outer, self.inner = outer, inner
        self.parts, base = [], 0
        for order, start, rows in parts:
            self.parts.append((base, order, start, rows))
            base += scatter_sems(order, outer.size, inner.size)

    def along_outer(self, part, place):
        base, order, start, rows = part
        span = pl.ds(start, rows)
        base += self.outer.size * (2 * self.inner.size + 1) if order == 0 else place * (2 * self.outer.size + 1)
        return Reduce(
            self.outer,
            lambda owner: self.terms.at[owner, place, span],
            lambda way, owner: self.landed.at[0, way, owner, place, span],
            self.sems,
            base,
        )

    def along_inner(self, part, row):
        base, order, start, rows = part
        span = pl.ds(start, rows)
        base += self.inner.size * (2 * self.outer.size + 1) if order == 1 else row * (2 * self.inner.size + 1)
        return Reduce(
            self.inner,
            lambda owner: self.terms.at[row, owner, span],
            lambda way, owner: self.landed.at[1, way, row, owner, span],
            self.sems,
            base,
        )

    def steps_inner(self, part, row):
        line = self.along_inner(part, row)
        for distance in range(self.inner.size - 1, 0, -1):
            line.step(distance)

    def start_row(self, row):
        for part in self.parts:
            if part[1] == 0:
                self.steps_inner(part, row)

    def outer_first(self, distance):
        for part in self.parts:
            if part[1] == 1:
                for place in range(self.inner.size):
                    self.along_outer(part, place).step(distance)

    def outer_second(self, distance):
        for part in self.parts:
            if part[1] == 0:

                def act(way, row):
                    for side in (0, 1):
                        self.along_inner(part, row).add(side, self.inner.place)

                self.along_outer(part, self.inner.place).each(distance, act)
                self.along_outer(part, self.inner.place).step(distance)

    def turn(self):
        for part in self.parts:
            if part[1] == 1:
                for place in range(self.inner.size):

                    @pl.when(place != self.inner.place)
                    def _():
                        for way in (0, 1):
                            self.along_outer(part, place).add(way, self.outer.place)

                self.steps_inner(part, self.outer.place)

    def total(self, out):
        row, place = self.outer.place, self.inner.place
        for part in self.parts:
            span = pl.ds(part[2], part[3])
            held = [self.terms[row, place, span].astype(WIDE)]
            out[span, :] = held[0].astype(out.dtype)

            def act(value):
                out[span, :] = (out[span, :].astype(WIDE) + value).astype(out.dtype)

            for way in (0, 1):
                self.along_outer(part, place).arrive(way, row, act)
                self.along_inner(part, row).arrive(way, place, act)

    def finish(self):
        for part in self.parts:
            if part[1] == 0:
                pl.loop(0, self.outer.size)(lambda row: self.along_inner(part, row).finish())
                self.along_outer(part, self.inner.place).finish()
            else:
                pl.loop(0, self.inner.size)(lambda place: self.along_outer(part, place).finish())
                self.along_inner(part, self.outer.place).finish()


def layer(
    sizes,
    tokens_in, wq_in, wk_in, wv_in, wo_in, cot_in, state_in,
    result, grad_tokens, grad_wq, grad_wk, grad_wv, grad_wo, grad_state,
    tok, cot, moved_tok, wq, wk, wv, wo, state,
    acc, grad_normed, mixed, query, keys, values, scores_t, prior,
    fore, rear, grads, normed,
    terms, terms_landed, inputs, inputs_landed, outers, outers_landed, total, total_wo,
    load_sem, fore_sem, rear_sem,
    tok_sem, tok_moved, tok_landed, cot_sem, grads_sem, terms_sem, inputs_sem, outers_sem,
):
    seq, head = sizes
    head_inner, seq_inner = inner_size(head), inner_size(seq)
    head_outer, seq_outer = head // head_inner, seq // seq_inner
    shared = head // seq
    rows, wide = tok.shape[1:]
    columns = wq.shape[1]
    heads_here = columns // DH
    s, h = lax.axis_index("seq"), lax.axis_index("head")
    z, y = h // head_inner, h % head_inner
    outer = Line(z, head_outer, lambda place: (s, place * head_inner + y))
    inner = Line(y, head_inner, lambda place: (s, z * head_inner + place))
    chip = Line(s // seq_inner, seq_outer, lambda place: (place * seq_inner + s % seq_inner, h))
    core = Line(s % seq_inner, seq_inner, lambda place: (s // seq_inner * seq_inner + place, h))

    loads = [
        pltpu.make_async_copy(source, target, load_sem.at[number])
        for number, (source, target) in enumerate(
            [
                (tokens_in, tok.at[h]),
                (wq_in, wq), (wk_in, wk), (wv_in, wv),
                (cot_in, cot.at[h]), (wo_in, wo), (state_in, state),
            ]
        )
    ]
    for load in loads:
        load.start()

    barrier = pltpu.get_barrier_semaphore()
    expected = seq - 1
    for line in (outer, inner):
        for way in (0, 1):
            expected = expected + line.has(way).astype(jnp.int32)

            @pl.when(line.has(way))
            def _():
                pl.semaphore_signal(barrier, inc=1, device_id=line.next(way), device_id_type=MESH)
    for other in range(1, seq):
        pl.semaphore_signal(barrier, inc=1, device_id=((s + other) % seq, h), device_id_type=MESH)
    pl.semaphore_wait(barrier, expected)

    def early(slot):
        distance = abs(slot // head_inner - z)
        at_end = (z == 0) | (z == head_outer - 1)
        direct = (slot % head_inner == y) & at_end
        return (distance < head_outer - 2) | ((distance == head_outer - 2) & direct)

    def moves(slots, moved, sent, landed):
        def copy(slot):
            return pltpu.make_async_remote_copy(
                src_ref=slots.at[slot],
                dst_ref=moved.at[s, slot % shared],
                send_sem=sent.at[slot],
                recv_sem=landed.at[s, slot % shared],
                device_id=(slot // shared, h),
                device_id_type=MESH,
            )

        def start(slot):
            @pl.when(slot // shared != s)
            def _():
                copy(slot).start()

            @pl.when(slot // shared == s)
            def _():
                own = moved.at[s, slot % shared]
                pltpu.make_async_copy(slots.at[slot], own, landed.at[s, slot % shared]).start()

        def soon(slot):
            pl.when(early(slot))(lambda: start(slot))

        def late():
            @pl.loop(0, head)
            def _(slot):
                pl.when(jnp.logical_not(early(slot)))(lambda: start(slot))

        def finish():
            @pl.loop(0, head)
            def _(slot):
                @pl.when(slot // shared != s)
                def _():
                    copy(slot).wait_send()

        return soon, late, finish

    move_tok, move_tok_late, finish_tok = moves(tok, moved_tok, tok_moved, tok_landed)

    def project(slot):
        block = tok[slot]
        span = pl.ds(pl.multiple_of(slot * wide, wide), wide)
        for number, weight in enumerate((wq, wk, wv)):
            acc[number] += mul(block, weight[span, :])
        move_tok(slot)

    def pull(slot):
        span = pl.ds(pl.multiple_of(slot * wide, wide), wide)
        grad_normed[...] += mul(cot[slot], wo[:, span], NT)

    def each_row(distance, act):
        @pl.loop(0, 2)
        def _(side):
            place = z + (2 * side - 1) * distance
            pl.when((place >= 0) & (place < head_outer) & ((distance > 0) | (side == 0)))(lambda: act(place))

    tok_gather = Gather(tokens_in, tok, tok_sem, outer, inner, gather_parts(rows), project)
    cot_gather = Gather(cot_in, cot, cot_sem, outer, inner, gather_parts(rows), pull)
    nothing = lambda slot: None
    grads_gather = Gather(grads.at[s], grads, grads_sem, chip, core, ((0, 0, rows),), nothing)

    tok_gather.own(inner, (1,))
    tok_gather.own(outer)
    tok_gather.own(inner, (0,))
    acc[...] = jnp.zeros_like(acc)
    grad_normed[...] = jnp.zeros_like(grad_normed)
    for load in loads[:4]:
        load.wait()
    project(h)
    tok_gather.cross_row()

    @pl.loop(1, head_outer)
    def _(distance):
        tok_gather.from_outer(distance)

        @pl.when(distance == head_outer - 2)
        def _():
            cot_gather.own(outer)
            cot_gather.own(inner, (1,))

        tok_gather.from_inner(distance - 1)

    cot_gather.own(inner, (0,))
    cot_gather.cross_row()
    tok_gather.from_inner(head_outer - 1)

    for number, target in enumerate((query, keys, values)):
        target[...] = acc[number].astype(HALF)

    def part(ref, number):
        return ref[:, number * DH : (number + 1) * DH]

    for number in range(heads_here):
        fore[s, number] = mul(part(keys, number), part(values, number), TN).astype(HALF)

    def share(states, sems, wanted):
        def copy(other):
            return pltpu.make_async_remote_copy(
                src_ref=states.at[s],
                dst_ref=states.at[s],
                send_sem=sems.at[0, other],
                recv_sem=sems.at[1, s],
                device_id=(other, h),
                device_id_type=MESH,
            )

        def start():
            for other in range(seq):
                pl.when((other != s) & wanted(s, other))(lambda: copy(other).start())

        def arrive():
            for other in range(seq):

                @pl.when((other != s) & wanted(other, s))
                def _():
                    pltpu.make_async_copy(states.at[other], states.at[other], sems.at[1, other]).wait()

        def finish():
            for other in range(seq):
                pl.when((other != s) & wanted(s, other))(lambda: copy(other).wait_send())

        return start, arrive, finish

    start_fore, arrive_fore, finish_fore = share(fore, fore_sem, lambda source, target: source < target)
    start_rear, arrive_rear, finish_rear = share(rear, rear_sem, lambda source, target: target >= 0)
    start_fore()
    for load in loads[4:]:
        load.wait()
    move_tok_late()
    pull(h)
    at_end = (z == 0) | (z == head_outer - 1)
    pl.when(jnp.logical_not(at_end))(lambda: cot_gather.from_outer(1))

    below = lax.broadcasted_iota(jnp.int32, (rows, rows), 1) <= lax.broadcasted_iota(jnp.int32, (rows, rows), 0)
    above = lax.broadcasted_iota(jnp.int32, (rows, rows), 1) >= lax.broadcasted_iota(jnp.int32, (rows, rows), 0)
    for number in range(heads_here):
        query_h, keys_h = part(query, number), part(keys, number)
        scores = jnp.where(below, mul(query_h, keys_h, NT), 0.0).astype(HALF)
        scores_t[number] = jnp.where(above, mul(keys_h, query_h, NT), 0.0).astype(HALF)
        mixed[:, number * DH : (number + 1) * DH] = mul(scores, part(values, number))
    arrive_fore()
    for number in range(heads_here):
        before = state[number]
        for other in range(seq):
            before = before + jnp.where(other < s, fore[other, number].astype(WIDE), 0.0)
        prior[number] = before.astype(HALF)
        whole = part(mixed, number) + mul(part(query, number), prior[number])
        mixed[:, number * DH : (number + 1) * DH] = whole
        inv_norm = lax.rsqrt(jnp.mean(whole * whole, axis=-1, keepdims=True) + EPSILON)
        normed[:, number * DH : (number + 1) * DH] = (whole * inv_norm).astype(HALF)

    result_sums = Scatter(terms, terms_landed, terms_sem, outer, inner, result_parts(rows))

    def result_terms(row):
        @pl.loop(0, head_inner)
        def _(place):
            span = pl.ds(pl.multiple_of((row * head_inner + place) * wide, wide), wide)
            terms[row, place] = mul(normed[...], wo[:, span]).astype(HALF)

    each_row(head_outer - 1, result_terms)
    result_sums.outer_first(head_outer - 1)

    for distance in range(head_outer - 2, 0, -1):
        each_row(distance, result_terms)
        pl.when(at_end)(lambda: result_sums.outer_first(distance))
    each_row(0, result_terms)
    pl.when(at_end)(lambda: cot_gather.from_outer(1))
    cot_gather.from_inner(0)
    for distance in range(2, head_outer):
        cot_gather.from_outer(distance)
        if distance < head_outer - 1:
            cot_gather.from_inner(distance - 1)
            pl.when(jnp.logical_not(at_end))(lambda: result_sums.outer_first(head_outer - distance))

    @pl.loop(0, head_outer)
    def _(turn):
        each_row(head_outer - 1 - turn, result_sums.start_row)

    cot_gather.from_inner(head_outer - 2)
    cot_gather.from_inner(head_outer - 1)

    for number in range(heads_here):
        whole, pulled = part(mixed, number), part(grad_normed, number)
        inv_norm = lax.rsqrt(jnp.mean(whole * whole, axis=-1, keepdims=True) + EPSILON)
        slope = jnp.mean(pulled * whole, axis=-1, keepdims=True)
        grad_mixed = (inv_norm * (pulled - whole * inv_norm * inv_norm * slope)).astype(HALF)
        grads[s, :, number * DH : (number + 1) * DH] = grad_mixed
        rear[s, number] = mul(part(query, number), grad_mixed, TN).astype(HALF)
    start_rear()

    outer_grads = Scatter(outers, outers_landed, outers_sem, chip, core, ((0, 0, shared * columns),))

    @pl.loop(0, head)
    def _(slot):
        owner = slot // shared
        span = pl.ds(pl.multiple_of(slot % shared * columns, columns), columns)
        share_wo = mul(normed[...], cot[slot], TN).astype(HALF)
        outers[owner // seq_inner, owner % seq_inner, span] = share_wo

    pl.loop(0, seq_outer)(outer_grads.start_row)
    for number in range(heads_here):
        span = slice(number * DH, (number + 1) * DH)
        grad_mixed = grads[s, :, span]
        query_h, keys_h, values_h = part(query, number), part(keys, number), part(values, number)
        grad_scores = jnp.where(below, mul(grad_mixed, values_h, NT), 0.0).astype(HALF)
        grad_scores_t = jnp.where(above, mul(values_h, grad_mixed, NT), 0.0).astype(HALF)
        acc[0, :, span] = mul(grad_scores, keys_h) + mul(grad_mixed, prior[number], NT)
        acc[1, :, span] = mul(grad_scores_t, query_h)
        acc[2, :, span] = mul(scores_t[number], grad_mixed)
    if head_outer > 2:
        pl.when(jnp.logical_not(at_end))(lambda: result_sums.outer_first(1))
    result_sums.outer_second(head_outer - 1)
    tok_gather.finish()
    finish_tok()
    finish_fore()
    arrive_rear()
    for number in range(heads_here):
        later = jnp.zeros((DH, DH), WIDE)
        every = jnp.zeros((DH, DH), WIDE)
        for other in range(seq):
            one = rear[other, number].astype(WIDE)
            later = later + jnp.where(other > s, one, 0.0)
            every = every + one
        grad_state[number] = every
        later = later.astype(HALF)
        span = slice(number * DH, (number + 1) * DH)
        acc[1, :, span] += mul(part(values, number), later, NT)
        acc[2, :, span] += mul(part(keys, number), later)
    for number in range(3):
        grads[s, :, number * columns : (number + 1) * columns] = acc[number].astype(HALF)

    input_sums = Scatter(inputs, inputs_landed, inputs_sem, outer, inner, input_parts(rows))

    def input_terms(place):
        @pl.loop(0, head_inner)
        def _(turn):
            owner = (y + 1 + turn) % head_inner
            span = pl.ds(pl.multiple_of((place * head_inner + owner) * wide, wide), wide)
            term = mul(grads[s, :, :columns], wq[span, :], NT)
            term += mul(grads[s, :, columns : 2 * columns], wk[span, :], NT)
            term += mul(grads[s, :, 2 * columns :], wv[span, :], NT)
            inputs[place, owner] = term.astype(HALF)

            @pl.when(turn == head_inner - 2)
            def _():
                input_sums.start_row(place)

    each_row(head_outer - 1, input_terms)
    input_sums.outer_first(head_outer - 1)
    grads_gather.own(chip)
    grads_gather.own(core)

    for distance in range(head_outer - 2, 0, -1):
        each_row(distance, input_terms)
        pl.when(at_end)(lambda: input_sums.outer_first(distance))
    each_row(0, input_terms)

    def weight_grads(place):
        for number in range(shared):
            piece = moved_tok.at[place, number]
            span = slice(number * wide, (number + 1) * wide)
            pltpu.make_async_copy(piece, piece, tok_landed.at[place, number]).wait()
            for target, start in ((grad_wq, 0), (grad_wk, columns), (grad_wv, 2 * columns)):
                target[span, :] += mul(piece[...], grads[place, :, start : start + columns], TN)

    for target in (grad_wq, grad_wk, grad_wv):
        target[...] = jnp.zeros_like(target)
    for distance in range(seq_outer - 1, 0, -1):
        outer_grads.outer_second(distance)
    for distance in range(head_outer - 2, 1, -1):
        result_sums.outer_second(distance)
    weight_grads(s)
    grads_gather.from_inner(0)

    @pl.loop(1, seq_inner)
    def _(step):
        weight_grads(chip.place * seq_inner + (core.place + step) % seq_inner)

    input_sums.outer_second(head_outer - 1)
    if head_outer > 2:
        result_sums.outer_second(1)
    for distance in range(head_outer - 2, 0, -1):
        pl.when(jnp.logical_not(at_end))(lambda: input_sums.outer_first(distance))
    for distance in range(head_outer - 2, 0, -1):
        input_sums.outer_second(distance)
        if distance == head_outer - 2:
            grads_gather.from_outer(1)
    for distance in range(2, seq_outer):
        grads_gather.from_outer(distance)
        grads_gather.from_inner(distance - 1)
    result_sums.turn()
    input_sums.turn()
    grads_gather.from_inner(seq_outer - 1)

    @pl.loop(seq_inner, seq)
    def _(step):
        place = (chip.place + step // seq_inner) % seq_outer
        weight_grads(place * seq_inner + step % seq_inner)

    outer_grads.total(total_wo)
    for number in range(shared):
        grad_wo[:, number * wide : (number + 1) * wide] = total_wo[number * columns : (number + 1) * columns, :]
    result_sums.total(total)
    result[...] = total[...].astype(HALF)
    cot_gather.finish()
    finish_rear()
    outer_grads.finish()
    input_sums.total(grad_tokens)
    for one in (grads_gather, result_sums, input_sums):
        one.finish()


def write_out(*refs):
    count = (len(refs) - 1) // 2
    copies = [pltpu.make_async_copy(refs[k], refs[count + k], refs[-1].at[k]) for k in range(count)]
    for copy in copies:
        copy.start()
    for copy in copies:
        copy.wait()


def solution(mesh):
    seq, head = mesh.shape["seq"], mesh.shape["head"]

    def on_device(tokens, w_query, w_key, w_value, w_out, grad_out, state_in):
        rows, wide = tokens.shape
        depth, columns = w_query.shape
        heads_here = columns // DH
        shared = head // seq
        assert rows == BLOCK and head % seq == 0
        head_inner, seq_inner = inner_size(head), inner_size(seq)
        head_outer, seq_outer = head // head_inner, seq // seq_inner
        vmem = lambda *shape: pltpu.VMEM(shape, HALF)
        full = lambda *shape: pltpu.VMEM(shape, WIDE)
        dma = lambda *shape: pltpu.SemaphoreType.DMA(shape)
        gathers = dma(sum(gather_sems(order, head_outer, head_inner) for order, *_ in gather_parts(rows)))
        sums = lambda parts: dma(sum(scatter_sems(order, head_outer, head_inner) for order, *_ in parts))
        outs = [
            ((rows, wide), HALF), ((rows, wide), WIDE),
            ((shared * wide, columns), WIDE), ((shared * wide, columns), WIDE), ((shared * wide, columns), WIDE),
            ((columns, shared * wide), WIDE), ((heads_here, DH, DH), WIDE),
        ]
        done = pl.pallas_call(
            lambda *refs: layer((seq, head), *refs),
            out_shape=[pltpu.VMEM(shape, kind) for shape, kind in outs],
            in_specs=[pl.BlockSpec(memory_space=pltpu.HBM)] * 7,
            out_specs=[pl.BlockSpec(memory_space=pltpu.VMEM)] * 7,
            scratch_shapes=[
                vmem(head, rows, wide), vmem(head, rows, wide),
                vmem(seq, shared, rows, wide),
                vmem(depth, columns), vmem(depth, columns), vmem(depth, columns), vmem(columns, depth),
                full(heads_here, DH, DH),
                full(3, rows, columns), full(rows, columns), full(rows, columns),
                vmem(rows, columns), vmem(rows, columns), vmem(rows, columns),
                vmem(heads_here, rows, rows), vmem(heads_here, DH, DH),
                vmem(seq, heads_here, DH, DH), vmem(seq, heads_here, DH, DH),
                vmem(seq, rows, 3 * columns), vmem(rows, columns),
                vmem(head_outer, head_inner, rows, wide), vmem(2, 2, head_outer, head_inner, rows, wide),
                vmem(head_outer, head_inner, rows, wide), vmem(2, 2, head_outer, head_inner, rows, wide),
                vmem(seq_outer, seq_inner, shared * columns, wide),
                vmem(2, 2, seq_outer, seq_inner, shared * columns, wide),
                full(rows, wide), full(shared * columns, wide),
                dma(7), dma(2, seq), dma(2, seq),
                gathers, dma(head), dma(seq, shared), gathers, dma(gather_sems(0, seq_outer, seq_inner)),
                sums(result_parts(rows)), sums(input_parts(rows)), dma(scatter_sems(0, seq_outer, seq_inner)),
            ],
            compiler_params=pltpu.CompilerParams(
                collective_id=0, has_side_effects=True, vmem_limit_bytes=54 * 1024 * 1024
            ),
        )(tokens, w_query, w_key, w_value, w_out, grad_out, state_in)
        return pl.pallas_call(
            write_out,
            out_shape=[jax.ShapeDtypeStruct(shape, kind) for shape, kind in outs],
            in_specs=[pl.BlockSpec(memory_space=pl.ANY)] * 7,
            out_specs=[pl.BlockSpec(memory_space=pltpu.HBM)] * 7,
            scratch_shapes=[dma(7)],
            compiler_params=pltpu.CompilerParams(vmem_limit_bytes=1024 * 1024),
        )(*done)

    by_head = P(None, "head")
    tiled = P("seq", "head")
    return jax.shard_map(
        on_device,
        mesh=mesh,
        in_specs=(tiled, by_head, by_head, by_head, P("head", None), tiled, P("head", None, None)),
        out_specs=(tiled, tiled, tiled, tiled, tiled, P("head", "seq"), P("head", None, None)),
        check_vma=False,
    )
```

```python
import jax
import jax.numpy as jnp
from jax import lax
from jax.experimental import pallas as pl
from jax.experimental.pallas import tpu as pltpu
from jax.sharding import PartitionSpec as P

DH = 128
BLOCK = 256
EPSILON = 1e-06
WIDE = jnp.float32
HALF = jnp.bfloat16
MESH = pl.DeviceIdType.MESH
NN = (((1,), (0,)), ((), ()))
NT = (((1,), (1,)), ((), ()))
TN = (((0,), (0,)), ((), ()))


def mul(left, right, dims=NN):
    return lax.dot_general(left, right, dims, preferred_element_type=WIDE)


def parts(rows, shares):
    unit, start, cut = rows // 16, 0, []
    for order, share in shares:
        cut.append((order, start, share * unit))
        start += share * unit
    return cut


def gather_parts(rows):
    return parts(rows, ((0, 7), (0, 6), (1, 3)))


def cot_parts(rows):
    return parts(rows, ((0, 7), (0, 6), (1, 3)))


def result_parts(rows):
    return parts(rows, ((1, 10), (0, 6)))


def input_parts(rows):
    return parts(rows, ((0, 7), (0, 7), (1, 2)))


def inner_size(count):
    inner = 1
    while 4 * inner * inner <= count:
        inner *= 2
    return inner


class Line:
    def __init__(self, place, size, device):
        self.place, self.size, self.device = place, size, device

    def has(self, way):
        return self.place < self.size - 1 if way == 0 else self.place > 0

    def next(self, way):
        return self.device(self.place + (1 if way == 0 else -1))


def gather_sems(count, outer, inner):
    return count * outer * inner + 4


def scatter_sems(parts, outer, inner):
    total = 4
    for order, *_ in parts:
        first, second = (inner, outer) if order == 0 else (outer, inner)
        total += second * (first + 1) + second + 1
    return total


class Gather:
    def __init__(self, source, slots, sems, outer, inner, parts, seen):
        self.source, self.slots, self.sems = source, slots, sems
        self.outer, self.inner, self.seen = outer, inner, seen
        self.parts = [(number * outer.size * inner.size, *part) for number, part in enumerate(parts)]
        self.sent = len(parts) * outer.size * inner.size

    def slot(self, place_outer, place_inner):
        return place_outer * self.inner.size + place_inner

    def copy(self, part, slot, line, way, source=None):
        base, _, start, rows = part
        sent = self.sent + way + (0 if line is self.outer else 2)
        piece = self.slots.at[slot, pl.ds(start, rows)]
        return pltpu.make_async_remote_copy(
            src_ref=piece if source is None else source.at[pl.ds(start, rows)],
            dst_ref=piece,
            send_sem=self.sems.at[sent],
            recv_sem=self.sems.at[base + slot],
            device_id=line.next(way),
            device_id_type=MESH,
        )

    def send(self, part, slot, line, way, also=True, source=None):
        @pl.when(line.has(way) & also)
        def _():
            self.copy(part, slot, line, way, source).start()

    def arrive(self, part, slot):
        base, _, start, rows = part
        piece = self.slots.at[slot, pl.ds(start, rows)]
        pltpu.make_async_copy(piece, piece, self.sems.at[base + slot]).wait()

    def own(self, line, orders=(0, 1)):
        slot = self.slot(self.outer.place, self.inner.place)
        for part in self.parts:
            if part[1] in orders:
                for way in (0, 1):
                    self.send(part, slot, line, way, source=self.source)

    def cross_row(self):
        for part in self.parts:
            if part[1] == 1:
                for way in (0, 1):
                    for step in range(1, self.inner.size):
                        place = self.inner.place + (-step if way == 0 else step)

                        @pl.when((place >= 0) & (place < self.inner.size))
                        def _():
                            slot = self.slot(self.outer.place, place)
                            self.arrive(part, slot)
                            self.send(part, slot, self.inner, way)
                            self.send(part, slot, self.outer, 0)
                            self.send(part, slot, self.outer, 1)

    def each_side(self, distance, act):
        @pl.loop(0, 2)
        def _(side):
            row = self.outer.place + (2 * side - 1) * distance

            @pl.when((row >= 0) & (row < self.outer.size) & ((distance > 0) | (side == 0)))
            def _():
                act(side, row)

    def from_outer(self, distance):
        steps = [(part, 0) for part in self.parts]
        steps += [(part, turn) for turn in range(1, self.inner.size) for part in self.parts if part[1] == 1]
        for part, turn in steps:

            def pass_on(side, row):
                slot = self.slot(row, (self.inner.place + turn) % self.inner.size)
                self.arrive(part, slot)
                self.send(part, slot, self.outer, 0, side == 0)
                self.send(part, slot, self.outer, 1, side == 1)
                if part[1] == 0:
                    self.send(part, slot, self.inner, 0)
                    self.send(part, slot, self.inner, 1)

            self.each_side(distance, pass_on)
        self.each_side(distance, lambda side, row: self.seen(self.slot(row, self.inner.place)))

    def from_inner(self, distance):
        def each_place(side, row):
            @pl.loop(0, 2)
            def _(way):
                @pl.loop(1, self.inner.size)
                def _(step):
                    place = self.inner.place + (2 * way - 1) * step

                    @pl.when((place >= 0) & (place < self.inner.size))
                    def _():
                        slot = self.slot(row, place)
                        for part in self.parts:
                            if part[1] == 0:
                                self.arrive(part, slot)
                                self.send(part, slot, self.inner, 0, way == 0)
                                self.send(part, slot, self.inner, 1, way == 1)
                        self.seen(slot)

        self.each_side(distance, each_place)

    def finish(self):
        @pl.loop(0, self.outer.size)
        def _(row):
            @pl.loop(0, self.inner.size)
            def _(place):
                slot = self.slot(row, place)
                for part in self.parts:
                    for way in (0, 1):
                        passed = (row <= self.outer.place) if way == 0 else (row >= self.outer.place)
                        if part[1] == 0:
                            passed &= place == self.inner.place

                        @pl.when(self.outer.has(way) & passed)
                        def _():
                            self.copy(part, slot, self.outer, way).wait_send()

                        passed = (place <= self.inner.place) if way == 0 else (place >= self.inner.place)
                        if part[1] == 1:
                            passed &= row == self.outer.place

                        @pl.when(self.inner.has(way) & passed)
                        def _():
                            self.copy(part, slot, self.inner, way).wait_send()


class Reduce:
    def __init__(self, line, term, landed, sems, sent, base):
        self.line, self.term, self.landed, self.sems, self.sent, self.base = line, term, landed, sems, sent, base

    def landing(self, way, owner, place):
        index = self.base + owner
        return self.sems.at[index if way == 0 else jnp.where(owner == place, self.base + self.line.size, index)]

    def copy(self, way, owner):
        return pltpu.make_async_remote_copy(
            src_ref=self.term(owner),
            dst_ref=self.landed(way, owner),
            send_sem=self.sems.at[self.sent + way],
            recv_sem=self.landing(way, owner, self.line.place + (1 if way == 0 else -1)),
            device_id=self.line.next(way),
            device_id_type=MESH,
        )

    def arrive(self, way, owner, act):
        @pl.when(self.line.has(1 - way))
        def _():
            piece = self.landed(way, owner)
            pltpu.make_async_copy(piece, piece, self.landing(way, owner, self.line.place)).wait()
            act(piece[...].astype(WIDE))

    def add(self, way, owner):
        term = self.term(owner)

        def act(value):
            term[...] = (term[...].astype(WIDE) + value).astype(HALF)

        self.arrive(way, owner, act)

    def each(self, distance, act):
        for way in (0, 1):
            owner = self.line.place + (distance if way == 0 else -distance)
            pl.when((owner >= 0) & (owner < self.line.size))(lambda: act(way, owner))

    def step(self, distance):
        def act(way, owner):
            self.add(way, owner)
            self.copy(way, owner).start()

        self.each(distance, act)

    def finish(self):
        for distance in range(1, self.line.size):
            self.each(distance, lambda way, owner: self.copy(way, owner).wait_send())


class Scatter:
    def __init__(self, terms, landed, sems, outer, inner, parts):
        self.terms, self.landed, self.sems = terms, landed, sems
        self.outer, self.inner = outer, inner
        self.parts, base = [], 4
        for order, start, rows in parts:
            self.parts.append((base, order, start, rows))
            base += scatter_sems([(order,)], outer.size, inner.size) - 4

    def along_outer(self, part, place):
        base, order, start, rows = part
        span = pl.ds(start, rows)
        base += self.outer.size * (self.inner.size + 1) if order == 0 else place * (self.outer.size + 1)
        return Reduce(
            self.outer,
            lambda owner: self.terms.at[owner, place, span],
            lambda way, owner: self.landed.at[0, way, owner, place, span],
            self.sems,
            0,
            base,
        )

    def along_inner(self, part, row):
        base, order, start, rows = part
        span = pl.ds(start, rows)
        base += self.inner.size * (self.outer.size + 1) if order == 1 else row * (self.inner.size + 1)
        return Reduce(
            self.inner,
            lambda owner: self.terms.at[row, owner, span],
            lambda way, owner: self.landed.at[1, way, row, owner, span],
            self.sems,
            2,
            base,
        )

    def steps_inner(self, part, row):
        line = self.along_inner(part, row)
        for distance in range(self.inner.size - 1, 0, -1):
            line.step(distance)

    def start_row(self, row):
        for part in self.parts:
            if part[1] == 0:
                self.steps_inner(part, row)

    def outer_first(self, distance):
        for part in self.parts:
            if part[1] == 1:
                for place in range(self.inner.size):
                    self.along_outer(part, place).step(distance)

    def outer_second(self, distance):
        for part in self.parts:
            if part[1] == 0:

                def act(way, row):
                    for side in (0, 1):
                        self.along_inner(part, row).add(side, self.inner.place)

                self.along_outer(part, self.inner.place).each(distance, act)
                self.along_outer(part, self.inner.place).step(distance)

    def turn(self):
        for part in self.parts:
            if part[1] == 1:
                for place in range(self.inner.size):

                    @pl.when(place != self.inner.place)
                    def _():
                        for way in (0, 1):
                            self.along_outer(part, place).add(way, self.outer.place)

                self.steps_inner(part, self.outer.place)

    def total(self, out):
        row, place = self.outer.place, self.inner.place
        for part in self.parts:
            span = pl.ds(part[2], part[3])
            held = [self.terms[row, place, span].astype(WIDE)]
            out[span, :] = held[0].astype(out.dtype)

            def act(value):
                out[span, :] = (out[span, :].astype(WIDE) + value).astype(out.dtype)

            for way in (0, 1):
                self.along_outer(part, place).arrive(way, row, act)
                self.along_inner(part, row).arrive(way, place, act)

    def finish(self):
        for part in self.parts:
            if part[1] == 0:
                pl.loop(0, self.outer.size)(lambda row: self.along_inner(part, row).finish())
                self.along_outer(part, self.inner.place).finish()
            else:
                pl.loop(0, self.inner.size)(lambda place: self.along_outer(part, place).finish())
                self.along_inner(part, self.outer.place).finish()


def layer(
    sizes,
    tokens_in, wq_in, wk_in, wv_in, wo_in, cot_in, state_in,
    result, grad_tokens, grad_wq, grad_wk, grad_wv, grad_wo, grad_state,
    tok, cot, moved_tok, wq, wk, wv, wo, state,
    acc, grad_normed, mixed, query, keys, values, scores_t, prior,
    fore, rear, grads, normed,
    terms, terms_landed, inputs, inputs_landed, outers, outers_landed, total, total_wo,
    load_sem, fore_sem, rear_sem,
    tok_sem, tok_moved, tok_landed, cot_sem, grads_sem, terms_sem, inputs_sem, outers_sem,
):
    seq, head = sizes
    head_inner, seq_inner = inner_size(head), inner_size(seq)
    head_outer, seq_outer = head // head_inner, seq // seq_inner
    shared = head // seq
    rows, wide = tok.shape[1:]
    columns = wq.shape[1]
    heads_here = columns // DH
    s, h = lax.axis_index("seq"), lax.axis_index("head")
    z, y = h // head_inner, h % head_inner
    outer = Line(z, head_outer, lambda place: (s, place * head_inner + y))
    inner = Line(y, head_inner, lambda place: (s, z * head_inner + place))
    chip = Line(s // seq_inner, seq_outer, lambda place: (place * seq_inner + s % seq_inner, h))
    core = Line(s % seq_inner, seq_inner, lambda place: (s // seq_inner * seq_inner + place, h))

    loads = [
        pltpu.make_async_copy(source, target, load_sem.at[number])
        for number, (source, target) in enumerate(
            [
                (tokens_in, tok.at[h]),
                (wq_in, wq), (wk_in, wk), (wv_in, wv),
                (cot_in, cot.at[h]), (wo_in, wo), (state_in, state),
            ]
        )
    ]
    for load in loads:
        load.start()

    barrier = pltpu.get_barrier_semaphore()
    expected = seq - 1
    for line in (outer, inner):
        for way in (0, 1):
            expected = expected + line.has(way).astype(jnp.int32)

            @pl.when(line.has(way))
            def _():
                pl.semaphore_signal(barrier, inc=1, device_id=line.next(way), device_id_type=MESH)
    for other in range(1, seq):
        pl.semaphore_signal(barrier, inc=1, device_id=((s + other) % seq, h), device_id_type=MESH)
    pl.semaphore_wait(barrier, expected)

    def early(slot):
        distance = abs(slot // head_inner - z)
        at_end = (z == 0) | (z == head_outer - 1)
        direct = (slot % head_inner == y) & at_end
        return (distance < head_outer - 2) | ((distance == head_outer - 2) & direct)

    def moves(slots, moved, sent, landed):
        def copy(slot):
            return pltpu.make_async_remote_copy(
                src_ref=slots.at[slot],
                dst_ref=moved.at[s, slot % shared],
                send_sem=sent.at[0],
                recv_sem=landed.at[s, slot % shared],
                device_id=(slot // shared, h),
                device_id_type=MESH,
            )

        def start(slot):
            @pl.when(slot // shared != s)
            def _():
                copy(slot).start()

            @pl.when(slot // shared == s)
            def _():
                own = moved.at[s, slot % shared]
                pltpu.make_async_copy(slots.at[slot], own, landed.at[s, slot % shared]).start()

        def soon(slot):
            pl.when(early(slot))(lambda: start(slot))

        def late():
            @pl.loop(0, head)
            def _(slot):
                pl.when(jnp.logical_not(early(slot)))(lambda: start(slot))

        def finish():
            @pl.loop(0, head)
            def _(slot):
                @pl.when(slot // shared != s)
                def _():
                    copy(slot).wait_send()

        return soon, late, finish

    move_tok, move_tok_late, finish_tok = moves(tok, moved_tok, tok_moved, tok_landed)

    def project(slot):
        block = tok[slot]
        span = pl.ds(pl.multiple_of(slot * wide, wide), wide)
        for number, weight in enumerate((wq, wk, wv)):
            acc[number] += mul(block, weight[span, :])
        move_tok(slot)

    def pull(slot):
        span = pl.ds(pl.multiple_of(slot * wide, wide), wide)
        grad_normed[...] += mul(cot[slot], wo[:, span], NT)

    def each_row(distance, act):
        @pl.loop(0, 2)
        def _(side):
            place = z + (2 * side - 1) * distance
            pl.when((place >= 0) & (place < head_outer) & ((distance > 0) | (side == 0)))(lambda: act(place))

    tok_gather = Gather(tokens_in, tok, tok_sem, outer, inner, gather_parts(rows), project)
    cot_gather = Gather(cot_in, cot, cot_sem, outer, inner, cot_parts(rows), pull)
    nothing = lambda slot: None
    grads_gather = Gather(grads.at[s], grads, grads_sem, chip, core, ((0, 0, rows),), nothing)

    tok_gather.own(inner, (1,))
    tok_gather.own(outer)
    tok_gather.own(inner, (0,))
    acc[...] = jnp.zeros_like(acc)
    grad_normed[...] = jnp.zeros_like(grad_normed)
    for load in loads[:4]:
        load.wait()
    project(h)
    tok_gather.cross_row()

    @pl.loop(1, head_outer)
    def _(distance):
        tok_gather.from_outer(distance)

        @pl.when(distance == head_outer - 2)
        def _():
            cot_gather.own(outer)
            cot_gather.own(inner, (1,))

        tok_gather.from_inner(distance - 1)

    cot_gather.own(inner, (0,))
    cot_gather.cross_row()
    tok_gather.from_inner(head_outer - 1)

    for number, target in enumerate((query, keys, values)):
        target[...] = acc[number].astype(HALF)

    def part(ref, number):
        return ref[:, number * DH : (number + 1) * DH]

    for number in range(heads_here):
        fore[s, number] = mul(part(keys, number), part(values, number), TN).astype(HALF)

    def share(states, sems, wanted):
        def copy(other):
            return pltpu.make_async_remote_copy(
                src_ref=states.at[s],
                dst_ref=states.at[s],
                send_sem=sems.at[seq],
                recv_sem=sems.at[s],
                device_id=(other, h),
                device_id_type=MESH,
            )

        def start():
            for other in range(seq):
                pl.when((other != s) & wanted(s, other))(lambda: copy(other).start())

        def arrive():
            for other in range(seq):

                @pl.when((other != s) & wanted(other, s))
                def _():
                    pltpu.make_async_copy(states.at[other], states.at[other], sems.at[other]).wait()

        def finish():
            for other in range(seq):
                pl.when((other != s) & wanted(s, other))(lambda: copy(other).wait_send())

        return start, arrive, finish

    start_fore, arrive_fore, finish_fore = share(fore, fore_sem, lambda source, target: source < target)
    start_rear, arrive_rear, finish_rear = share(rear, rear_sem, lambda source, target: target >= 0)
    start_fore()
    for load in loads[4:]:
        load.wait()
    move_tok_late()
    pull(h)
    at_end = (z == 0) | (z == head_outer - 1)
    pl.when(jnp.logical_not(at_end))(lambda: cot_gather.from_outer(1))

    below = lax.broadcasted_iota(jnp.int32, (rows, rows), 1) <= lax.broadcasted_iota(jnp.int32, (rows, rows), 0)
    above = lax.broadcasted_iota(jnp.int32, (rows, rows), 1) >= lax.broadcasted_iota(jnp.int32, (rows, rows), 0)
    for number in range(heads_here):
        query_h, keys_h = part(query, number), part(keys, number)
        scores = jnp.where(below, mul(query_h, keys_h, NT), 0.0).astype(HALF)
        scores_t[number] = jnp.where(above, mul(keys_h, query_h, NT), 0.0).astype(HALF)
        mixed[:, number * DH : (number + 1) * DH] = mul(scores, part(values, number))
    arrive_fore()
    for number in range(heads_here):
        before = state[number]
        for other in range(seq):
            before = before + jnp.where(other < s, fore[other, number].astype(WIDE), 0.0)
        prior[number] = before.astype(HALF)
        whole = part(mixed, number) + mul(part(query, number), prior[number])
        mixed[:, number * DH : (number + 1) * DH] = whole
        inv_norm = lax.rsqrt(jnp.mean(whole * whole, axis=-1, keepdims=True) + EPSILON)
        normed[:, number * DH : (number + 1) * DH] = (whole * inv_norm).astype(HALF)

    result_sums = Scatter(terms, terms_landed, terms_sem, outer, inner, result_parts(rows))

    def result_terms(row):
        @pl.loop(0, head_inner)
        def _(place):
            span = pl.ds(pl.multiple_of((row * head_inner + place) * wide, wide), wide)
            terms[row, place] = mul(normed[...], wo[:, span]).astype(HALF)

    each_row(head_outer - 1, result_terms)
    result_sums.outer_first(head_outer - 1)

    for distance in range(head_outer - 2, 0, -1):
        each_row(distance, result_terms)
        pl.when(at_end)(lambda: result_sums.outer_first(distance))
    each_row(0, result_terms)
    pl.when(at_end)(lambda: cot_gather.from_outer(1))
    cot_gather.from_inner(0)
    for distance in range(2, head_outer):
        cot_gather.from_outer(distance)
        if distance < head_outer - 1:
            cot_gather.from_inner(distance - 1)
            pl.when(jnp.logical_not(at_end))(lambda: result_sums.outer_first(head_outer - distance))

    @pl.loop(0, head_outer)
    def _(turn):
        each_row(head_outer - 1 - turn, result_sums.start_row)

    cot_gather.from_inner(head_outer - 2)
    cot_gather.from_inner(head_outer - 1)

    for number in range(heads_here):
        whole, pulled = part(mixed, number), part(grad_normed, number)
        inv_norm = lax.rsqrt(jnp.mean(whole * whole, axis=-1, keepdims=True) + EPSILON)
        slope = jnp.mean(pulled * whole, axis=-1, keepdims=True)
        grad_mixed = (inv_norm * (pulled - whole * inv_norm * inv_norm * slope)).astype(HALF)
        grads[s, :, number * DH : (number + 1) * DH] = grad_mixed
        rear[s, number] = mul(part(query, number), grad_mixed, TN).astype(HALF)
    start_rear()

    outer_grads = Scatter(outers, outers_landed, outers_sem, chip, core, ((0, 0, shared * columns),))

    @pl.loop(0, head)
    def _(slot):
        owner = slot // shared
        span = pl.ds(pl.multiple_of(slot % shared * columns, columns), columns)
        share_wo = mul(normed[...], cot[slot], TN).astype(HALF)
        outers[owner // seq_inner, owner % seq_inner, span] = share_wo

    pl.loop(0, seq_outer)(outer_grads.start_row)
    for number in range(heads_here):
        span = slice(number * DH, (number + 1) * DH)
        grad_mixed = grads[s, :, span]
        query_h, keys_h, values_h = part(query, number), part(keys, number), part(values, number)
        grad_scores = jnp.where(below, mul(grad_mixed, values_h, NT), 0.0).astype(HALF)
        grad_scores_t = jnp.where(above, mul(values_h, grad_mixed, NT), 0.0).astype(HALF)
        acc[0, :, span] = mul(grad_scores, keys_h) + mul(grad_mixed, prior[number], NT)
        acc[1, :, span] = mul(grad_scores_t, query_h)
        acc[2, :, span] = mul(scores_t[number], grad_mixed)
    if head_outer > 2:
        pl.when(jnp.logical_not(at_end))(lambda: result_sums.outer_first(1))
    result_sums.outer_second(head_outer - 1)
    tok_gather.finish()
    finish_tok()
    finish_fore()
    arrive_rear()
    for number in range(heads_here):
        later = jnp.zeros((DH, DH), WIDE)
        every = jnp.zeros((DH, DH), WIDE)
        for other in range(seq):
            one = rear[other, number].astype(WIDE)
            later = later + jnp.where(other > s, one, 0.0)
            every = every + one
        grad_state[number] = every
        later = later.astype(HALF)
        span = slice(number * DH, (number + 1) * DH)
        acc[1, :, span] += mul(part(values, number), later, NT)
        acc[2, :, span] += mul(part(keys, number), later)
    for number in range(3):
        grads[s, :, number * columns : (number + 1) * columns] = acc[number].astype(HALF)

    input_sums = Scatter(inputs, inputs_landed, inputs_sem, outer, inner, input_parts(rows))

    def input_terms(place):
        @pl.loop(0, head_inner)
        def _(turn):
            owner = (y + 1 + turn) % head_inner
            span = pl.ds(pl.multiple_of((place * head_inner + owner) * wide, wide), wide)
            term = mul(grads[s, :, :columns], wq[span, :], NT)
            term += mul(grads[s, :, columns : 2 * columns], wk[span, :], NT)
            term += mul(grads[s, :, 2 * columns :], wv[span, :], NT)
            inputs[place, owner] = term.astype(HALF)

            @pl.when(turn == head_inner - 2)
            def _():
                input_sums.start_row(place)

    each_row(head_outer - 1, input_terms)
    input_sums.outer_first(head_outer - 1)
    grads_gather.own(chip)
    grads_gather.own(core)

    for distance in range(head_outer - 2, 0, -1):
        each_row(distance, input_terms)
        pl.when(at_end)(lambda: input_sums.outer_first(distance))
    each_row(0, input_terms)

    def weight_grads(place):
        for number in range(shared):
            piece = moved_tok.at[place, number]
            span = slice(number * wide, (number + 1) * wide)
            pltpu.make_async_copy(piece, piece, tok_landed.at[place, number]).wait()
            for target, start in ((grad_wq, 0), (grad_wk, columns), (grad_wv, 2 * columns)):
                target[span, :] += mul(piece[...], grads[place, :, start : start + columns], TN)

    for target in (grad_wq, grad_wk, grad_wv):
        target[...] = jnp.zeros_like(target)
    for distance in range(seq_outer - 1, 0, -1):
        outer_grads.outer_second(distance)
    for distance in range(head_outer - 2, 1, -1):
        result_sums.outer_second(distance)
    weight_grads(s)
    grads_gather.from_inner(0)

    @pl.loop(1, seq_inner)
    def _(step):
        weight_grads(chip.place * seq_inner + (core.place + step) % seq_inner)

    input_sums.outer_second(head_outer - 1)
    if head_outer > 2:
        result_sums.outer_second(1)
    for distance in range(head_outer - 2, 0, -1):
        pl.when(jnp.logical_not(at_end))(lambda: input_sums.outer_first(distance))
    for distance in range(head_outer - 2, 0, -1):
        input_sums.outer_second(distance)
        if distance == head_outer - 2:
            grads_gather.from_outer(1)
    for distance in range(2, seq_outer):
        grads_gather.from_outer(distance)
        grads_gather.from_inner(distance - 1)
    result_sums.turn()
    input_sums.turn()
    grads_gather.from_inner(seq_outer - 1)

    @pl.loop(seq_inner, seq)
    def _(step):
        place = (chip.place + step // seq_inner) % seq_outer
        weight_grads(place * seq_inner + step % seq_inner)

    outer_grads.total(total_wo)
    for number in range(shared):
        grad_wo[:, number * wide : (number + 1) * wide] = total_wo[number * columns : (number + 1) * columns, :]
    result_sums.total(total)
    result[...] = total[...].astype(HALF)
    cot_gather.finish()
    finish_rear()
    outer_grads.finish()
    input_sums.total(grad_tokens)
    for one in (grads_gather, result_sums, input_sums):
        one.finish()


def write_out(*refs):
    count = (len(refs) - 1) // 2
    copies = [pltpu.make_async_copy(refs[k], refs[count + k], refs[-1].at[k]) for k in range(count)]
    for copy in copies:
        copy.start()
    for copy in copies:
        copy.wait()


def solution(mesh):
    seq, head = mesh.shape["seq"], mesh.shape["head"]

    def on_device(tokens, w_query, w_key, w_value, w_out, grad_out, state_in):
        rows, wide = tokens.shape
        depth, columns = w_query.shape
        heads_here = columns // DH
        shared = head // seq
        assert rows == BLOCK and head % seq == 0
        head_inner, seq_inner = inner_size(head), inner_size(seq)
        head_outer, seq_outer = head // head_inner, seq // seq_inner
        vmem = lambda *shape: pltpu.VMEM(shape, HALF)
        full = lambda *shape: pltpu.VMEM(shape, WIDE)
        dma = lambda *shape: pltpu.SemaphoreType.DMA(shape)
        gathers = lambda parts: dma(gather_sems(len(parts(rows)), head_outer, head_inner))
        sums = lambda parts: dma(scatter_sems(parts, head_outer, head_inner))
        outs = [
            ((rows, wide), HALF), ((rows, wide), WIDE),
            ((shared * wide, columns), WIDE), ((shared * wide, columns), WIDE), ((shared * wide, columns), WIDE),
            ((columns, shared * wide), WIDE), ((heads_here, DH, DH), WIDE),
        ]
        done = pl.pallas_call(
            lambda *refs: layer((seq, head), *refs),
            out_shape=[pltpu.VMEM(shape, kind) for shape, kind in outs],
            in_specs=[pl.BlockSpec(memory_space=pltpu.HBM)] * 7,
            out_specs=[pl.BlockSpec(memory_space=pltpu.VMEM)] * 7,
            scratch_shapes=[
                vmem(head, rows, wide), vmem(head, rows, wide),
                vmem(seq, shared, rows, wide),
                vmem(depth, columns), vmem(depth, columns), vmem(depth, columns), vmem(columns, depth),
                full(heads_here, DH, DH),
                full(3, rows, columns), full(rows, columns), full(rows, columns),
                vmem(rows, columns), vmem(rows, columns), vmem(rows, columns),
                vmem(heads_here, rows, rows), vmem(heads_here, DH, DH),
                vmem(seq, heads_here, DH, DH), vmem(seq, heads_here, DH, DH),
                vmem(seq, rows, 3 * columns), vmem(rows, columns),
                vmem(head_outer, head_inner, rows, wide), vmem(2, 2, head_outer, head_inner, rows, wide),
                vmem(head_outer, head_inner, rows, wide), vmem(2, 2, head_outer, head_inner, rows, wide),
                vmem(seq_outer, seq_inner, shared * columns, wide),
                vmem(2, 2, seq_outer, seq_inner, shared * columns, wide),
                full(rows, wide), full(shared * columns, wide),
                dma(7), dma(seq + 1), dma(seq + 1),
                gathers(gather_parts), dma(1), dma(seq, shared), gathers(cot_parts), dma(gather_sems(1, seq_outer, seq_inner)),
                sums(result_parts(rows)), sums(input_parts(rows)), dma(scatter_sems([(0,)], seq_outer, seq_inner)),
            ],
            compiler_params=pltpu.CompilerParams(
                collective_id=0, has_side_effects=True, vmem_limit_bytes=54 * 1024 * 1024
            ),
        )(tokens, w_query, w_key, w_value, w_out, grad_out, state_in)
        return pl.pallas_call(
            write_out,
            out_shape=[jax.ShapeDtypeStruct(shape, kind) for shape, kind in outs],
            in_specs=[pl.BlockSpec(memory_space=pl.ANY)] * 7,
            out_specs=[pl.BlockSpec(memory_space=pltpu.HBM)] * 7,
            scratch_shapes=[dma(7)],
            compiler_params=pltpu.CompilerParams(vmem_limit_bytes=1024 * 1024),
        )(*done)

    by_head = P(None, "head")
    tiled = P("seq", "head")
    return jax.shard_map(
        on_device,
        mesh=mesh,
        in_specs=(tiled, by_head, by_head, by_head, P("head", None), tiled, P("head", None, None)),
        out_specs=(tiled, tiled, tiled, tiled, tiled, P("head", "seq"), P("head", None, None)),
        check_vma=False,
    )
```

```python
import jax
import jax.numpy as jnp
from jax import lax
from jax.experimental import pallas as pl
from jax.experimental.pallas import tpu as pltpu
from jax.sharding import PartitionSpec as P

DH = 128
BLOCK = 256
EPSILON = 1e-06
WIDE = jnp.float32
HALF = jnp.bfloat16
MESH = pl.DeviceIdType.MESH
NN = (((1,), (0,)), ((), ()))
NT = (((1,), (1,)), ((), ()))
TN = (((0,), (0,)), ((), ()))


def mul(left, right, dims=NN):
    return lax.dot_general(left, right, dims, preferred_element_type=WIDE)


def parts(rows, shares):
    unit, start, cut = rows // 16, 0, []
    for order, share in shares:
        cut.append((order, start, share * unit))
        start += share * unit
    return cut


def gather_parts(rows):
    return parts(rows, ((0, 7), (0, 6), (1, 3)))


def cot_parts(rows):
    return parts(rows, ((0, 6), (0, 5), (1, 5)))


def result_parts(rows):
    return parts(rows, ((1, 10), (0, 6)))


def input_parts(rows):
    return parts(rows, ((0, 7), (0, 7), (1, 2)))


def inner_size(count):
    inner = 1
    while 4 * inner * inner <= count:
        inner *= 2
    return inner


class Line:
    def __init__(self, place, size, device):
        self.place, self.size, self.device = place, size, device

    def has(self, way):
        return self.place < self.size - 1 if way == 0 else self.place > 0

    def next(self, way):
        return self.device(self.place + (1 if way == 0 else -1))


def gather_sems(count, outer, inner):
    return count * outer * inner + 4


def scatter_sems(parts, outer, inner):
    total = 4
    for order, *_ in parts:
        first, second = (inner, outer) if order == 0 else (outer, inner)
        total += second * (first + 1) + second + 1
    return total


class Gather:
    def __init__(self, source, slots, sems, outer, inner, parts, seen):
        self.source, self.slots, self.sems = source, slots, sems
        self.outer, self.inner, self.seen = outer, inner, seen
        self.parts = [(number * outer.size * inner.size, *part) for number, part in enumerate(parts)]
        self.sent = len(parts) * outer.size * inner.size

    def slot(self, place_outer, place_inner):
        return place_outer * self.inner.size + place_inner

    def copy(self, part, slot, line, way, source=None):
        base, _, start, rows = part
        sent = self.sent + way + (0 if line is self.outer else 2)
        piece = self.slots.at[slot, pl.ds(start, rows)]
        return pltpu.make_async_remote_copy(
            src_ref=piece if source is None else source.at[pl.ds(start, rows)],
            dst_ref=piece,
            send_sem=self.sems.at[sent],
            recv_sem=self.sems.at[base + slot],
            device_id=line.next(way),
            device_id_type=MESH,
        )

    def send(self, part, slot, line, way, also=True, source=None):
        @pl.when(line.has(way) & also)
        def _():
            self.copy(part, slot, line, way, source).start()

    def arrive(self, part, slot):
        base, _, start, rows = part
        piece = self.slots.at[slot, pl.ds(start, rows)]
        pltpu.make_async_copy(piece, piece, self.sems.at[base + slot]).wait()

    def own(self, line, orders=(0, 1)):
        slot = self.slot(self.outer.place, self.inner.place)
        for part in self.parts:
            if part[1] in orders:
                for way in (0, 1):
                    self.send(part, slot, line, way, source=self.source)

    def cross_row(self):
        for part in self.parts:
            if part[1] == 1:
                for way in (0, 1):
                    for step in range(1, self.inner.size):
                        place = self.inner.place + (-step if way == 0 else step)

                        @pl.when((place >= 0) & (place < self.inner.size))
                        def _():
                            slot = self.slot(self.outer.place, place)
                            self.arrive(part, slot)
                            self.send(part, slot, self.inner, way)
                            self.send(part, slot, self.outer, 0)
                            self.send(part, slot, self.outer, 1)

    def each_side(self, distance, act):
        @pl.loop(0, 2)
        def _(side):
            row = self.outer.place + (2 * side - 1) * distance

            @pl.when((row >= 0) & (row < self.outer.size) & ((distance > 0) | (side == 0)))
            def _():
                act(side, row)

    def from_outer(self, distance):
        steps = [(part, 0) for part in self.parts]
        steps += [(part, turn) for turn in range(1, self.inner.size) for part in self.parts if part[1] == 1]
        for part, turn in steps:

            def pass_on(side, row):
                slot = self.slot(row, (self.inner.place + turn) % self.inner.size)
                self.arrive(part, slot)
                self.send(part, slot, self.outer, 0, side == 0)
                self.send(part, slot, self.outer, 1, side == 1)
                if part[1] == 0:
                    self.send(part, slot, self.inner, 0)
                    self.send(part, slot, self.inner, 1)

            self.each_side(distance, pass_on)
        self.each_side(distance, lambda side, row: self.seen(self.slot(row, self.inner.place)))

    def from_inner(self, distance):
        def each_place(side, row):
            @pl.loop(0, 2)
            def _(way):
                @pl.loop(1, self.inner.size)
                def _(step):
                    place = self.inner.place + (2 * way - 1) * step

                    @pl.when((place >= 0) & (place < self.inner.size))
                    def _():
                        slot = self.slot(row, place)
                        for part in self.parts:
                            if part[1] == 0:
                                self.arrive(part, slot)
                                self.send(part, slot, self.inner, 0, way == 0)
                                self.send(part, slot, self.inner, 1, way == 1)
                        self.seen(slot)

        self.each_side(distance, each_place)

    def finish(self):
        @pl.loop(0, self.outer.size)
        def _(row):
            @pl.loop(0, self.inner.size)
            def _(place):
                slot = self.slot(row, place)
                for part in self.parts:
                    for way in (0, 1):
                        passed = (row <= self.outer.place) if way == 0 else (row >= self.outer.place)
                        if part[1] == 0:
                            passed &= place == self.inner.place

                        @pl.when(self.outer.has(way) & passed)
                        def _():
                            self.copy(part, slot, self.outer, way).wait_send()

                        passed = (place <= self.inner.place) if way == 0 else (place >= self.inner.place)
                        if part[1] == 1:
                            passed &= row == self.outer.place

                        @pl.when(self.inner.has(way) & passed)
                        def _():
                            self.copy(part, slot, self.inner, way).wait_send()


class Reduce:
    def __init__(self, line, term, landed, sems, sent, base):
        self.line, self.term, self.landed, self.sems, self.sent, self.base = line, term, landed, sems, sent, base

    def landing(self, way, owner, place):
        index = self.base + owner
        return self.sems.at[index if way == 0 else jnp.where(owner == place, self.base + self.line.size, index)]

    def copy(self, way, owner):
        return pltpu.make_async_remote_copy(
            src_ref=self.term(owner),
            dst_ref=self.landed(way, owner),
            send_sem=self.sems.at[self.sent + way],
            recv_sem=self.landing(way, owner, self.line.place + (1 if way == 0 else -1)),
            device_id=self.line.next(way),
            device_id_type=MESH,
        )

    def arrive(self, way, owner, act):
        @pl.when(self.line.has(1 - way))
        def _():
            piece = self.landed(way, owner)
            pltpu.make_async_copy(piece, piece, self.landing(way, owner, self.line.place)).wait()
            act(piece[...].astype(WIDE))

    def add(self, way, owner):
        term = self.term(owner)

        def act(value):
            term[...] = (term[...].astype(WIDE) + value).astype(HALF)

        self.arrive(way, owner, act)

    def each(self, distance, act):
        for way in (0, 1):
            owner = self.line.place + (distance if way == 0 else -distance)
            pl.when((owner >= 0) & (owner < self.line.size))(lambda: act(way, owner))

    def step(self, distance):
        def act(way, owner):
            self.add(way, owner)
            self.copy(way, owner).start()

        self.each(distance, act)

    def finish(self):
        for distance in range(1, self.line.size):
            self.each(distance, lambda way, owner: self.copy(way, owner).wait_send())


class Scatter:
    def __init__(self, terms, landed, sems, outer, inner, parts):
        self.terms, self.landed, self.sems = terms, landed, sems
        self.outer, self.inner = outer, inner
        self.parts, base = [], 4
        for order, start, rows in parts:
            self.parts.append((base, order, start, rows))
            base += scatter_sems([(order,)], outer.size, inner.size) - 4

    def along_outer(self, part, place):
        base, order, start, rows = part
        span = pl.ds(start, rows)
        base += self.outer.size * (self.inner.size + 1) if order == 0 else place * (self.outer.size + 1)
        return Reduce(
            self.outer,
            lambda owner: self.terms.at[owner, place, span],
            lambda way, owner: self.landed.at[0, way, owner, place, span],
            self.sems,
            0,
            base,
        )

    def along_inner(self, part, row):
        base, order, start, rows = part
        span = pl.ds(start, rows)
        base += self.inner.size * (self.outer.size + 1) if order == 1 else row * (self.inner.size + 1)
        return Reduce(
            self.inner,
            lambda owner: self.terms.at[row, owner, span],
            lambda way, owner: self.landed.at[1, way, row, owner, span],
            self.sems,
            2,
            base,
        )

    def steps_inner(self, part, row):
        line = self.along_inner(part, row)
        for distance in range(self.inner.size - 1, 0, -1):
            line.step(distance)

    def start_row(self, row):
        for part in self.parts:
            if part[1] == 0:
                self.steps_inner(part, row)

    def outer_first(self, distance):
        for part in self.parts:
            if part[1] == 1:
                for place in range(self.inner.size):
                    self.along_outer(part, place).step(distance)

    def outer_second(self, distance):
        for part in self.parts:
            if part[1] == 0:

                def act(way, row):
                    for side in (0, 1):
                        self.along_inner(part, row).add(side, self.inner.place)

                self.along_outer(part, self.inner.place).each(distance, act)
                self.along_outer(part, self.inner.place).step(distance)

    def turn(self):
        for part in self.parts:
            if part[1] == 1:
                for place in range(self.inner.size):

                    @pl.when(place != self.inner.place)
                    def _():
                        for way in (0, 1):
                            self.along_outer(part, place).add(way, self.outer.place)

                self.steps_inner(part, self.outer.place)

    def total(self, out):
        row, place = self.outer.place, self.inner.place
        for part in self.parts:
            span = pl.ds(part[2], part[3])
            held = [self.terms[row, place, span].astype(WIDE)]
            out[span, :] = held[0].astype(out.dtype)

            def act(value):
                out[span, :] = (out[span, :].astype(WIDE) + value).astype(out.dtype)

            for way in (0, 1):
                self.along_outer(part, place).arrive(way, row, act)
                self.along_inner(part, row).arrive(way, place, act)

    def finish(self):
        for part in self.parts:
            if part[1] == 0:
                pl.loop(0, self.outer.size)(lambda row: self.along_inner(part, row).finish())
                self.along_outer(part, self.inner.place).finish()
            else:
                pl.loop(0, self.inner.size)(lambda place: self.along_outer(part, place).finish())
                self.along_inner(part, self.outer.place).finish()


def layer(
    sizes,
    tokens_in, wq_in, wk_in, wv_in, wo_in, cot_in, state_in,
    result, grad_tokens, grad_wq, grad_wk, grad_wv, grad_wo, grad_state,
    tok, cot, moved_tok, wq, wk, wv, wo, state,
    acc, grad_normed, mixed, query, keys, values, scores_t, prior,
    fore, rear, grads, normed,
    terms, terms_landed, inputs, inputs_landed, outers, outers_landed, total, total_wo,
    load_sem, fore_sem, rear_sem,
    tok_sem, tok_moved, tok_landed, cot_sem, grads_sem, terms_sem, inputs_sem, outers_sem,
):
    seq, head = sizes
    head_inner, seq_inner = inner_size(head), inner_size(seq)
    head_outer, seq_outer = head // head_inner, seq // seq_inner
    shared = head // seq
    rows, wide = tok.shape[1:]
    columns = wq.shape[1]
    heads_here = columns // DH
    s, h = lax.axis_index("seq"), lax.axis_index("head")
    z, y = h // head_inner, h % head_inner
    outer = Line(z, head_outer, lambda place: (s, place * head_inner + y))
    inner = Line(y, head_inner, lambda place: (s, z * head_inner + place))
    chip = Line(s // seq_inner, seq_outer, lambda place: (place * seq_inner + s % seq_inner, h))
    core = Line(s % seq_inner, seq_inner, lambda place: (s // seq_inner * seq_inner + place, h))

    loads = [
        pltpu.make_async_copy(source, target, load_sem.at[number])
        for number, (source, target) in enumerate(
            [
                (tokens_in, tok.at[h]),
                (wq_in, wq), (wk_in, wk), (wv_in, wv),
                (cot_in, cot.at[h]), (wo_in, wo), (state_in, state),
            ]
        )
    ]
    for load in loads:
        load.start()

    barrier = pltpu.get_barrier_semaphore()
    expected = seq - 1
    for line in (outer, inner):
        for way in (0, 1):
            expected = expected + line.has(way).astype(jnp.int32)

            @pl.when(line.has(way))
            def _():
                pl.semaphore_signal(barrier, inc=1, device_id=line.next(way), device_id_type=MESH)
    for other in range(1, seq):
        pl.semaphore_signal(barrier, inc=1, device_id=((s + other) % seq, h), device_id_type=MESH)
    pl.semaphore_wait(barrier, expected)

    def early(slot):
        distance = abs(slot // head_inner - z)
        at_end = (z == 0) | (z == head_outer - 1)
        direct = (slot % head_inner == y) & at_end
        return (distance < head_outer - 2) | ((distance == head_outer - 2) & direct)

    def moves(slots, moved, sent, landed):
        def copy(slot):
            return pltpu.make_async_remote_copy(
                src_ref=slots.at[slot],
                dst_ref=moved.at[s, slot % shared],
                send_sem=sent.at[0],
                recv_sem=landed.at[s, slot % shared],
                device_id=(slot // shared, h),
                device_id_type=MESH,
            )

        def start(slot):
            @pl.when(slot // shared != s)
            def _():
                copy(slot).start()

            @pl.when(slot // shared == s)
            def _():
                own = moved.at[s, slot % shared]
                pltpu.make_async_copy(slots.at[slot], own, landed.at[s, slot % shared]).start()

        def soon(slot):
            pl.when(early(slot))(lambda: start(slot))

        def late():
            @pl.loop(0, head)
            def _(slot):
                pl.when(jnp.logical_not(early(slot)))(lambda: start(slot))

        def finish():
            @pl.loop(0, head)
            def _(slot):
                @pl.when(slot // shared != s)
                def _():
                    copy(slot).wait_send()

        return soon, late, finish

    move_tok, move_tok_late, finish_tok = moves(tok, moved_tok, tok_moved, tok_landed)

    def project(slot):
        block = tok[slot]
        span = pl.ds(pl.multiple_of(slot * wide, wide), wide)
        for number, weight in enumerate((wq, wk, wv)):
            acc[number] += mul(block, weight[span, :])
        move_tok(slot)

    def pull(slot):
        span = pl.ds(pl.multiple_of(slot * wide, wide), wide)
        grad_normed[...] += mul(cot[slot], wo[:, span], NT)

    def each_row(distance, act):
        @pl.loop(0, 2)
        def _(side):
            place = z + (2 * side - 1) * distance
            pl.when((place >= 0) & (place < head_outer) & ((distance > 0) | (side == 0)))(lambda: act(place))

    tok_gather = Gather(tokens_in, tok, tok_sem, outer, inner, gather_parts(rows), project)
    cot_gather = Gather(cot_in, cot, cot_sem, outer, inner, cot_parts(rows), pull)
    nothing = lambda slot: None
    grads_gather = Gather(grads.at[s], grads, grads_sem, chip, core, ((0, 0, rows),), nothing)

    tok_gather.own(inner, (1,))
    tok_gather.own(outer)
    tok_gather.own(inner, (0,))
    acc[...] = jnp.zeros_like(acc)
    grad_normed[...] = jnp.zeros_like(grad_normed)
    for load in loads[:4]:
        load.wait()
    project(h)
    tok_gather.cross_row()

    @pl.loop(1, head_outer)
    def _(distance):
        tok_gather.from_outer(distance)

        @pl.when(distance == head_outer - 2)
        def _():
            cot_gather.own(outer)
            cot_gather.own(inner, (1,))

        tok_gather.from_inner(distance - 1)

    cot_gather.own(inner, (0,))
    cot_gather.cross_row()
    tok_gather.from_inner(head_outer - 1)

    for number, target in enumerate((query, keys, values)):
        target[...] = acc[number].astype(HALF)

    def part(ref, number):
        return ref[:, number * DH : (number + 1) * DH]

    for number in range(heads_here):
        fore[s, number] = mul(part(keys, number), part(values, number), TN).astype(HALF)

    def share(states, sems, wanted):
        def copy(other):
            return pltpu.make_async_remote_copy(
                src_ref=states.at[s],
                dst_ref=states.at[s],
                send_sem=sems.at[seq],
                recv_sem=sems.at[s],
                device_id=(other, h),
                device_id_type=MESH,
            )

        def start():
            for other in range(seq):
                pl.when((other != s) & wanted(s, other))(lambda: copy(other).start())

        def arrive():
            for other in range(seq):

                @pl.when((other != s) & wanted(other, s))
                def _():
                    pltpu.make_async_copy(states.at[other], states.at[other], sems.at[other]).wait()

        def finish():
            for other in range(seq):
                pl.when((other != s) & wanted(s, other))(lambda: copy(other).wait_send())

        return start, arrive, finish

    start_fore, arrive_fore, finish_fore = share(fore, fore_sem, lambda source, target: source < target)
    start_rear, arrive_rear, finish_rear = share(rear, rear_sem, lambda source, target: target >= 0)
    start_fore()
    for load in loads[4:]:
        load.wait()
    move_tok_late()
    pull(h)
    at_end = (z == 0) | (z == head_outer - 1)
    pl.when(jnp.logical_not(at_end))(lambda: cot_gather.from_outer(1))

    below = lax.broadcasted_iota(jnp.int32, (rows, rows), 1) <= lax.broadcasted_iota(jnp.int32, (rows, rows), 0)
    above = lax.broadcasted_iota(jnp.int32, (rows, rows), 1) >= lax.broadcasted_iota(jnp.int32, (rows, rows), 0)
    for number in range(heads_here):
        query_h, keys_h = part(query, number), part(keys, number)
        scores = jnp.where(below, mul(query_h, keys_h, NT), 0.0).astype(HALF)
        scores_t[number] = jnp.where(above, mul(keys_h, query_h, NT), 0.0).astype(HALF)
        mixed[:, number * DH : (number + 1) * DH] = mul(scores, part(values, number))
    arrive_fore()
    for number in range(heads_here):
        before = state[number]
        for other in range(seq):
            before = before + jnp.where(other < s, fore[other, number].astype(WIDE), 0.0)
        prior[number] = before.astype(HALF)
        whole = part(mixed, number) + mul(part(query, number), prior[number])
        mixed[:, number * DH : (number + 1) * DH] = whole
        inv_norm = lax.rsqrt(jnp.mean(whole * whole, axis=-1, keepdims=True) + EPSILON)
        normed[:, number * DH : (number + 1) * DH] = (whole * inv_norm).astype(HALF)

    result_sums = Scatter(terms, terms_landed, terms_sem, outer, inner, result_parts(rows))

    def result_terms(row):
        @pl.loop(0, head_inner)
        def _(place):
            span = pl.ds(pl.multiple_of((row * head_inner + place) * wide, wide), wide)
            terms[row, place] = mul(normed[...], wo[:, span]).astype(HALF)

    each_row(head_outer - 1, result_terms)
    result_sums.outer_first(head_outer - 1)

    for distance in range(head_outer - 2, 0, -1):
        each_row(distance, result_terms)
        pl.when(at_end)(lambda: result_sums.outer_first(distance))
    each_row(0, result_terms)
    pl.when(at_end)(lambda: cot_gather.from_outer(1))
    cot_gather.from_inner(0)
    for distance in range(2, head_outer):
        cot_gather.from_outer(distance)
        if distance < head_outer - 1:
            cot_gather.from_inner(distance - 1)
            pl.when(jnp.logical_not(at_end))(lambda: result_sums.outer_first(head_outer - distance))

    @pl.loop(0, head_outer)
    def _(turn):
        each_row(head_outer - 1 - turn, result_sums.start_row)

    cot_gather.from_inner(head_outer - 2)
    cot_gather.from_inner(head_outer - 1)

    for number in range(heads_here):
        whole, pulled = part(mixed, number), part(grad_normed, number)
        inv_norm = lax.rsqrt(jnp.mean(whole * whole, axis=-1, keepdims=True) + EPSILON)
        slope = jnp.mean(pulled * whole, axis=-1, keepdims=True)
        grad_mixed = (inv_norm * (pulled - whole * inv_norm * inv_norm * slope)).astype(HALF)
        grads[s, :, number * DH : (number + 1) * DH] = grad_mixed
        rear[s, number] = mul(part(query, number), grad_mixed, TN).astype(HALF)
    start_rear()

    outer_grads = Scatter(outers, outers_landed, outers_sem, chip, core, ((0, 0, shared * columns),))

    @pl.loop(0, head)
    def _(slot):
        owner = slot // shared
        span = pl.ds(pl.multiple_of(slot % shared * columns, columns), columns)
        share_wo = mul(normed[...], cot[slot], TN).astype(HALF)
        outers[owner // seq_inner, owner % seq_inner, span] = share_wo

    pl.loop(0, seq_outer)(outer_grads.start_row)
    for number in range(heads_here):
        span = slice(number * DH, (number + 1) * DH)
        grad_mixed = grads[s, :, span]
        query_h, keys_h, values_h = part(query, number), part(keys, number), part(values, number)
        grad_scores = jnp.where(below, mul(grad_mixed, values_h, NT), 0.0).astype(HALF)
        grad_scores_t = jnp.where(above, mul(values_h, grad_mixed, NT), 0.0).astype(HALF)
        acc[0, :, span] = mul(grad_scores, keys_h) + mul(grad_mixed, prior[number], NT)
        acc[1, :, span] = mul(grad_scores_t, query_h)
        acc[2, :, span] = mul(scores_t[number], grad_mixed)
    if head_outer > 2:
        pl.when(jnp.logical_not(at_end))(lambda: result_sums.outer_first(1))
    result_sums.outer_second(head_outer - 1)
    tok_gather.finish()
    finish_tok()
    finish_fore()
    arrive_rear()
    for number in range(heads_here):
        later = jnp.zeros((DH, DH), WIDE)
        every = jnp.zeros((DH, DH), WIDE)
        for other in range(seq):
            one = rear[other, number].astype(WIDE)
            later = later + jnp.where(other > s, one, 0.0)
            every = every + one
        grad_state[number] = every
        later = later.astype(HALF)
        span = slice(number * DH, (number + 1) * DH)
        acc[1, :, span] += mul(part(values, number), later, NT)
        acc[2, :, span] += mul(part(keys, number), later)
    for number in range(3):
        grads[s, :, number * columns : (number + 1) * columns] = acc[number].astype(HALF)

    input_sums = Scatter(inputs, inputs_landed, inputs_sem, outer, inner, input_parts(rows))

    def input_terms(place):
        @pl.loop(0, head_inner)
        def _(turn):
            owner = (y + 1 + turn) % head_inner
            span = pl.ds(pl.multiple_of((place * head_inner + owner) * wide, wide), wide)
            term = mul(grads[s, :, :columns], wq[span, :], NT)
            term += mul(grads[s, :, columns : 2 * columns], wk[span, :], NT)
            term += mul(grads[s, :, 2 * columns :], wv[span, :], NT)
            inputs[place, owner] = term.astype(HALF)

            @pl.when(turn == head_inner - 2)
            def _():
                input_sums.start_row(place)

    each_row(head_outer - 1, input_terms)
    input_sums.outer_first(head_outer - 1)
    grads_gather.own(chip)
    grads_gather.own(core)

    for distance in range(head_outer - 2, 0, -1):
        each_row(distance, input_terms)
        pl.when(at_end)(lambda: input_sums.outer_first(distance))
    each_row(0, input_terms)

    def weight_grads(place):
        for number in range(shared):
            piece = moved_tok.at[place, number]
            span = slice(number * wide, (number + 1) * wide)
            pltpu.make_async_copy(piece, piece, tok_landed.at[place, number]).wait()
            for target, start in ((grad_wq, 0), (grad_wk, columns), (grad_wv, 2 * columns)):
                target[span, :] += mul(piece[...], grads[place, :, start : start + columns], TN)

    for target in (grad_wq, grad_wk, grad_wv):
        target[...] = jnp.zeros_like(target)
    for distance in range(seq_outer - 1, 0, -1):
        outer_grads.outer_second(distance)
    for distance in range(head_outer - 2, 1, -1):
        result_sums.outer_second(distance)
    weight_grads(s)
    grads_gather.from_inner(0)

    @pl.loop(1, seq_inner)
    def _(step):
        weight_grads(chip.place * seq_inner + (core.place + step) % seq_inner)

    input_sums.outer_second(head_outer - 1)
    if head_outer > 2:
        result_sums.outer_second(1)
    for distance in range(head_outer - 2, 0, -1):
        pl.when(jnp.logical_not(at_end))(lambda: input_sums.outer_first(distance))
    for distance in range(head_outer - 2, 0, -1):
        input_sums.outer_second(distance)
        if distance == head_outer - 2:
            grads_gather.from_outer(1)
    for distance in range(2, seq_outer):
        grads_gather.from_outer(distance)
        grads_gather.from_inner(distance - 1)
    result_sums.turn()
    input_sums.turn()
    grads_gather.from_inner(seq_outer - 1)

    @pl.loop(seq_inner, seq)
    def _(step):
        place = (chip.place + step // seq_inner) % seq_outer
        weight_grads(place * seq_inner + step % seq_inner)

    outer_grads.total(total_wo)
    for number in range(shared):
        grad_wo[:, number * wide : (number + 1) * wide] = total_wo[number * columns : (number + 1) * columns, :]
    result_sums.total(total)
    result[...] = total[...].astype(HALF)
    cot_gather.finish()
    finish_rear()
    outer_grads.finish()
    input_sums.total(grad_tokens)
    for one in (grads_gather, result_sums, input_sums):
        one.finish()


def write_out(*refs):
    count = (len(refs) - 1) // 2
    copies = [pltpu.make_async_copy(refs[k], refs[count + k], refs[-1].at[k]) for k in range(count)]
    for copy in copies:
        copy.start()
    for copy in copies:
        copy.wait()


def solution(mesh):
    seq, head = mesh.shape["seq"], mesh.shape["head"]

    def on_device(tokens, w_query, w_key, w_value, w_out, grad_out, state_in):
        rows, wide = tokens.shape
        depth, columns = w_query.shape
        heads_here = columns // DH
        shared = head // seq
        assert rows == BLOCK and head % seq == 0
        head_inner, seq_inner = inner_size(head), inner_size(seq)
        head_outer, seq_outer = head // head_inner, seq // seq_inner
        vmem = lambda *shape: pltpu.VMEM(shape, HALF)
        full = lambda *shape: pltpu.VMEM(shape, WIDE)
        dma = lambda *shape: pltpu.SemaphoreType.DMA(shape)
        gathers = lambda parts: dma(gather_sems(len(parts(rows)), head_outer, head_inner))
        sums = lambda parts: dma(scatter_sems(parts, head_outer, head_inner))
        outs = [
            ((rows, wide), HALF), ((rows, wide), WIDE),
            ((shared * wide, columns), WIDE), ((shared * wide, columns), WIDE), ((shared * wide, columns), WIDE),
            ((columns, shared * wide), WIDE), ((heads_here, DH, DH), WIDE),
        ]
        done = pl.pallas_call(
            lambda *refs: layer((seq, head), *refs),
            out_shape=[pltpu.VMEM(shape, kind) for shape, kind in outs],
            in_specs=[pl.BlockSpec(memory_space=pltpu.HBM)] * 7,
            out_specs=[pl.BlockSpec(memory_space=pltpu.VMEM)] * 7,
            scratch_shapes=[
                vmem(head, rows, wide), vmem(head, rows, wide),
                vmem(seq, shared, rows, wide),
                vmem(depth, columns), vmem(depth, columns), vmem(depth, columns), vmem(columns, depth),
                full(heads_here, DH, DH),
                full(3, rows, columns), full(rows, columns), full(rows, columns),
                vmem(rows, columns), vmem(rows, columns), vmem(rows, columns),
                vmem(heads_here, rows, rows), vmem(heads_here, DH, DH),
                vmem(seq, heads_here, DH, DH), vmem(seq, heads_here, DH, DH),
                vmem(seq, rows, 3 * columns), vmem(rows, columns),
                vmem(head_outer, head_inner, rows, wide), vmem(2, 2, head_outer, head_inner, rows, wide),
                vmem(head_outer, head_inner, rows, wide), vmem(2, 2, head_outer, head_inner, rows, wide),
                vmem(seq_outer, seq_inner, shared * columns, wide),
                vmem(2, 2, seq_outer, seq_inner, shared * columns, wide),
                full(rows, wide), full(shared * columns, wide),
                dma(7), dma(seq + 1), dma(seq + 1),
                gathers(gather_parts), dma(1), dma(seq, shared), gathers(cot_parts), dma(gather_sems(1, seq_outer, seq_inner)),
                sums(result_parts(rows)), sums(input_parts(rows)), dma(scatter_sems([(0,)], seq_outer, seq_inner)),
            ],
            compiler_params=pltpu.CompilerParams(
                collective_id=0, has_side_effects=True, vmem_limit_bytes=54 * 1024 * 1024
            ),
        )(tokens, w_query, w_key, w_value, w_out, grad_out, state_in)
        return pl.pallas_call(
            write_out,
            out_shape=[jax.ShapeDtypeStruct(shape, kind) for shape, kind in outs],
            in_specs=[pl.BlockSpec(memory_space=pl.ANY)] * 7,
            out_specs=[pl.BlockSpec(memory_space=pltpu.HBM)] * 7,
            scratch_shapes=[dma(7)],
            compiler_params=pltpu.CompilerParams(vmem_limit_bytes=1024 * 1024),
        )(*done)

    by_head = P(None, "head")
    tiled = P("seq", "head")
    return jax.shard_map(
        on_device,
        mesh=mesh,
        in_specs=(tiled, by_head, by_head, by_head, P("head", None), tiled, P("head", None, None)),
        out_specs=(tiled, tiled, tiled, tiled, tiled, P("head", "seq"), P("head", None, None)),
        check_vma=False,
    )
```

```python
import jax
import jax.numpy as jnp
from jax import lax
from jax.experimental import pallas as pl
from jax.experimental.pallas import tpu as pltpu
from jax.sharding import PartitionSpec as P

DH = 128
BLOCK = 256
EPSILON = 1e-06
WIDE = jnp.float32
HALF = jnp.bfloat16
MESH = pl.DeviceIdType.MESH
NN = (((1,), (0,)), ((), ()))
NT = (((1,), (1,)), ((), ()))
TN = (((0,), (0,)), ((), ()))


def mul(left, right, dims=NN):
    return lax.dot_general(left, right, dims, preferred_element_type=WIDE)


def parts(rows, shares):
    unit, start, cut = rows // 16, 0, []
    for order, share in shares:
        cut.append((order, start, share * unit))
        start += share * unit
    return cut


def gather_parts(rows):
    return parts(rows, ((0, 7), (0, 6), (1, 3)))


def cot_parts(rows):
    return parts(rows, ((0, 6), (0, 5), (1, 5)))


def result_parts(rows):
    return parts(rows, ((1, 10), (0, 6)))


def input_parts(rows):
    return parts(rows, ((0, 7), (0, 7), (1, 2)))


def inner_size(count):
    inner = 1
    while 4 * inner * inner <= count:
        inner *= 2
    return inner


class Line:
    def __init__(self, place, size, device):
        self.place, self.size, self.device = place, size, device

    def has(self, way):
        return self.place < self.size - 1 if way == 0 else self.place > 0

    def next(self, way):
        return self.device(self.place + (1 if way == 0 else -1))


def gather_sems(count, outer, inner):
    return count * outer * inner + 4


def scatter_sems(parts, outer, inner):
    total = 4
    for order, *_ in parts:
        first, second = (inner, outer) if order == 0 else (outer, inner)
        total += second * (first + 1) + second + 1
    return total


class Gather:
    def __init__(self, source, slots, sems, outer, inner, parts, seen):
        self.source, self.slots, self.sems = source, slots, sems
        self.outer, self.inner, self.seen = outer, inner, seen
        self.parts = [(number * outer.size * inner.size, *part) for number, part in enumerate(parts)]
        self.sent = len(parts) * outer.size * inner.size

    def slot(self, place_outer, place_inner):
        return place_outer * self.inner.size + place_inner

    def copy(self, part, slot, line, way, source=None):
        base, _, start, rows = part
        sent = self.sent + way + (0 if line is self.outer else 2)
        piece = self.slots.at[slot, pl.ds(start, rows)]
        return pltpu.make_async_remote_copy(
            src_ref=piece if source is None else source.at[pl.ds(start, rows)],
            dst_ref=piece,
            send_sem=self.sems.at[sent],
            recv_sem=self.sems.at[base + slot],
            device_id=line.next(way),
            device_id_type=MESH,
        )

    def send(self, part, slot, line, way, also=True, source=None):
        @pl.when(line.has(way) & also)
        def _():
            self.copy(part, slot, line, way, source).start()

    def arrive(self, part, slot):
        base, _, start, rows = part
        piece = self.slots.at[slot, pl.ds(start, rows)]
        pltpu.make_async_copy(piece, piece, self.sems.at[base + slot]).wait()

    def own(self, line, orders=(0, 1)):
        slot = self.slot(self.outer.place, self.inner.place)
        for part in self.parts:
            if part[1] in orders:
                for way in (0, 1):
                    self.send(part, slot, line, way, source=self.source)

    def cross_row(self):
        for part in self.parts:
            if part[1] == 1:
                for way in (0, 1):
                    for step in range(1, self.inner.size):
                        place = self.inner.place + (-step if way == 0 else step)

                        @pl.when((place >= 0) & (place < self.inner.size))
                        def _():
                            slot = self.slot(self.outer.place, place)
                            self.arrive(part, slot)
                            self.send(part, slot, self.inner, way)
                            self.send(part, slot, self.outer, 0)
                            self.send(part, slot, self.outer, 1)

    def each_side(self, distance, act):
        @pl.loop(0, 2)
        def _(side):
            row = self.outer.place + (2 * side - 1) * distance

            @pl.when((row >= 0) & (row < self.outer.size) & ((distance > 0) | (side == 0)))
            def _():
                act(side, row)

    def from_outer(self, distance):
        steps = [(part, 0) for part in self.parts]
        steps += [(part, turn) for turn in range(1, self.inner.size) for part in self.parts if part[1] == 1]
        for part, turn in steps:

            def pass_on(side, row):
                slot = self.slot(row, (self.inner.place + turn) % self.inner.size)
                self.arrive(part, slot)
                self.send(part, slot, self.outer, 0, side == 0)
                self.send(part, slot, self.outer, 1, side == 1)
                if part[1] == 0:
                    self.send(part, slot, self.inner, 0)
                    self.send(part, slot, self.inner, 1)

            self.each_side(distance, pass_on)
        self.each_side(distance, lambda side, row: self.seen(self.slot(row, self.inner.place)))

    def from_inner(self, distance):
        def each_place(side, row):
            @pl.loop(0, 2)
            def _(way):
                @pl.loop(1, self.inner.size)
                def _(step):
                    place = self.inner.place + (2 * way - 1) * step

                    @pl.when((place >= 0) & (place < self.inner.size))
                    def _():
                        slot = self.slot(row, place)
                        for part in self.parts:
                            if part[1] == 0:
                                self.arrive(part, slot)
                                self.send(part, slot, self.inner, 0, way == 0)
                                self.send(part, slot, self.inner, 1, way == 1)
                        self.seen(slot)

        self.each_side(distance, each_place)

    def finish(self):
        @pl.loop(0, self.outer.size)
        def _(row):
            @pl.loop(0, self.inner.size)
            def _(place):
                slot = self.slot(row, place)
                for part in self.parts:
                    for way in (0, 1):
                        passed = (row <= self.outer.place) if way == 0 else (row >= self.outer.place)
                        if part[1] == 0:
                            passed &= place == self.inner.place

                        @pl.when(self.outer.has(way) & passed)
                        def _():
                            self.copy(part, slot, self.outer, way).wait_send()

                        passed = (place <= self.inner.place) if way == 0 else (place >= self.inner.place)
                        if part[1] == 1:
                            passed &= row == self.outer.place

                        @pl.when(self.inner.has(way) & passed)
                        def _():
                            self.copy(part, slot, self.inner, way).wait_send()


class Reduce:
    def __init__(self, line, term, landed, sems, sent, base):
        self.line, self.term, self.landed, self.sems, self.sent, self.base = line, term, landed, sems, sent, base

    def landing(self, way, owner, place):
        index = self.base + owner
        return self.sems.at[index if way == 0 else jnp.where(owner == place, self.base + self.line.size, index)]

    def copy(self, way, owner):
        return pltpu.make_async_remote_copy(
            src_ref=self.term(owner),
            dst_ref=self.landed(way, owner),
            send_sem=self.sems.at[self.sent + way],
            recv_sem=self.landing(way, owner, self.line.place + (1 if way == 0 else -1)),
            device_id=self.line.next(way),
            device_id_type=MESH,
        )

    def arrive(self, way, owner, act):
        @pl.when(self.line.has(1 - way))
        def _():
            piece = self.landed(way, owner)
            pltpu.make_async_copy(piece, piece, self.landing(way, owner, self.line.place)).wait()
            act(piece[...].astype(WIDE))

    def add(self, way, owner):
        term = self.term(owner)

        def act(value):
            term[...] = (term[...].astype(WIDE) + value).astype(HALF)

        self.arrive(way, owner, act)

    def each(self, distance, act):
        for way in (0, 1):
            owner = self.line.place + (distance if way == 0 else -distance)
            pl.when((owner >= 0) & (owner < self.line.size))(lambda: act(way, owner))

    def step(self, distance):
        def act(way, owner):
            self.add(way, owner)
            self.copy(way, owner).start()

        self.each(distance, act)

    def finish(self):
        for distance in range(1, self.line.size):
            self.each(distance, lambda way, owner: self.copy(way, owner).wait_send())


class Scatter:
    def __init__(self, terms, landed, sems, outer, inner, parts):
        self.terms, self.landed, self.sems = terms, landed, sems
        self.outer, self.inner = outer, inner
        self.parts, base = [], 4
        for order, start, rows in parts:
            self.parts.append((base, order, start, rows))
            base += scatter_sems([(order,)], outer.size, inner.size) - 4

    def along_outer(self, part, place):
        base, order, start, rows = part
        span = pl.ds(start, rows)
        base += self.outer.size * (self.inner.size + 1) if order == 0 else place * (self.outer.size + 1)
        return Reduce(
            self.outer,
            lambda owner: self.terms.at[owner, place, span],
            lambda way, owner: self.landed.at[0, way, owner, place, span],
            self.sems,
            0,
            base,
        )

    def along_inner(self, part, row):
        base, order, start, rows = part
        span = pl.ds(start, rows)
        base += self.inner.size * (self.outer.size + 1) if order == 1 else row * (self.inner.size + 1)
        return Reduce(
            self.inner,
            lambda owner: self.terms.at[row, owner, span],
            lambda way, owner: self.landed.at[1, way, row, owner, span],
            self.sems,
            2,
            base,
        )

    def steps_inner(self, part, row):
        line = self.along_inner(part, row)
        for distance in range(self.inner.size - 1, 0, -1):
            line.step(distance)

    def start_row(self, row):
        for part in self.parts:
            if part[1] == 0:
                self.steps_inner(part, row)

    def outer_first(self, distance):
        for part in self.parts:
            if part[1] == 1:
                for place in range(self.inner.size):
                    self.along_outer(part, place).step(distance)

    def outer_second(self, distance):
        for part in self.parts:
            if part[1] == 0:

                def act(way, row):
                    for side in (0, 1):
                        self.along_inner(part, row).add(side, self.inner.place)

                self.along_outer(part, self.inner.place).each(distance, act)
                self.along_outer(part, self.inner.place).step(distance)

    def turn(self):
        for part in self.parts:
            if part[1] == 1:
                for place in range(self.inner.size):

                    @pl.when(place != self.inner.place)
                    def _():
                        for way in (0, 1):
                            self.along_outer(part, place).add(way, self.outer.place)

                self.steps_inner(part, self.outer.place)

    def total(self, out):
        row, place = self.outer.place, self.inner.place
        for part in self.parts:
            span = pl.ds(part[2], part[3])
            held = [self.terms[row, place, span].astype(WIDE)]
            out[span, :] = held[0].astype(out.dtype)

            def act(value):
                out[span, :] = (out[span, :].astype(WIDE) + value).astype(out.dtype)

            for way in (0, 1):
                self.along_outer(part, place).arrive(way, row, act)
                self.along_inner(part, row).arrive(way, place, act)

    def finish(self):
        for part in self.parts:
            if part[1] == 0:
                pl.loop(0, self.outer.size)(lambda row: self.along_inner(part, row).finish())
                self.along_outer(part, self.inner.place).finish()
            else:
                pl.loop(0, self.inner.size)(lambda place: self.along_outer(part, place).finish())
                self.along_inner(part, self.outer.place).finish()


def layer(
    sizes,
    tokens_in, wq_in, wk_in, wv_in, wo_in, cot_in, state_in,
    result, grad_tokens, grad_wq, grad_wk, grad_wv, grad_wo, grad_state,
    tok, cot, moved_tok, wq, wk, wv, wo, state,
    acc, grad_normed, mixed, query, keys, values, scores_t, prior,
    fore, rear, grads, normed,
    terms, terms_landed, inputs, inputs_landed, outers, outers_landed, total, total_wo,
    load_sem, fore_sem, rear_sem,
    tok_sem, tok_moved, tok_landed, cot_sem, grads_sem, terms_sem, inputs_sem, outers_sem,
):
    seq, head = sizes
    head_inner, seq_inner = inner_size(head), inner_size(seq)
    head_outer, seq_outer = head // head_inner, seq // seq_inner
    shared = head // seq
    rows, wide = tok.shape[1:]
    columns = wq.shape[1]
    heads_here = columns // DH
    s, h = lax.axis_index("seq"), lax.axis_index("head")
    z, y = h // head_inner, h % head_inner
    outer = Line(z, head_outer, lambda place: (s, place * head_inner + y))
    inner = Line(y, head_inner, lambda place: (s, z * head_inner + place))
    chip = Line(s // seq_inner, seq_outer, lambda place: (place * seq_inner + s % seq_inner, h))
    core = Line(s % seq_inner, seq_inner, lambda place: (s // seq_inner * seq_inner + place, h))

    loads = [
        pltpu.make_async_copy(source, target, load_sem.at[number])
        for number, (source, target) in enumerate(
            [
                (tokens_in, tok.at[h]),
                (wq_in, wq), (wk_in, wk), (wv_in, wv),
                (cot_in, cot.at[h]), (wo_in, wo), (state_in, state),
            ]
        )
    ]
    for load in loads:
        load.start()

    barrier = pltpu.get_barrier_semaphore()
    expected = seq - 1
    for line in (outer, inner):
        for way in (0, 1):
            expected = expected + line.has(way).astype(jnp.int32)

            @pl.when(line.has(way))
            def _():
                pl.semaphore_signal(barrier, inc=1, device_id=line.next(way), device_id_type=MESH)
    for other in range(1, seq):
        pl.semaphore_signal(barrier, inc=1, device_id=((s + other) % seq, h), device_id_type=MESH)
    pl.semaphore_wait(barrier, expected)

    def early(slot):
        distance = abs(slot // head_inner - z)
        at_end = (z == 0) | (z == head_outer - 1)
        direct = (slot % head_inner == y) & at_end
        return (distance < head_outer - 2) | ((distance == head_outer - 2) & direct)

    def moves(slots, moved, sent, landed):
        def copy(slot):
            return pltpu.make_async_remote_copy(
                src_ref=slots.at[slot],
                dst_ref=moved.at[s, slot % shared],
                send_sem=sent.at[0],
                recv_sem=landed.at[s, slot % shared],
                device_id=(slot // shared, h),
                device_id_type=MESH,
            )

        def start(slot):
            @pl.when(slot // shared != s)
            def _():
                copy(slot).start()

            @pl.when(slot // shared == s)
            def _():
                own = moved.at[s, slot % shared]
                pltpu.make_async_copy(slots.at[slot], own, landed.at[s, slot % shared]).start()

        def soon(slot):
            pl.when(early(slot))(lambda: start(slot))

        def late():
            @pl.loop(0, head)
            def _(slot):
                pl.when(jnp.logical_not(early(slot)))(lambda: start(slot))

        def finish():
            @pl.loop(0, head)
            def _(slot):
                @pl.when(slot // shared != s)
                def _():
                    copy(slot).wait_send()

        return soon, late, finish

    move_tok, move_tok_late, finish_tok = moves(tok, moved_tok, tok_moved, tok_landed)

    def project(slot):
        block = tok[slot]
        span = pl.ds(pl.multiple_of(slot * wide, wide), wide)
        for number, weight in enumerate((wq, wk, wv)):
            acc[number] += mul(block, weight[span, :])
        move_tok(slot)

    def pull(slot):
        span = pl.ds(pl.multiple_of(slot * wide, wide), wide)
        grad_normed[...] += mul(cot[slot], wo[:, span], NT)

    def each_row(distance, act):
        @pl.loop(0, 2)
        def _(side):
            place = z + (2 * side - 1) * distance
            pl.when((place >= 0) & (place < head_outer) & ((distance > 0) | (side == 0)))(lambda: act(place))

    tok_gather = Gather(tokens_in, tok, tok_sem, outer, inner, gather_parts(rows), project)
    cot_gather = Gather(cot_in, cot, cot_sem, outer, inner, cot_parts(rows), pull)
    nothing = lambda slot: None
    grads_gather = Gather(grads.at[s], grads, grads_sem, chip, core, ((0, 0, rows),), nothing)

    tok_gather.own(inner, (1,))
    tok_gather.own(outer)
    tok_gather.own(inner, (0,))
    acc[...] = jnp.zeros_like(acc)
    grad_normed[...] = jnp.zeros_like(grad_normed)
    for load in loads[:4]:
        load.wait()
    project(h)
    tok_gather.cross_row()

    @pl.loop(1, head_outer)
    def _(distance):
        tok_gather.from_outer(distance)

        @pl.when(distance == head_outer - 2)
        def _():
            cot_gather.own(outer)
            cot_gather.own(inner, (1,))

        tok_gather.from_inner(distance - 1)

    cot_gather.own(inner, (0,))
    cot_gather.cross_row()
    tok_gather.from_inner(head_outer - 1)

    for number, target in enumerate((query, keys, values)):
        target[...] = acc[number].astype(HALF)

    def part(ref, number):
        return ref[:, number * DH : (number + 1) * DH]

    for number in range(heads_here):
        fore[s, number] = mul(part(keys, number), part(values, number), TN).astype(HALF)

    def share(states, sems, wanted):
        def copy(other):
            return pltpu.make_async_remote_copy(
                src_ref=states.at[s],
                dst_ref=states.at[s],
                send_sem=sems.at[seq],
                recv_sem=sems.at[s],
                device_id=(other, h),
                device_id_type=MESH,
            )

        def start():
            for other in range(seq):
                pl.when((other != s) & wanted(s, other))(lambda: copy(other).start())

        def arrive():
            for other in range(seq):

                @pl.when((other != s) & wanted(other, s))
                def _():
                    pltpu.make_async_copy(states.at[other], states.at[other], sems.at[other]).wait()

        def finish():
            for other in range(seq):
                pl.when((other != s) & wanted(s, other))(lambda: copy(other).wait_send())

        return start, arrive, finish

    start_fore, arrive_fore, finish_fore = share(fore, fore_sem, lambda source, target: source < target)
    start_rear, arrive_rear, finish_rear = share(rear, rear_sem, lambda source, target: target >= 0)
    start_fore()
    for load in loads[4:]:
        load.wait()
    move_tok_late()
    pull(h)
    at_end = (z == 0) | (z == head_outer - 1)
    pl.when(jnp.logical_not(at_end))(lambda: cot_gather.from_outer(1))

    below = lax.broadcasted_iota(jnp.int32, (rows, rows), 1) <= lax.broadcasted_iota(jnp.int32, (rows, rows), 0)
    above = lax.broadcasted_iota(jnp.int32, (rows, rows), 1) >= lax.broadcasted_iota(jnp.int32, (rows, rows), 0)
    for number in range(heads_here):
        query_h, keys_h = part(query, number), part(keys, number)
        scores = jnp.where(below, mul(query_h, keys_h, NT), 0.0).astype(HALF)
        scores_t[number] = jnp.where(above, mul(keys_h, query_h, NT), 0.0).astype(HALF)
        mixed[:, number * DH : (number + 1) * DH] = mul(scores, part(values, number))
    arrive_fore()
    for number in range(heads_here):
        before = state[number]
        for other in range(seq):
            before = before + jnp.where(other < s, fore[other, number].astype(WIDE), 0.0)
        prior[number] = before.astype(HALF)
        whole = part(mixed, number) + mul(part(query, number), prior[number])
        mixed[:, number * DH : (number + 1) * DH] = whole
        inv_norm = lax.rsqrt(jnp.mean(whole * whole, axis=-1, keepdims=True) + EPSILON)
        normed[:, number * DH : (number + 1) * DH] = (whole * inv_norm).astype(HALF)

    result_sums = Scatter(terms, terms_landed, terms_sem, outer, inner, result_parts(rows))

    def result_terms(row):
        @pl.loop(0, head_inner)
        def _(place):
            span = pl.ds(pl.multiple_of((row * head_inner + place) * wide, wide), wide)
            terms[row, place] = mul(normed[...], wo[:, span]).astype(HALF)

    each_row(head_outer - 1, result_terms)
    result_sums.outer_first(head_outer - 1)

    for distance in range(head_outer - 2, 0, -1):
        each_row(distance, result_terms)
        pl.when(at_end)(lambda: result_sums.outer_first(distance))
    each_row(0, result_terms)
    pl.when(at_end)(lambda: cot_gather.from_outer(1))
    cot_gather.from_inner(0)
    for distance in range(2, head_outer):
        cot_gather.from_outer(distance)
        if distance < head_outer - 1:
            cot_gather.from_inner(distance - 1)
            pl.when(jnp.logical_not(at_end))(lambda: result_sums.outer_first(head_outer - distance))

    @pl.loop(0, head_outer)
    def _(turn):
        each_row(head_outer - 1 - turn, result_sums.start_row)

    cot_gather.from_inner(head_outer - 2)
    cot_gather.from_inner(head_outer - 1)

    for number in range(heads_here):
        whole, pulled = part(mixed, number), part(grad_normed, number)
        inv_norm = lax.rsqrt(jnp.mean(whole * whole, axis=-1, keepdims=True) + EPSILON)
        slope = jnp.mean(pulled * whole, axis=-1, keepdims=True)
        grad_mixed = (inv_norm * (pulled - whole * inv_norm * inv_norm * slope)).astype(HALF)
        grads[s, :, number * DH : (number + 1) * DH] = grad_mixed
        rear[s, number] = mul(part(query, number), grad_mixed, TN).astype(HALF)
    start_rear()

    outer_grads = Scatter(outers, outers_landed, outers_sem, chip, core, ((0, 0, shared * columns),))

    @pl.loop(0, head)
    def _(slot):
        owner = slot // shared
        span = pl.ds(pl.multiple_of(slot % shared * columns, columns), columns)
        share_wo = mul(normed[...], cot[slot], TN).astype(HALF)
        outers[owner // seq_inner, owner % seq_inner, span] = share_wo

    pl.loop(0, seq_outer)(outer_grads.start_row)
    for number in range(heads_here):
        span = slice(number * DH, (number + 1) * DH)
        grad_mixed = grads[s, :, span]
        query_h, keys_h, values_h = part(query, number), part(keys, number), part(values, number)
        grad_scores = jnp.where(below, mul(grad_mixed, values_h, NT), 0.0).astype(HALF)
        grad_scores_t = jnp.where(above, mul(values_h, grad_mixed, NT), 0.0).astype(HALF)
        acc[0, :, span] = mul(grad_scores, keys_h) + mul(grad_mixed, prior[number], NT)
        acc[1, :, span] = mul(grad_scores_t, query_h)
        acc[2, :, span] = mul(scores_t[number], grad_mixed)
    if head_outer > 2:
        pl.when(jnp.logical_not(at_end))(lambda: result_sums.outer_first(1))
    result_sums.outer_second(head_outer - 1)
    tok_gather.finish()
    finish_tok()
    finish_fore()
    arrive_rear()
    for number in range(heads_here):
        later = jnp.zeros((DH, DH), WIDE)
        every = jnp.zeros((DH, DH), WIDE)
        for other in range(seq):
            one = rear[other, number].astype(WIDE)
            later = later + jnp.where(other > s, one, 0.0)
            every = every + one
        grad_state[number] = every
        later = later.astype(HALF)
        span = slice(number * DH, (number + 1) * DH)
        acc[1, :, span] += mul(part(values, number), later, NT)
        acc[2, :, span] += mul(part(keys, number), later)
    for number in range(3):
        grads[s, :, number * columns : (number + 1) * columns] = acc[number].astype(HALF)

    input_sums = Scatter(inputs, inputs_landed, inputs_sem, outer, inner, input_parts(rows))

    def input_terms(place):
        @pl.loop(0, head_inner)
        def _(turn):
            owner = (y + 1 + turn) % head_inner
            span = pl.ds(pl.multiple_of((place * head_inner + owner) * wide, wide), wide)
            term = mul(grads[s, :, :columns], wq[span, :], NT)
            term += mul(grads[s, :, columns : 2 * columns], wk[span, :], NT)
            term += mul(grads[s, :, 2 * columns :], wv[span, :], NT)
            inputs[place, owner] = term.astype(HALF)

            @pl.when(turn == head_inner - 2)
            def _():
                input_sums.start_row(place)

    each_row(head_outer - 1, input_terms)
    input_sums.outer_first(head_outer - 1)
    grads_gather.own(chip)
    grads_gather.own(core)

    for distance in range(head_outer - 2, 0, -1):
        each_row(distance, input_terms)
        pl.when(at_end)(lambda: input_sums.outer_first(distance))
    each_row(0, input_terms)

    def weight_grads(place):
        for number in range(shared):
            piece = moved_tok.at[place, number]
            span = slice(number * wide, (number + 1) * wide)
            pltpu.make_async_copy(piece, piece, tok_landed.at[place, number]).wait()
            for target, start in ((grad_wq, 0), (grad_wk, columns), (grad_wv, 2 * columns)):
                target[span, :] += mul(piece[...], grads[place, :, start : start + columns], TN)

    for target in (grad_wq, grad_wk, grad_wv):
        target[...] = jnp.zeros_like(target)
    for distance in range(seq_outer - 1, 0, -1):
        outer_grads.outer_second(distance)
    for distance in range(head_outer - 2, 1, -1):
        result_sums.outer_second(distance)
    weight_grads(s)
    grads_gather.from_inner(0)

    @pl.loop(1, seq_inner)
    def _(step):
        weight_grads(chip.place * seq_inner + (core.place + step) % seq_inner)

    input_sums.outer_second(head_outer - 1)
    if head_outer > 2:
        result_sums.outer_second(1)
    for distance in range(head_outer - 2, 0, -1):
        pl.when(jnp.logical_not(at_end))(lambda: input_sums.outer_first(distance))
    for distance in range(head_outer - 2, 0, -1):
        input_sums.outer_second(distance)
        if distance == head_outer - 2:
            grads_gather.from_outer(1)
    for distance in range(2, seq_outer):
        grads_gather.from_outer(distance)
        grads_gather.from_inner(distance - 1)
    result_sums.turn()
    input_sums.turn()
    grads_gather.from_inner(seq_outer - 1)

    @pl.loop(seq_inner, seq)
    def _(step):
        place = (chip.place + step // seq_inner) % seq_outer
        weight_grads(place * seq_inner + step % seq_inner)

    outer_grads.total(total_wo)
    for number in range(shared):
        grad_wo[:, number * wide : (number + 1) * wide] = total_wo[number * columns : (number + 1) * columns, :]
    cot_gather.finish()
    finish_rear()
    outer_grads.finish()
    grads_gather.finish()
    result_sums.total(total)
    result[...] = total[...].astype(HALF)
    input_sums.total(grad_tokens)
    for one in (result_sums, input_sums):
        one.finish()


def write_out(*refs):
    count = (len(refs) - 1) // 2
    copies = [pltpu.make_async_copy(refs[k], refs[count + k], refs[-1].at[k]) for k in range(count)]
    for copy in copies:
        copy.start()
    for copy in copies:
        copy.wait()


def solution(mesh):
    seq, head = mesh.shape["seq"], mesh.shape["head"]

    def on_device(tokens, w_query, w_key, w_value, w_out, grad_out, state_in):
        rows, wide = tokens.shape
        depth, columns = w_query.shape
        heads_here = columns // DH
        shared = head // seq
        assert rows == BLOCK and head % seq == 0
        head_inner, seq_inner = inner_size(head), inner_size(seq)
        head_outer, seq_outer = head // head_inner, seq // seq_inner
        vmem = lambda *shape: pltpu.VMEM(shape, HALF)
        full = lambda *shape: pltpu.VMEM(shape, WIDE)
        dma = lambda *shape: pltpu.SemaphoreType.DMA(shape)
        gathers = lambda parts: dma(gather_sems(len(parts(rows)), head_outer, head_inner))
        sums = lambda parts: dma(scatter_sems(parts, head_outer, head_inner))
        outs = [
            ((rows, wide), HALF), ((rows, wide), WIDE),
            ((shared * wide, columns), WIDE), ((shared * wide, columns), WIDE), ((shared * wide, columns), WIDE),
            ((columns, shared * wide), WIDE), ((heads_here, DH, DH), WIDE),
        ]
        done = pl.pallas_call(
            lambda *refs: layer((seq, head), *refs),
            out_shape=[pltpu.VMEM(shape, kind) for shape, kind in outs],
            in_specs=[pl.BlockSpec(memory_space=pltpu.HBM)] * 7,
            out_specs=[pl.BlockSpec(memory_space=pltpu.VMEM)] * 7,
            scratch_shapes=[
                vmem(head, rows, wide), vmem(head, rows, wide),
                vmem(seq, shared, rows, wide),
                vmem(depth, columns), vmem(depth, columns), vmem(depth, columns), vmem(columns, depth),
                full(heads_here, DH, DH),
                full(3, rows, columns), full(rows, columns), full(rows, columns),
                vmem(rows, columns), vmem(rows, columns), vmem(rows, columns),
                vmem(heads_here, rows, rows), vmem(heads_here, DH, DH),
                vmem(seq, heads_here, DH, DH), vmem(seq, heads_here, DH, DH),
                vmem(seq, rows, 3 * columns), vmem(rows, columns),
                vmem(head_outer, head_inner, rows, wide), vmem(2, 2, head_outer, head_inner, rows, wide),
                vmem(head_outer, head_inner, rows, wide), vmem(2, 2, head_outer, head_inner, rows, wide),
                vmem(seq_outer, seq_inner, shared * columns, wide),
                vmem(2, 2, seq_outer, seq_inner, shared * columns, wide),
                full(rows, wide), full(shared * columns, wide),
                dma(7), dma(seq + 1), dma(seq + 1),
                gathers(gather_parts), dma(1), dma(seq, shared), gathers(cot_parts), dma(gather_sems(1, seq_outer, seq_inner)),
                sums(result_parts(rows)), sums(input_parts(rows)), dma(scatter_sems([(0,)], seq_outer, seq_inner)),
            ],
            compiler_params=pltpu.CompilerParams(
                collective_id=0, has_side_effects=True, vmem_limit_bytes=54 * 1024 * 1024
            ),
        )(tokens, w_query, w_key, w_value, w_out, grad_out, state_in)
        return pl.pallas_call(
            write_out,
            out_shape=[jax.ShapeDtypeStruct(shape, kind) for shape, kind in outs],
            in_specs=[pl.BlockSpec(memory_space=pl.ANY)] * 7,
            out_specs=[pl.BlockSpec(memory_space=pltpu.HBM)] * 7,
            scratch_shapes=[dma(7)],
            compiler_params=pltpu.CompilerParams(vmem_limit_bytes=1024 * 1024),
        )(*done)

    by_head = P(None, "head")
    tiled = P("seq", "head")
    return jax.shard_map(
        on_device,
        mesh=mesh,
        in_specs=(tiled, by_head, by_head, by_head, P("head", None), tiled, P("head", None, None)),
        out_specs=(tiled, tiled, tiled, tiled, tiled, P("head", "seq"), P("head", None, None)),
        check_vma=False,
    )
```
